32 devices in a mesh: cls: 2 (over x), wide: 16 (over z, y, core).
Axes of the slice: x: 2, y: 2, z: 4, core: 2. Of those that a mesh axis runs over, the one named last changes fastest.
Arguments:
- syn_images: float32 [2, 32, 3, 128, 128], P('cls', 'wide'), may hold values from -6 to 6
- adam_first: float32 [2, 32, 3, 128, 128], P('cls', 'wide'), may hold values from -6 to 6
- adam_second: float32 [2, 32, 3, 128, 128], P('cls', 'wide'), may hold values from 0.25 to 4
- real_pool: bfloat16 [2, 128, 3, 128, 128], P('cls', 'wide'), may hold values from -6 to 6
- real_pick: int32 [2, 16, 8], P('cls', 'wide'), may hold values from 0 to 7, each once within a row
- real_count: int32 [2, 16], P('cls'), may hold values from 2 to 8, as said below
- syn_order: int32 [2, 32], P('cls'), may hold values from 0 to 31, each once within a row
- conv_weight: bfloat16 [27, 128], P(None, 'cls'), may hold values from -1.25 to 1.25
- norm_gain: bfloat16 [128], P('cls'), may hold values from 0.099609375 to 1.8984375
- norm_bias: bfloat16 [128], P('cls'), may hold values from -3 to 3
Outputs:
- new_images: float32 [2, 32, 3, 128, 128], P('cls', 'wide')
- new_first: float32 [2, 32, 3, 128, 128], P('cls', 'wide')
- new_second: float32 [2, 32, 3, 128, 128], P('cls', 'wide')
The draws below stay inside these ranges and needn't reach their ends.
Inputs may be any that keep to these rules, and one draw needn't show every extreme that they name: `real_count`: in every class exactly one device of wide takes all 8 of its real images; every other device takes 2 to 4.
All inputs are finite; a program needn't handle non-finite values.
Results may differ from the reference program's by a relative error of at most 0.0012.
The reference program's roundings to bfloat16 on the way count: a program that leaves them out, or rounds other values in their place, can miss the bound.
Values may be sent and summed in bfloat16 or wider, within the bound.
No kernel may reach another device: no remote copies, remote signals or barrier semaphores. Data moves between devices by JAX's collectives and lax.ppermute only.
A program may use at most 64 MiB of HBM per device.

```python
import math
import jax
import jax.numpy as jnp
from jax import lax

CH = 3
HT = 128
WD = 128
WIDTH = 128
RLOC = 8
NCLS = 2
IPC = 32
SBATCH = 16
RPOOL = 128
TAPS = 27
N_WIDE = 16


def draw_real_count(key, part):
    key_base, key_full = jax.random.split(jax.random.fold_in(key, 17))
    base = jax.random.randint(key_base, (NCLS, N_WIDE), 2, RLOC // 2 + 1)
    full_at = jax.random.randint(key_full, (NCLS, 1), 0, N_WIDE)
    wide_ids = jnp.arange(N_WIDE, dtype=jnp.int32)[None, :]
    return jnp.where(wide_ids == full_at, RLOC, base).astype(jnp.int32)


def shard_levels(stream_key, shape, cuts, smallest, largest):
    level, own = 1.0, jax.random.fold_in(stream_key, 6)
    for axis_at, blocks in cuts:
        draws = jnp.exp(jax.random.uniform(jax.random.fold_in(own, axis_at), (blocks,), jnp.float32, smallest / len(cuts), largest / len(cuts)))
        level = level * jnp.repeat(draws, shape[axis_at] // blocks).reshape([-1 if axis == axis_at else 1 for axis in range(len(shape))])
    return level


def normal_values(key, shape, scale, limit, cuts=(), kind=jnp.bfloat16):
    drawn = scale * jax.random.normal(key, shape, jnp.float32)
    if cuts:
        drawn = drawn * shard_levels(key, shape, cuts, -0.22, 0.18)
    return jnp.clip(drawn, -limit, limit).astype(kind)


def setup_inputs(seed: int = 0) -> dict:
    key_list = jax.random.split(jax.random.key(seed), 11)
    syn_images = normal_values(key_list[0], (NCLS, IPC, CH, HT, WD), 1.0, 6.0, ((0, 2), (1, 16)), jnp.float32)
    adam_first = normal_values(key_list[1], (NCLS, IPC, CH, HT, WD), 1.0, 6.0, ((0, 2), (1, 16)), jnp.float32)
    adam_second = jnp.clip(jnp.exp(math.log(4.0) - 2.7725887 * jax.random.uniform(key_list[2], (NCLS, IPC, CH, HT, WD), jnp.float32) ** shard_levels(key_list[2], (NCLS, IPC, CH, HT, WD), ((0, 2), (1, 16)), -0.2, 0.2)), 0.25, 4.0)
    real_pool = normal_values(key_list[3], (NCLS, RPOOL, CH, HT, WD), 1.0, 6.0, ((0, 2), (1, 16)))
    real_pick = jax.vmap(lambda own: jax.random.permutation(own, RLOC))(jax.random.split(key_list[4], NCLS * N_WIDE)).reshape((NCLS, N_WIDE, RLOC)).astype(jnp.int32)
    real_count = draw_real_count(jax.random.fold_in(key_list[10], 71), 0)
    syn_order = jax.vmap(lambda own: jax.random.permutation(own, IPC))(jax.random.split(key_list[6], NCLS)).reshape((NCLS, IPC)).astype(jnp.int32)
    conv_weight = normal_values(key_list[7], (TAPS, WIDTH), (9 * CH) ** -0.5, 1.25, ((1, 2),))
    norm_gain = jnp.clip(1.0 + 0.18 * jax.random.normal(key_list[8], (WIDTH,), jnp.float32), 0.099609375, 1.8984375).astype(jnp.bfloat16)
    norm_bias = normal_values(key_list[9], (WIDTH,), 0.5, 3.0, ((0, 2),))
    return {"syn_images": syn_images, "adam_first": adam_first, "adam_second": adam_second, "real_pool": real_pool, "real_pick": real_pick, "real_count": real_count, "syn_order": syn_order, "conv_weight": conv_weight, "norm_gain": norm_gain, "norm_bias": norm_bias}


beta_one = 0.9
beta_two = 0.99
adam_step = 10.0
learn_rate = 0.1
adam_eps = 1e-08
loss_scale = 512.0
norm_eps = 1e-05

def image_columns(picture):
    channels, img_height, img_width = picture.shape
    padded = jnp.pad(picture, ((0, 0), (1, 1), (1, 1)))
    shifted = [padded[:, tap_row:tap_row + img_height, tap_col:tap_col + img_width] for tap_row in range(3) for tap_col in range(3)]
    return jnp.concatenate(shifted, 0).reshape(9 * channels, img_height * img_width)

def normalized(picture, filters, norm_scale, norm_shift):
    columns = image_columns(picture.astype(jnp.bfloat16))
    conv_out = lax.dot_general(filters, columns, (((0,), (0,)), ((), ())), preferred_element_type=jnp.float32)
    center = conv_out - lax.optimization_barrier(jnp.mean(conv_out, axis=1, keepdims=True))
    factor = lax.rsqrt(lax.optimization_barrier(jnp.mean(center * center, axis=1, keepdims=True)) + norm_eps)
    normed = center * factor
    active = norm_scale.astype(jnp.float32)[:, None] * normed + norm_shift.astype(jnp.float32)[:, None]
    return (normed, factor, active)

def embed(picture, filters, norm_scale, norm_shift):
    img_height, img_width = (picture.shape[1], picture.shape[2])
    normed, factor, active = normalized(picture, filters, norm_scale, norm_shift)
    rectified = jnp.maximum(active, 0.0)
    pooled = rectified.reshape(-1, img_height // 2, 2, img_width // 2, 2).mean(axis=(2, 4))
    return pooled.reshape(pooled.shape[0], -1)

def image_grad(picture, filters, norm_scale, norm_shift, upstream):
    channels, img_height, img_width = picture.shape
    normed, factor, active = normalized(picture, filters, norm_scale, norm_shift)
    depth = upstream.shape[0]
    spread = jnp.broadcast_to(upstream.reshape(depth, img_height // 2, 1, img_width // 2, 1), (depth, img_height // 2, 2, img_width // 2, 2))
    spread = spread.reshape(depth, img_height * img_width) * 0.25
    through = jnp.where(active > 0.0, spread, 0.0) * norm_scale.astype(jnp.float32)[:, None]
    inner_grad = factor * (through - lax.optimization_barrier(jnp.mean(through, axis=1, keepdims=True)) - normed * lax.optimization_barrier(jnp.mean(through * normed, axis=1, keepdims=True)))
    column_grad = jnp.dot(filters, inner_grad.astype(jnp.bfloat16), preferred_element_type=jnp.float32)
    pieces = column_grad.reshape(9, channels, img_height, img_width)
    canvas = jnp.zeros((channels, img_height + 2, img_width + 2), jnp.float32)
    for tap_row in range(3):
        for tap_col in range(3):
            canvas = canvas + jnp.pad(pieces[tap_row * 3 + tap_col], ((0, 0), (tap_row, 2 - tap_row), (tap_col, 2 - tap_col)))
    return canvas[:, 1:-1, 1:-1]

def adam_update(synthetic, first, second, image_grads):
    first_new = beta_one * first + (1.0 - beta_one) * image_grads
    second_new = beta_two * second + (1.0 - beta_two) * image_grads * image_grads
    corrected = first_new / (1.0 - beta_one ** adam_step)
    scale_hat = jnp.sqrt(second_new / (1.0 - beta_two ** adam_step))
    return (synthetic - learn_rate * corrected / (scale_hat + adam_eps), first_new, second_new)

def reference(syn_images, adam_first, adam_second, real_pool, real_pick, real_count, syn_order, conv_weight, norm_gain, norm_bias):
    zero_feats = jnp.zeros((WIDTH, HT // 2 * (WD // 2)), jnp.float32)

    def per_class(element):
        synthetic, first, second, pool_rows, pick_rows, all_counts, order = element
        row_ids = (jnp.arange(N_WIDE, dtype=jnp.int32)[:, None] * RLOC + pick_rows).reshape(-1)
        used = (jnp.arange(RLOC, dtype=jnp.int32)[None, :] < all_counts[:, None]).reshape(-1)

        def add_real(running, entry):
            row_id, flag = entry
            picture = pool_rows[row_id]
            return (running + lax.cond(flag, lambda: embed(picture, conv_weight, norm_gain, norm_bias), lambda: zero_feats), None)
        real_sum, _ = lax.scan(add_real, zero_feats, (row_ids, used))
        chosen = jnp.any(order[:SBATCH][None, :] == jnp.arange(IPC, dtype=jnp.int32)[:, None], axis=1)

        def add_syn(running, entry):
            picture, flag = entry
            return (running + lax.cond(flag, lambda: embed(picture, conv_weight, norm_gain, norm_bias), lambda: zero_feats), None)
        syn_sum, _ = lax.scan(add_syn, zero_feats, (synthetic, chosen))
        mean_gap = syn_sum / SBATCH - real_sum / jnp.sum(all_counts).astype(jnp.float32)
        upstream = 2.0 * loss_scale / SBATCH * mean_gap

        def one_grad(entry):
            picture, flag = entry
            return lax.cond(flag, lambda: image_grad(picture, conv_weight, norm_gain, norm_bias, upstream), lambda: jnp.zeros_like(picture))
        image_grads = lax.map(one_grad, (synthetic, chosen))
        return adam_update(synthetic, first, second, image_grads)
    new_images, new_first, new_second = lax.map(per_class, (syn_images, adam_first, adam_second, real_pool, real_pick, real_count, syn_order))
    return (new_images, new_first, new_second)
```

```python
import functools

import jax
import jax.numpy as jnp
import numpy as np
from jax import lax
from jax.experimental import pallas as pl
from jax.experimental.pallas import tpu as pltpu
from jax.sharding import PartitionSpec as P

beta_one = 0.9
beta_two = 0.99
adam_step = 10.0
learn_rate = 0.1
adam_eps = 1e-08
loss_scale = 512.0
norm_eps = 1e-05

LANES = 128
SLOTS = 8
f32 = jnp.float32
bf16 = jnp.bfloat16


def mm(a, b):
    return lax.dot_general(a, b, (((1,), (0,)), ((), ())), preferred_element_type=f32)


class Plan:
    def __init__(self, channels, height, width, depth):
        self.channels, self.height, self.width, self.depth = channels, height, width, depth
        self.cols = width // 2
        self.halves = LANES // self.cols
        self.rows = height // self.halves
        self.pairs = self.rows // 4
        self.span = self.pairs * SLOTS
        self.lanes = self.pairs * LANES
        self.taps = 9 * channels
        self.taps_pad = -(-self.taps // 32) * 32
        self.used = 4 * channels * SLOTS
        self.deep = -(-self.used // LANES) * LANES
        self.groups = 8
        self.pixels = height * width

    def pick_rows(self):
        out = np.zeros((self.halves, self.pairs, SLOTS, self.height), np.float32)
        for half in range(self.halves):
            for pair in range(self.pairs):
                for slot in range(6):
                    row = half * self.rows + 4 * pair + slot - 1
                    if 0 <= row < self.height:
                        out[half, pair, slot, row] = 1.0
        return out.reshape(self.halves * self.span, self.height)

    def pick_cols(self):
        out = np.zeros((self.halves, self.width, 4, self.halves, self.cols), np.float32)
        for shift in range(4):
            for col in range(self.cols):
                src = 2 * col + shift - 1
                if 0 <= src < self.width:
                    for half in range(self.halves):
                        out[half, src, shift, half, col] = 1.0
        return out.reshape(self.halves * self.width, 4 * LANES)

    def pick_taps(self):
        out = np.zeros((2, 2, 2, self.deep, self.taps_pad), np.float32)
        for odd in range(2):
            for a in range(2):
                for b in range(2):
                    for i in range(3):
                        for j in range(3):
                            for c in range(self.channels):
                                k = ((b + j) * self.channels + c) * SLOTS + 2 * odd + a + i
                                out[odd, a, b, k, (i * 3 + j) * self.channels + c] = 1.0
        return out.reshape(self.groups * self.deep, self.taps_pad)


def spread(row):
    return jnp.broadcast_to(row, (LANES, row.shape[1])).T


def split_two(x):
    high = x.astype(bf16)
    return high, (x - high.astype(f32)).astype(bf16)


def build_cols(plan, planes, prow, pcol):
    picked = mm(prow, jnp.concatenate(planes, axis=1)).astype(bf16)
    blocks = []
    for c in range(plan.channels):
        blocks.append(
            jnp.concatenate(
                [
                    picked[half * plan.span : (half + 1) * plan.span, c * plan.width : (c + 1) * plan.width]
                    for half in range(plan.halves)
                ],
                axis=1,
            )
        )
    moved = mm(jnp.concatenate(blocks, axis=0), pcol)
    out = []
    for pair in range(plan.pairs):
        out.append(
            jnp.concatenate(
                [
                    moved[
                        c * plan.span + pair * SLOTS : c * plan.span + (pair + 1) * SLOTS,
                        s * LANES : (s + 1) * LANES,
                    ]
                    for s in range(4)
                    for c in range(plan.channels)
                ],
                axis=0,
            )
        )
    return out


def forward_kernel(
    plan, n_own, batch, where_ref, pick_ref, count_ref, order_ref,
    pool_ref, syn_ref, prow_ref, pcol_ref, ptap_ref, param_ref,
    part_ref, cols_ref, vsum_ref, hits_ref, stat_ref, wl_ref, wt_ref,
    rcols_ref, thr_ref, coef_ref,
):
    D, G, KP, KU = plan.depth, plan.groups, plan.deep, plan.used
    pos = where_ref[0]
    own_count = count_ref[0, pos]
    total = lax.fori_loop(0, count_ref.shape[1], lambda i, t: t + count_ref[0, i], jnp.int32(0))

    taps = param_ref[0 : plan.taps_pad, :]
    spread_taps = mm(ptap_ref[...], taps)
    for g in range(G):
        block = spread_taps[g * KP : (g + 1) * KP, :]
        wt_ref[:, g * D : (g + 1) * D] = block.astype(bf16)
        wl_ref[g * D : (g + 1) * D, :] = block.T.astype(bf16)
    gain = param_ref[plan.taps_pad : plan.taps_pad + 1, :].astype(f32)
    bias = param_ref[plan.taps_pad + 1 : plan.taps_pad + 2, :].astype(f32)

    part_ref[...] = jnp.zeros_like(part_ref)

    def prepare(planes, cref):
        pieces = build_cols(plan, planes, prow_ref[...], pcol_ref[...])
        sums = functools.reduce(lambda a, b: a + b, pieces)
        mean_k = jnp.sum(sums, axis=1, keepdims=True) * (1.0 / plan.lanes)
        shift = jnp.round(mean_k * 4.0) * 0.25
        gram = None
        for pair, piece in enumerate(pieces):
            cref[0:KU, pair * LANES : (pair + 1) * LANES] = piece.astype(bf16)
        moved = jnp.concatenate([(piece - shift).astype(bf16) for piece in pieces], axis=1)
        gram = lax.dot_general(moved, moved, (((1,), (1,)), ((), ())), preferred_element_type=f32)
        wt = wt_ref[0:KU, :]
        g_high = gram.astype(bf16)
        rest = gram - g_high.astype(f32)
        g_mid = rest.astype(bf16)
        g_low = (rest - g_mid.astype(f32)).astype(bf16)
        quad = mm(g_high, wt) + (mm(g_mid, wt) + mm(g_low, wt))
        wide = wt.astype(f32)
        second = jnp.sum(quad * wide, axis=0, keepdims=True)
        rest_mean = jnp.sum(wide * (mean_k - shift), axis=0, keepdims=True)
        shift_mean = jnp.sum(wide * shift, axis=0, keepdims=True)

        def over_groups(row):
            return functools.reduce(lambda a, b: a + b, [row[:, g * D : (g + 1) * D] for g in range(G)])

        off = over_groups(rest_mean) * (1.0 / G)
        mean = off + over_groups(shift_mean) * (1.0 / G)
        var = jnp.maximum(over_groups(second) * (1.0 / plan.pixels) - off * off, 0.0)
        factor = lax.rsqrt(var + norm_eps)
        scale = gain * factor
        thr = mean - bias / scale
        return mean, factor, scale, thr

    def zero_tail(cref):
        if KP > KU:
            cref[KU:KP, :] = jnp.zeros((KP - KU, plan.lanes), bf16)

    zero_tail(rcols_ref)
    tile = 2 * LANES

    def widen(x):
        return jnp.concatenate([x, x], axis=1)

    def real_step(i, carry):
        row = pick_ref[0, 0, i]
        planes = [pool_ref[row, c] for c in range(plan.channels)]
        mean, factor, scale, thr = prepare(planes, rcols_ref)
        thr_ref[...] = spread(thr)
        coef_ref[...] = spread(scale) * (-0.25 / total.astype(f32))

        def one_tile(t, c2):
            at = pl.multiple_of(t * tile, tile)
            y = mm(wl_ref[...], rcols_ref[:, pl.ds(at, tile)])
            thr_w = widen(thr_ref[...])
            coef_w = widen(coef_ref[...])
            for odd in range(2):
                ys = [jnp.maximum(y[(odd * 4 + p) * D : (odd * 4 + p + 1) * D, :], thr_w) for p in range(4)]
                v = (ys[0] + ys[1]) + (ys[2] + ys[3]) - 4.0 * thr_w
                part_ref[odd * D : (odd + 1) * D, pl.ds(at, tile)] += coef_w * v
            return c2

        lax.fori_loop(0, plan.lanes // tile, one_tile, 0)
        return carry

    lax.fori_loop(0, own_count, real_step, 0)

    for i in range(n_own):
        gid = pos * n_own + i
        flag = lax.fori_loop(0, batch, lambda j, t: t | (order_ref[0, j] == gid).astype(jnp.int32), jnp.int32(0))

        @pl.when(flag > 0)
        def _():
            cref = cols_ref.at[i]
            zero_tail(cref)
            planes = [syn_ref[i, c].astype(bf16) for c in range(plan.channels)]
            mean, factor, scale, thr = prepare(planes, cref)
            for n, row in enumerate((mean, factor, scale, thr, gain, bias)):
                stat_ref[i, n] = spread(row)
            coef_ref[...] = spread(scale) * (0.25 / batch)

            def one_tile(t, c2):
                at = pl.multiple_of(t * tile, tile)
                y = mm(wl_ref[...], cols_ref[i, :, pl.ds(at, tile)])
                thr_w = widen(stat_ref[i, 3])
                coef_w = widen(coef_ref[...])
                for odd in range(2):
                    yp = [y[(odd * 4 + p) * D : (odd * 4 + p + 1) * D, :] for p in range(4)]
                    ys = [jnp.maximum(a, thr_w) for a in yp]
                    hs = [jnp.where(a > thr_w, 1.0, 0.0) for a in yp]
                    v = (ys[0] + ys[1]) + (ys[2] + ys[3]) - 4.0 * thr_w
                    h = (hs[0] + hs[1]) + (hs[2] + hs[3])
                    rows = slice(odd * D, (odd + 1) * D)
                    part_ref[rows, pl.ds(at, tile)] += coef_w * v
                    vsum_ref[i, rows, pl.ds(at, tile)] = v
                    hits_ref[i, rows, pl.ds(at, tile)] = h.astype(bf16)
                return c2

            lax.fori_loop(0, plan.lanes // tile, one_tile, 0)


def backward_kernel(
    plan, n_own, batch, where_ref, order_ref,
    gap_ref, cols_ref, vsum_ref, hits_ref, stat_ref, wl_ref, wt_ref, prow_ref, pcol_ref,
    syn_ref, first_ref, second_ref,
    new_syn_ref, new_first_ref, new_second_ref,
    grad_ref, inner_ref, dcols_ref, col_ref,
):
    D, KU = plan.depth, plan.used
    pos = where_ref[0]
    tile = 2 * LANES
    grad_factor = 2.0 * loss_scale / batch

    def widen(x):
        return jnp.concatenate([x, x], axis=1)

    for i in range(n_own):
        gid = pos * n_own + i
        flag = lax.fori_loop(0, batch, lambda j, t: t | (order_ref[0, j] == gid).astype(jnp.int32), jnp.int32(0))

        @pl.when(flag == 0)
        def _():
            grad_ref[...] = jnp.zeros_like(grad_ref)

        @pl.when(flag > 0)
        def _():
            mean, factor, scale, thr, gain, bias = [stat_ref[i, n] for n in range(6)]

            def sums(t, carry):
                one, two = carry
                at = pl.multiple_of(t * LANES, LANES)
                for odd in range(2):
                    rows = slice(odd * D, (odd + 1) * D)
                    gap = gap_ref[rows, pl.ds(at, LANES)]
                    one = one + gap * hits_ref[i, rows, pl.ds(at, LANES)].astype(f32)
                    two = two + gap * vsum_ref[i, rows, pl.ds(at, LANES)]
                return one, two

            zero = jnp.zeros((D, LANES), f32)
            one, two = lax.fori_loop(0, plan.pairs, sums, (zero, zero))
            unit = grad_factor / (4.0 * plan.pixels)
            one = jnp.broadcast_to(jnp.sum(one, axis=1, keepdims=True), (D, LANES)) * unit
            two = jnp.broadcast_to(jnp.sum(two, axis=1, keepdims=True), (D, LANES)) * unit
            mean_one = gain * one
            mean_two = scale * (two - one * (bias / scale))
            slope = factor * factor * mean_two
            col_ref[0] = factor * gain * (0.25 * grad_factor)
            col_ref[1] = slope
            col_ref[2] = factor * mean_one - slope * mean

            def one_tile(t, c2):
                at = pl.multiple_of(t * tile, tile)
                y = mm(wl_ref[...], cols_ref[i, :, pl.ds(at, tile)])
                thr_w, up_w, slope_w, base_w = [widen(a) for a in (stat_ref[i, 3], col_ref[0], col_ref[1], col_ref[2])]
                for odd in range(2):
                    off = -base_w
                    on = up_w * gap_ref[odd * D : (odd + 1) * D, pl.ds(at, tile)] - base_w
                    for p in range(4):
                        rows = slice((odd * 4 + p) * D, (odd * 4 + p + 1) * D)
                        yp = y[rows, :]
                        inner_ref[rows, :] = (jnp.where(yp > thr_w, on, off) - slope_w * yp).astype(bf16)
                dcols_ref[:, pl.ds(at, tile)] = mm(wt_ref[0:KU, :], inner_ref[...])
                return c2

            lax.fori_loop(0, plan.lanes // tile, one_tile, 0)

            shifts = []
            for s in range(4):
                shifts.append(
                    jnp.concatenate(
                        [
                            dcols_ref[
                                (s * plan.channels + c) * SLOTS : (s * plan.channels + c + 1) * SLOTS,
                                pair * LANES : (pair + 1) * LANES,
                            ]
                            for c in range(plan.channels)
                            for pair in range(plan.pairs)
                        ],
                        axis=0,
                    )
                )
            high, low = split_two(jnp.concatenate(shifts, axis=1))
            back = (((1,), (1,)), ((), ()))
            pcol = pcol_ref[...]
            wide = lax.dot_general(high, pcol, back, preferred_element_type=f32) + lax.dot_general(
                low, pcol, back, preferred_element_type=f32
            )
            tall = jnp.concatenate(
                [
                    jnp.concatenate(
                        [
                            wide[c * plan.span : (c + 1) * plan.span, half * plan.width : (half + 1) * plan.width]
                            for c in range(plan.channels)
                        ],
                        axis=1,
                    )
                    for half in range(plan.halves)
                ],
                axis=0,
            )
            high, low = split_two(tall)
            prow = prow_ref[...].T
            image = mm(prow, high) + mm(prow, low)
            for c in range(plan.channels):
                grad_ref[c] = image[:, c * plan.width : (c + 1) * plan.width]

        for c in range(plan.channels):
            grad = grad_ref[c]
            first_new = beta_one * first_ref[i, c] + (1.0 - beta_one) * grad
            second_new = beta_two * second_ref[i, c] + (1.0 - beta_two) * grad * grad
            corrected = first_new / (1.0 - beta_one**adam_step)
            scale_hat = jnp.sqrt(second_new / (1.0 - beta_two**adam_step))
            new_syn_ref[i, c] = syn_ref[i, c] - learn_rate * corrected / (scale_hat + adam_eps)
            new_first_ref[i, c] = first_new
            new_second_ref[i, c] = second_new


def gather_params(conv_weight, norm_gain, norm_bias, taps_pad):
    taps, width = conv_weight.shape
    own = jnp.concatenate(
        [
            conv_weight,
            jnp.zeros((taps_pad - taps, width), conv_weight.dtype),
            norm_gain[None],
            norm_bias[None],
            jnp.zeros((14, width), conv_weight.dtype),
        ],
        axis=0,
    )
    if lax.axis_size("cls") == 2:
        other = lax.ppermute(own, "cls", [(0, 1), (1, 0)])
        low = lax.axis_index("cls") == 0
        return jnp.concatenate([jnp.where(low, own, other), jnp.where(low, other, own)], axis=1)
    return lax.all_gather(own, "cls", axis=1, tiled=True)


def exchange_sum(part):
    n = lax.axis_size("wide")
    pos = lax.axis_index("wide")
    steps = []
    step = 1
    while step < n:
        steps.append(step)
        step *= 2

    def swap(x, step):
        return lax.ppermute(x, "wide", [(i, i ^ step) for i in range(n)])

    own = part
    for step in steps:
        high = (pos & step) > 0
        rows = own.shape[0] // 2
        kept = jnp.where(high, own[rows:], own[:rows])
        sent = jnp.where(high, own[:rows], own[rows:])
        own = kept + swap(sent.astype(jnp.float16), step).astype(f32)
    own = own.astype(jnp.float16)
    for step in reversed(steps):
        high = (pos & step) > 0
        other = swap(own, step)
        own = jnp.concatenate([jnp.where(high, other, own), jnp.where(high, own, other)], axis=0)
    return own.astype(f32)


def body(
    syn_images, adam_first, adam_second, real_pool, real_pick, real_count, syn_order,
    conv_weight, norm_gain, norm_bias,
):
    _, n_own, channels, height, width = syn_images.shape
    batch = syn_order.shape[1] // 2
    depth = conv_weight.shape[1] * lax.axis_size("cls")
    plan = Plan(channels, height, width, depth)
    prow = jnp.asarray(plan.pick_rows(), bf16)
    pcol = jnp.asarray(plan.pick_cols(), bf16)
    ptap = jnp.asarray(plan.pick_taps(), bf16)
    params = gather_params(conv_weight, norm_gain, norm_bias, plan.taps_pad)
    where = lax.axis_index("wide").astype(jnp.int32)[None]

    smem = pl.BlockSpec(memory_space=pltpu.SMEM)
    vmem = pl.BlockSpec(memory_space=pltpu.VMEM)
    shape = jax.ShapeDtypeStruct
    rows = 2 * depth
    m_rows = plan.groups * depth
    part, cols, vsum, hits, stat, wl, wt = pl.pallas_call(
        functools.partial(forward_kernel, plan, n_own, batch),
        in_specs=[smem] * 4 + [vmem] * 6,
        out_specs=[vmem] * 7,
        out_shape=[
            shape((rows, plan.lanes), f32),
            shape((n_own, plan.deep, plan.lanes), bf16),
            shape((n_own, rows, plan.lanes), f32),
            shape((n_own, rows, plan.lanes), bf16),
            shape((n_own, 6, depth, LANES), f32),
            shape((m_rows, plan.deep), bf16),
            shape((plan.deep, m_rows), bf16),
        ],
        scratch_shapes=[
            pltpu.VMEM((plan.deep, plan.lanes), bf16),
            pltpu.VMEM((depth, LANES), f32),
            pltpu.VMEM((depth, LANES), f32),
        ],
        name="embed_sums",
    )(where, real_pick, real_count, syn_order, real_pool[0], syn_images[0], prow, pcol, ptap, params)

    gap = exchange_sum(part)

    img = shape((n_own, channels, height, width), f32)
    outs = pl.pallas_call(
        functools.partial(backward_kernel, plan, n_own, batch),
        in_specs=[smem] * 2 + [vmem] * 12,
        out_specs=[vmem] * 3,
        out_shape=[img] * 3,
        scratch_shapes=[
            pltpu.VMEM((channels, height, width), f32),
            pltpu.VMEM((m_rows, 2 * LANES), bf16),
            pltpu.VMEM((plan.used, plan.lanes), f32),
            pltpu.VMEM((3, depth, LANES), f32),
        ],
        name="image_grads",
    )(where, syn_order, gap, cols, vsum, hits, stat, wl, wt, prow, pcol, syn_images[0], adam_first[0], adam_second[0])
    return tuple(out[None] for out in outs)


def solution(mesh):
    image = P("cls", "wide", None, None, None)
    return jax.shard_map(
        body,
        mesh=mesh,
        in_specs=(
            image, image, image, image, P("cls", "wide", None), P("cls", None), P("cls", None),
            P(None, "cls"), P("cls"), P("cls"),
        ),
        out_specs=(image, image, image),
        check_vma=False,
    )
```

```python
import functools

import jax
import jax.numpy as jnp
import numpy as np
from jax import lax
from jax.experimental import pallas as pl
from jax.experimental.pallas import tpu as pltpu
from jax.sharding import PartitionSpec as P

beta_one = 0.9
beta_two = 0.99
adam_step = 10.0
learn_rate = 0.1
adam_eps = 1e-08
loss_scale = 512.0
norm_eps = 1e-05

LANES = 128
SLOTS = 8
f32 = jnp.float32
bf16 = jnp.bfloat16


def mm(a, b):
    return lax.dot_general(a, b, (((1,), (0,)), ((), ())), preferred_element_type=f32)


class Plan:
    def __init__(self, channels, height, width, depth):
        self.channels, self.height, self.width, self.depth = channels, height, width, depth
        self.cols = width // 2
        self.halves = LANES // self.cols
        self.rows = height // self.halves
        self.pairs = self.rows // 4
        self.span = self.pairs * SLOTS
        self.lanes = self.pairs * LANES
        self.taps = 9 * channels
        self.taps_pad = -(-self.taps // 32) * 32
        self.used = 4 * channels * SLOTS
        self.deep = -(-self.used // LANES) * LANES
        self.groups = 8
        self.pixels = height * width

    def pick_rows(self):
        out = np.zeros((self.halves, self.pairs, SLOTS, self.height), np.float32)
        for half in range(self.halves):
            for pair in range(self.pairs):
                for slot in range(6):
                    row = half * self.rows + 4 * pair + slot - 1
                    if 0 <= row < self.height:
                        out[half, pair, slot, row] = 1.0
        return out.reshape(self.halves * self.span, self.height)

    def pick_cols(self):
        out = np.zeros((self.halves, self.width, 4, self.halves, self.cols), np.float32)
        for shift in range(4):
            for col in range(self.cols):
                src = 2 * col + shift - 1
                if 0 <= src < self.width:
                    for half in range(self.halves):
                        out[half, src, shift, half, col] = 1.0
        return out.reshape(self.halves * self.width, 4 * LANES)

    def pick_taps(self):
        out = np.zeros((2, 2, 2, self.deep, self.taps_pad), np.float32)
        for odd in range(2):
            for a in range(2):
                for b in range(2):
                    for i in range(3):
                        for j in range(3):
                            for c in range(self.channels):
                                k = ((b + j) * self.channels + c) * SLOTS + 2 * odd + a + i
                                out[odd, a, b, k, (i * 3 + j) * self.channels + c] = 1.0
        return out.reshape(self.groups * self.deep, self.taps_pad)


def spread(row):
    return jnp.broadcast_to(row, (LANES, row.shape[1])).T


def split_two(x):
    high = x.astype(bf16)
    return high, (x - high.astype(f32)).astype(bf16)


class Prepare:
    def __init__(self, plan, planes, consts, wide_ref, wt_ref, gain, bias, tap_sum_ref):
        self.plan, self.planes, self.consts = plan, planes, consts
        self.wide_ref, self.wt_ref, self.gain, self.bias, self.tap_sum_ref = wide_ref, wt_ref, gain, bias, tap_sum_ref

    def stages(self, cols_ref):
        plan = self.plan
        D, G, KU, C = plan.depth, plan.groups, plan.used, plan.channels
        prow, pcol = self.consts
        shifts = []
        for plane in self.planes:
            rows = plane.astype(f32)
            total = functools.reduce(lambda a, b: a + b, [rows[r : r + 8] for r in range(0, plan.height, 8)])
            total = jnp.sum(jnp.sum(total, axis=1, keepdims=True), axis=0, keepdims=True)
            shifts.append(jnp.round(total * (4.0 / plan.pixels)) * 0.25)
        picked = mm(prow, jnp.concatenate(self.planes, axis=1)).astype(bf16)
        yield
        blocks = []
        for c in range(C):
            blocks.append(
                jnp.concatenate(
                    [
                        picked[h * plan.span : (h + 1) * plan.span, c * plan.width : (c + 1) * plan.width]
                        for h in range(plan.halves)
                    ],
                    axis=1,
                )
            )
        moved = mm(jnp.concatenate(blocks, axis=0), pcol)
        yield
        lean = []
        for pair in range(plan.pairs):
            parts = [
                (c, moved[c * plan.span + pair * SLOTS : c * plan.span + (pair + 1) * SLOTS, s * LANES : (s + 1) * LANES])
                for s in range(4)
                for c in range(C)
            ]
            cols_ref[0:KU, pair * LANES : (pair + 1) * LANES] = jnp.concatenate([x for _, x in parts], axis=0).astype(bf16)
            lean.append(jnp.concatenate([x - shifts[c] for c, x in parts], axis=0).astype(bf16))
            if pair == plan.pairs // 2 - 1:
                yield
        lean = jnp.concatenate(lean, axis=1)
        lean = jnp.concatenate([lean, jnp.ones((16, plan.lanes), bf16)], axis=0)
        yield
        gram = lax.dot_general(lean, lean, (((1,), (1,)), ((), ())), preferred_element_type=f32)
        gram = gram[:, 0:KU]
        high = gram.astype(bf16)
        rest = gram - high.astype(f32)
        mid = rest.astype(bf16)
        low = (rest - mid.astype(f32)).astype(bf16)
        yield
        fill = jnp.zeros((KU + 16, plan.deep - KU), bf16)
        three = jnp.concatenate([high, fill, mid, fill, low, fill] if plan.deep > KU else [high, mid, low], axis=1)
        wt = self.wt_ref[...]
        quad = mm(three, jnp.concatenate([wt, wt, wt], axis=0))
        yield
        second = jnp.sum(quad[0:KU, :] * self.wide_ref[...], axis=0, keepdims=True)

        def over_groups(row):
            return functools.reduce(lambda a, b: a + b, [row[:, g * D : (g + 1) * D] for g in range(G)])

        off = over_groups(quad[KU : KU + 1, :]) * (1.0 / plan.pixels)
        mean = off
        for c in range(C):
            mean = mean + shifts[c] * self.tap_sum_ref[c : c + 1, :]
        var = jnp.maximum(over_groups(second) * (1.0 / plan.pixels) - off * off, 0.0)
        self.factor = lax.rsqrt(var + norm_eps)
        self.scale = self.gain * self.factor
        self.mean = mean
        self.thr = mean - self.bias / self.scale
        yield


def is_chosen(order_ref, batch, gid):
    return lax.fori_loop(0, batch, lambda j, t: t | (order_ref[0, j] == gid).astype(jnp.int32), jnp.int32(0))


def make_weights(plan, param_ref, ptap_ref, wide_ref, wt_ref, wl_ref, tap_sum_ref):
    D, G, KP, KU, C = plan.depth, plan.groups, plan.deep, plan.used, plan.channels
    spread_taps = mm(ptap_ref[...], param_ref[0 : plan.taps_pad, :])
    for g in range(G):
        odd, phase = divmod(g, 4)
        block = spread_taps[g * KP : (g + 1) * KP, :]
        wt_ref[:, g * D : (g + 1) * D] = block.astype(bf16)
        wide_ref[:, g * D : (g + 1) * D] = block[0:KU]
        turned = block.T.astype(bf16)
        for blk in range(D // 16):
            at = ((odd * (D // 16) + blk) * 4 + phase) * 16
            wl_ref[at : at + 16, :] = turned[blk * 16 : (blk + 1) * 16, :]
    first = spread_taps[0:KU, :]
    for c in range(C):
        tap_sum_ref[c : c + 1, :] = jnp.sum(
            functools.reduce(lambda a, b: a + b, [first[(s * C + c) * SLOTS : (s * C + c + 1) * SLOTS] for s in range(4)]),
            axis=0,
            keepdims=True,
        )


def forward_kernel(
    plan, n_own, batch, where_ref, pick_ref, count_ref, order_ref,
    pool_ref, syn_ref, prow_ref, pcol_ref, ptap_ref, param_ref,
    part_ref, wl_ref,
    all_ref, wide_ref, wt_ref, tap_sum_ref, now_ref, next_ref, thr_ref, coef_ref, thr_next_ref, coef_next_ref,
):
    D, KP, KU, C = plan.depth, plan.deep, plan.used, plan.channels
    pos = where_ref[0]
    n_pool = pool_ref.shape[0]
    own_count = count_ref[0, pos]
    total = lax.fori_loop(0, count_ref.shape[1], lambda i, t: t + count_ref[0, i], jnp.int32(0)).astype(f32)
    flags = [is_chosen(order_ref, batch, pos * n_own + i) for i in range(n_own)]
    n_syn = functools.reduce(lambda a, b: a + b, flags)

    make_weights(plan, param_ref, ptap_ref, wide_ref, wt_ref, wl_ref, tap_sum_ref)
    gain = param_ref[plan.taps_pad : plan.taps_pad + 1, :].astype(f32)
    bias = param_ref[plan.taps_pad + 1 : plan.taps_pad + 2, :].astype(f32)
    for i in range(n_own):
        all_ref[n_pool + i] = syn_ref[i].astype(bf16)
    all_ref[0:n_pool] = pool_ref[...]
    part_ref[...] = jnp.zeros_like(part_ref)
    if KP > KU:
        now_ref[KU:KP, :] = jnp.zeros((KP - KU, plan.lanes), bf16)

    def image_of(i):
        syn_at = jnp.int32(n_pool + n_own - 1)
        before = n_syn
        for s in reversed(range(n_own)):
            before = before - flags[s]
            syn_at = jnp.where((flags[s] > 0) & (i == before), n_pool + s, syn_at)
        real_at = pick_ref[0, 0, jnp.clip(i - n_syn, 0, n_pool - 1)]
        return jnp.where(i < n_syn, syn_at, real_at), jnp.where(i < n_syn, 0.25 / batch, -0.25 / total)

    def begin(i):
        at, weight = image_of(i)
        planes = [all_ref[at, c] for c in range(C)]
        return Prepare(plan, planes, (prow_ref[...], pcol_ref[...]), wide_ref, wt_ref, gain, bias, tap_sum_ref), weight

    prep, weight = begin(jnp.int32(0))
    for _ in prep.stages(now_ref):
        pass
    thr_ref[...] = spread(prep.thr)
    coef_ref[...] = spread(prep.scale * weight)
    tile = 2 * LANES

    def step(i, base):
        prep, weight = begin(i + 1)
        ahead = prep.stages(next_ref)
        base = base + coef_ref[...] * thr_ref[...]
        for t in range(plan.lanes // tile):
            at = t * tile
            y = mm(wl_ref[...], now_ref[:, at : at + tile])
            next(ahead, None)
            for odd in range(2):
                for blk in range(D // 16):
                    r0 = (odd * (D // 16) + blk) * 64
                    thr = thr_ref[blk * 16 : (blk + 1) * 16, :]
                    coef = coef_ref[blk * 16 : (blk + 1) * 16, :]
                    out = slice(odd * D + blk * 16, odd * D + (blk + 1) * 16)
                    for half in range(2):
                        lanes = slice(half * LANES, (half + 1) * LANES)
                        ys = [jnp.maximum(y[r0 + p * 16 : r0 + (p + 1) * 16, lanes], thr) for p in range(4)]
                        here = slice(at + half * LANES, at + (half + 1) * LANES)
                        part_ref[out, here] += coef * ((ys[0] + ys[1]) + (ys[2] + ys[3]))
        for _ in ahead:
            pass
        now_ref[0:KU, :] = next_ref[0:KU, :]
        thr_ref[...] = spread(prep.thr)
        coef_ref[...] = spread(prep.scale * weight)
        return base

    base = lax.fori_loop(0, n_syn + own_count, step, jnp.zeros((D, LANES), f32))
    base = 4.0 * base
    for pair in range(plan.pairs):
        for odd in range(2):
            part_ref[odd * D : (odd + 1) * D, pair * LANES : (pair + 1) * LANES] -= base


def middle_kernel(
    plan, n_own, batch, where_ref, order_ref, syn_ref, prow_ref, pcol_ref, ptap_ref, param_ref,
    cols_ref, vsum_ref, hits_ref, stat_ref, wlt_ref,
    wl_ref, wide_ref, wt_ref, tap_sum_ref,
):
    D, KP, KU, C = plan.depth, plan.deep, plan.used, plan.channels
    pos = where_ref[0]
    make_weights(plan, param_ref, ptap_ref, wide_ref, wt_ref, wl_ref, tap_sum_ref)
    for g in range(plan.groups):
        wlt_ref[:, g * D : (g + 1) * D] = wl_ref[g * D : (g + 1) * D, :].astype(f32).T.astype(bf16)[0:KU, :]
    gain = param_ref[plan.taps_pad : plan.taps_pad + 1, :].astype(f32)
    bias = param_ref[plan.taps_pad + 1 : plan.taps_pad + 2, :].astype(f32)
    tile = 2 * LANES
    for i in range(n_own):
        flag = is_chosen(order_ref, batch, pos * n_own + i)

        @pl.when(flag > 0)
        def _():
            if KP > KU:
                cols_ref[i, KU:KP, :] = jnp.zeros((KP - KU, plan.lanes), bf16)
            planes = [syn_ref[i, c].astype(bf16) for c in range(C)]
            prep = Prepare(plan, planes, (prow_ref[...], pcol_ref[...]), wide_ref, wt_ref, gain, bias, tap_sum_ref)
            for _ in prep.stages(cols_ref.at[i]):
                pass
            for n, row in enumerate((prep.mean, prep.factor, prep.scale, prep.thr, gain, bias)):
                stat_ref[i, n] = spread(row)

            def one_tile(t, carry):
                at = pl.multiple_of(t * tile, tile)
                y = mm(wl_ref[...], cols_ref[i, :, pl.ds(at, tile)])
                for odd in range(2):
                    for blk in range(D // 16):
                        r0 = (odd * (D // 16) + blk) * 64
                        thr = stat_ref[i, 3, blk * 16 : (blk + 1) * 16, :]
                        out = slice(odd * D + blk * 16, odd * D + (blk + 1) * 16)
                        for half in range(2):
                            lanes = slice(half * LANES, (half + 1) * LANES)
                            yp = [y[r0 + p * 16 : r0 + (p + 1) * 16, lanes] for p in range(4)]
                            ys = [jnp.maximum(a, thr) for a in yp]
                            hs = [jnp.where(a > thr, 1.0, 0.0) for a in yp]
                            here = pl.ds(at + half * LANES, LANES)
                            vsum_ref[i, out, here] = (((ys[0] + ys[1]) + (ys[2] + ys[3])) - 4.0 * thr)
                            hits_ref[i, out, here] = ((hs[0] + hs[1]) + (hs[2] + hs[3])).astype(bf16)
                return carry

            lax.fori_loop(0, plan.lanes // tile, one_tile, 0)


def backward_kernel(
    plan, n_own, batch, where_ref, order_ref,
    gap_ref, cols_ref, vsum_ref, hits_ref, stat_ref, wl_ref, wlt_ref, prow_ref, pcol_ref,
    syn_ref, first_ref, second_ref,
    new_syn_ref, new_first_ref, new_second_ref,
    grad_ref, inner_ref, dcols_ref, col_ref,
):
    D, KU = plan.depth, plan.used
    pos = where_ref[0]
    tile = 2 * LANES
    grad_factor = 2.0 * loss_scale / batch

    for i in range(n_own):
        flag = is_chosen(order_ref, batch, pos * n_own + i)

        @pl.when(flag == 0)
        def _():
            grad_ref[...] = jnp.zeros_like(grad_ref)

        @pl.when(flag > 0)
        def _():
            mean, factor, scale, thr, gain, bias = [stat_ref[i, n] for n in range(6)]

            def sums(t, carry):
                one, two = carry
                at = pl.multiple_of(t * LANES, LANES)
                for odd in range(2):
                    rows = slice(odd * D, (odd + 1) * D)
                    gap = gap_ref[rows, pl.ds(at, LANES)]
                    one = one + gap * hits_ref[i, rows, pl.ds(at, LANES)].astype(f32)
                    two = two + gap * vsum_ref[i, rows, pl.ds(at, LANES)]
                return one, two

            zero = jnp.zeros((D, LANES), f32)
            one, two = lax.fori_loop(0, plan.pairs, sums, (zero, zero))
            unit = grad_factor / (4.0 * plan.pixels)
            one = jnp.broadcast_to(jnp.sum(one, axis=1, keepdims=True), (D, LANES)) * unit
            two = jnp.broadcast_to(jnp.sum(two, axis=1, keepdims=True), (D, LANES)) * unit
            mean_one = gain * one
            mean_two = scale * (two - one * (bias / scale))
            slope = factor * factor * mean_two
            col_ref[0] = factor * gain * (0.25 * grad_factor)
            col_ref[1] = slope
            col_ref[2] = slope * mean - factor * mean_one

            for t in range(plan.lanes // tile):
                at = t * tile
                y = mm(wl_ref[...], cols_ref[i, :, at : at + tile])
                slot = t % 2
                for odd in range(2):
                    for blk in range(D // 16):
                        r0 = (odd * (D // 16) + blk) * 64
                        chan = slice(blk * 16, (blk + 1) * 16)
                        thr_b, up_b, slope_b, off = stat_ref[i, 3, chan, :], col_ref[0, chan, :], col_ref[1, chan, :], col_ref[2, chan, :]
                        for half in range(2):
                            lanes = slice(half * LANES, (half + 1) * LANES)
                            gap = gap_ref[odd * D + blk * 16 : odd * D + (blk + 1) * 16, at + half * LANES : at + (half + 1) * LANES]
                            on = up_b * gap + off
                            for p in range(4):
                                rows = slice(r0 + p * 16, r0 + (p + 1) * 16)
                                yp = y[rows, lanes]
                                inner_ref[slot, rows, lanes] = (jnp.where(yp > thr_b, on, off) - slope_b * yp).astype(bf16)
                dcols_ref[:, at : at + tile] = mm(wlt_ref[...], inner_ref[slot])

            shifts = []
            for s in range(4):
                shifts.append(
                    jnp.concatenate(
                        [
                            dcols_ref[
                                (s * plan.channels + c) * SLOTS : (s * plan.channels + c + 1) * SLOTS,
                                pair * LANES : (pair + 1) * LANES,
                            ]
                            for c in range(plan.channels)
                            for pair in range(plan.pairs)
                        ],
                        axis=0,
                    )
                )
            high, low = split_two(jnp.concatenate(shifts, axis=1))
            back = (((1,), (1,)), ((), ()))
            pcol = pcol_ref[...]
            wide = lax.dot_general(high, pcol, back, preferred_element_type=f32) + lax.dot_general(
                low, pcol, back, preferred_element_type=f32
            )
            tall = jnp.concatenate(
                [
                    jnp.concatenate(
                        [
                            wide[c * plan.span : (c + 1) * plan.span, half * plan.width : (half + 1) * plan.width]
                            for c in range(plan.channels)
                        ],
                        axis=1,
                    )
                    for half in range(plan.halves)
                ],
                axis=0,
            )
            high, low = split_two(tall)
            prow = prow_ref[...].T
            image = mm(prow, high) + mm(prow, low)
            for c in range(plan.channels):
                grad_ref[c] = image[:, c * plan.width : (c + 1) * plan.width]

        for c in range(plan.channels):
            grad = grad_ref[c]
            first_new = beta_one * first_ref[i, c] + (1.0 - beta_one) * grad
            second_new = beta_two * second_ref[i, c] + (1.0 - beta_two) * grad * grad
            corrected = first_new / (1.0 - beta_one**adam_step)
            scale_hat = jnp.sqrt(second_new / (1.0 - beta_two**adam_step))
            new_syn_ref[i, c] = syn_ref[i, c] - learn_rate * corrected / (scale_hat + adam_eps)
            new_first_ref[i, c] = first_new
            new_second_ref[i, c] = second_new


def gather_params(conv_weight, norm_gain, norm_bias, taps_pad):
    taps, width = conv_weight.shape
    own = jnp.concatenate(
        [
            conv_weight,
            jnp.zeros((taps_pad - taps, width), conv_weight.dtype),
            norm_gain[None],
            norm_bias[None],
            jnp.zeros((14, width), conv_weight.dtype),
        ],
        axis=0,
    )
    if lax.axis_size("cls") == 2:
        other = lax.ppermute(own, "cls", [(0, 1), (1, 0)])
        low = lax.axis_index("cls") == 0
        return jnp.concatenate([jnp.where(low, own, other), jnp.where(low, other, own)], axis=1)
    return lax.all_gather(own, "cls", axis=1, tiled=True)


def exchange_sum(part):
    n = lax.axis_size("wide")
    pos = lax.axis_index("wide")
    steps = []
    step = 1
    while step < n:
        steps.append(step)
        step *= 2

    def swap(x, step):
        return lax.ppermute(x, "wide", [(i, i ^ step) for i in range(n)])

    own = part
    for step in steps:
        high = (pos & step) > 0
        rows = own.shape[0] // 2
        kept = jnp.where(high, own[rows:], own[:rows])
        sent = jnp.where(high, own[:rows], own[rows:])
        own = kept + swap(sent.astype(jnp.float16), step).astype(f32)
    own = own.astype(jnp.float16)
    for step in reversed(steps):
        high = (pos & step) > 0
        other = swap(own, step)
        own = jnp.concatenate([jnp.where(high, other, own), jnp.where(high, own, other)], axis=0)
    return own.astype(f32)


def body(
    syn_images, adam_first, adam_second, real_pool, real_pick, real_count, syn_order,
    conv_weight, norm_gain, norm_bias,
):
    _, n_own, channels, height, width = syn_images.shape
    batch = syn_order.shape[1] // 2
    depth = conv_weight.shape[1] * lax.axis_size("cls")
    plan = Plan(channels, height, width, depth)
    prow = jnp.asarray(plan.pick_rows(), bf16)
    pcol = jnp.asarray(plan.pick_cols(), bf16)
    ptap = jnp.asarray(plan.pick_taps(), bf16)
    params = gather_params(conv_weight, norm_gain, norm_bias, plan.taps_pad)
    where = lax.axis_index("wide").astype(jnp.int32)[None]

    smem = pl.BlockSpec(memory_space=pltpu.SMEM)
    vmem = pl.BlockSpec(memory_space=pltpu.VMEM)
    shape = jax.ShapeDtypeStruct
    rows = 2 * depth
    m_rows = plan.groups * depth
    weights = [
        pltpu.VMEM((plan.used, m_rows), f32),
        pltpu.VMEM((plan.deep, m_rows), bf16),
        pltpu.VMEM((8, depth), f32),
    ]
    part, wl = pl.pallas_call(
        functools.partial(forward_kernel, plan, n_own, batch),
        in_specs=[smem] * 4 + [vmem] * 6,
        out_specs=[vmem] * 2,
        out_shape=[shape((rows, plan.lanes), f32), shape((m_rows, plan.deep), bf16)],
        scratch_shapes=[
            pltpu.VMEM((real_pool.shape[1] + n_own, channels, height, width), bf16),
            *weights,
            pltpu.VMEM((plan.deep, plan.lanes), bf16),
            pltpu.VMEM((plan.used, plan.lanes), bf16),
            *[pltpu.VMEM((depth, LANES), f32)] * 4,
        ],
        name="embed_sums",
    )(where, real_pick, real_count, syn_order, real_pool[0], syn_images[0], prow, pcol, ptap, params)

    cols, vsum, hits, stat, wlt = pl.pallas_call(
        functools.partial(middle_kernel, plan, n_own, batch),
        in_specs=[smem] * 2 + [vmem] * 5,
        out_specs=[vmem] * 5,
        out_shape=[
            shape((n_own, plan.deep, plan.lanes), bf16),
            shape((n_own, rows, plan.lanes), f32),
            shape((n_own, rows, plan.lanes), bf16),
            shape((n_own, 6, depth, LANES), f32),
            shape((plan.used, m_rows), bf16),
        ],
        scratch_shapes=[pltpu.VMEM((m_rows, plan.deep), bf16), *weights],
        name="syn_features",
    )(where, syn_order, syn_images[0], prow, pcol, ptap, params)

    gap = exchange_sum(part)

    img = shape((n_own, channels, height, width), f32)
    outs = pl.pallas_call(
        functools.partial(backward_kernel, plan, n_own, batch),
        in_specs=[smem] * 2 + [vmem] * 12,
        out_specs=[vmem] * 3,
        out_shape=[img] * 3,
        scratch_shapes=[
            pltpu.VMEM((channels, height, width), f32),
            pltpu.VMEM((2, m_rows, 2 * LANES), bf16),
            pltpu.VMEM((plan.used, plan.lanes), f32),
            pltpu.VMEM((3, depth, LANES), f32),
        ],
        name="image_grads",
    )(where, syn_order, gap, cols, vsum, hits, stat, wl, wlt, prow, pcol, syn_images[0], adam_first[0], adam_second[0])
    return tuple(out[None] for out in outs)


def solution(mesh):
    image = P("cls", "wide", None, None, None)
    return jax.shard_map(
        body,
        mesh=mesh,
        in_specs=(
            image, image, image, image, P("cls", "wide", None), P("cls", None), P("cls", None),
            P(None, "cls"), P("cls"), P("cls"),
        ),
        out_specs=(image, image, image),
        check_vma=False,
    )
```

```python
import functools

import jax
import jax.numpy as jnp
import numpy as np
from jax import lax
from jax.experimental import pallas as pl
from jax.experimental.pallas import tpu as pltpu
from jax.sharding import PartitionSpec as P

beta_one = 0.9
beta_two = 0.99
adam_step = 10.0
learn_rate = 0.1
adam_eps = 1e-08
loss_scale = 512.0
norm_eps = 1e-05

LANES = 128
SLOTS = 8
f32 = jnp.float32
bf16 = jnp.bfloat16


def mm(a, b):
    return lax.dot_general(a, b, (((1,), (0,)), ((), ())), preferred_element_type=f32)


class Plan:
    def __init__(self, channels, height, width, depth):
        self.channels, self.height, self.width, self.depth = channels, height, width, depth
        self.cols = width // 2
        self.halves = LANES // self.cols
        self.rows = height // self.halves
        self.pairs = self.rows // 4
        self.span = self.pairs * SLOTS
        self.lanes = self.pairs * LANES
        self.taps = 9 * channels
        self.taps_pad = -(-self.taps // 32) * 32
        self.used = 4 * channels * SLOTS
        self.deep = -(-self.used // LANES) * LANES
        self.groups = 8
        self.pixels = height * width

    def pick_rows(self):
        out = np.zeros((self.halves, self.pairs, SLOTS, self.height), np.float32)
        for half in range(self.halves):
            for pair in range(self.pairs):
                for slot in range(6):
                    row = half * self.rows + 4 * pair + slot - 1
                    if 0 <= row < self.height:
                        out[half, pair, slot, row] = 1.0
        return out.reshape(self.halves * self.span, self.height)

    def pick_cols(self):
        out = np.zeros((self.halves, self.width, 4, self.halves, self.cols), np.float32)
        for shift in range(4):
            for col in range(self.cols):
                src = 2 * col + shift - 1
                if 0 <= src < self.width:
                    for half in range(self.halves):
                        out[half, src, shift, half, col] = 1.0
        return out.reshape(self.halves * self.width, 4 * LANES)

    def pick_taps(self):
        out = np.zeros((2, 2, 2, self.deep, self.taps_pad), np.float32)
        for odd in range(2):
            for a in range(2):
                for b in range(2):
                    for i in range(3):
                        for j in range(3):
                            for c in range(self.channels):
                                k = ((b + j) * self.channels + c) * SLOTS + 2 * odd + a + i
                                out[odd, a, b, k, (i * 3 + j) * self.channels + c] = 1.0
        return out.reshape(self.groups * self.deep, self.taps_pad)


def spread(row):
    return jnp.broadcast_to(row, (LANES, row.shape[1])).T


def split_two(x):
    high = x.astype(bf16)
    return high, (x - high.astype(f32)).astype(bf16)


class Prepare:
    def __init__(self, plan, planes, prow, pcol, wl3_ref, sums_ref, chan_ref):
        self.plan, self.planes, self.prow, self.pcol = plan, planes, prow, pcol
        self.wl3_ref, self.sums_ref, self.chan_ref = wl3_ref, sums_ref, chan_ref

    def stages(self, cols_ref):
        plan = self.plan
        D, KU, KP, C = plan.depth, plan.used, plan.deep, plan.channels
        shifts = []
        for plane in self.planes:
            rows = plane.astype(f32)
            total = functools.reduce(lambda a, b: a + b, [rows[r : r + 8] for r in range(0, plan.height, 8)])
            total = jnp.sum(jnp.sum(total, axis=1, keepdims=True), axis=0, keepdims=True)
            shifts.append(jnp.round(total * (4.0 / plan.pixels)) * 0.25)
        picked = mm(self.prow, jnp.concatenate(self.planes, axis=1)).astype(bf16)
        yield
        blocks = []
        for c in range(C):
            blocks.append(
                jnp.concatenate(
                    [
                        picked[h * plan.span : (h + 1) * plan.span, c * plan.width : (c + 1) * plan.width]
                        for h in range(plan.halves)
                    ],
                    axis=1,
                )
            )
        moved = mm(jnp.concatenate(blocks, axis=0), self.pcol)
        yield
        tail = jnp.ones((KP - KU, LANES), bf16)
        gram = None
        for half in range(2):
            lean = []
            for pair in range(half * plan.pairs // 2, (half + 1) * plan.pairs // 2):
                parts = [
                    (c, moved[c * plan.span + pair * SLOTS : c * plan.span + (pair + 1) * SLOTS, s * LANES : (s + 1) * LANES])
                    for s in range(4)
                    for c in range(C)
                ]
                cols_ref[0:KU, pair * LANES : (pair + 1) * LANES] = jnp.concatenate([x for _, x in parts], axis=0).astype(bf16)
                own = jnp.concatenate([x - shifts[c] for c, x in parts], axis=0).astype(bf16)
                lean.append(jnp.concatenate([own, tail], axis=0))
            yield
            lean = jnp.concatenate(lean, axis=1)
            part = GRAM(lean)
            gram = part if gram is None else gram + part
            yield
        high = gram.astype(bf16)
        rest = gram - high.astype(f32)
        mid = rest.astype(bf16)
        low = (rest - mid.astype(f32)).astype(bf16)
        quad = mm(self.wl3_ref[...], jnp.concatenate([high, mid, low], axis=0))
        yield
        blocks = D // 16
        second = []
        for blk in range(blocks):
            rows = [slice(((odd * blocks + blk) * 4 + p) * 16, ((odd * blocks + blk) * 4 + p + 1) * 16) for odd in range(2) for p in range(4)]
            second.append(functools.reduce(lambda a, b: a + b, [quad[r] * self.wl3_ref[r, 0:KP].astype(f32) for r in rows]))
        second = jnp.sum(jnp.concatenate(second, axis=0), axis=1, keepdims=True) * (1.0 / plan.pixels)
        off = jnp.sum(self.sums_ref[...] * gram[KU : KU + 1, :], axis=1, keepdims=True) * (1.0 / plan.pixels)
        second = jnp.broadcast_to(second, (D, LANES))
        off = jnp.broadcast_to(off, (D, LANES))
        mean = off
        for c in range(C):
            mean = mean + shifts[c] * self.chan_ref[2 + c]
        var = jnp.maximum(second - off * off, 0.0) + norm_eps
        self.factor = lax.rsqrt(var)
        self.scale = self.chan_ref[0] * self.factor
        self.mean = mean
        self.thr = mean - self.chan_ref[1] * (var * self.factor)
        yield


def GRAM(lean):
    return lax.dot_general(lean, lean, (((1,), (1,)), ((), ())), preferred_element_type=f32)


def is_chosen(order_ref, batch, gid):
    return lax.fori_loop(0, batch, lambda j, t: t | (order_ref[0, j] == gid).astype(jnp.int32), jnp.int32(0))


def make_weights(plan, param_ref, ptap_ref, wl_ref, wl3_ref, sums_ref, chan_ref):
    D, KP, C = plan.depth, plan.deep, plan.channels
    spread_taps = mm(ptap_ref[...], param_ref[0 : plan.taps_pad, :])
    sums = None
    for g in range(plan.groups):
        odd, phase = divmod(g, 4)
        turned = spread_taps[g * KP : (g + 1) * KP, :].T
        sums = turned if sums is None else sums + turned
        turned = turned.astype(bf16)
        for blk in range(D // 16):
            at = ((odd * (D // 16) + blk) * 4 + phase) * 16
            rows = turned[blk * 16 : (blk + 1) * 16, :]
            wl_ref[at : at + 16, :] = rows
            for n in range(3):
                wl3_ref[at : at + 16, n * KP : (n + 1) * KP] = rows
    sums_ref[...] = sums
    gain = param_ref[plan.taps_pad : plan.taps_pad + 1, :].astype(f32)
    bias = param_ref[plan.taps_pad + 1 : plan.taps_pad + 2, :].astype(f32)
    chan_ref[0] = spread(gain)
    chan_ref[1] = spread(bias / gain)
    first = spread_taps[0:KP, :]
    for c in range(C):
        total = functools.reduce(lambda a, b: a + b, [first[(s * C + c) * SLOTS : (s * C + c + 1) * SLOTS] for s in range(4)])
        chan_ref[2 + c] = spread(jnp.sum(total, axis=0, keepdims=True))


def forward_kernel(
    plan, n_own, batch, where_ref, pick_ref, count_ref, order_ref,
    pool_ref, syn_ref, prow_ref, pcol_ref, ptap_ref, param_ref,
    part_ref, wl_ref,
    all_ref, wl3_ref, sums_ref, chan_ref, now_ref, next_ref, thr_ref, coef_ref,
):
    D, KP, KU, C = plan.depth, plan.deep, plan.used, plan.channels
    pos = where_ref[0]
    n_pool = pool_ref.shape[0]
    own_count = count_ref[0, pos]
    total = lax.fori_loop(0, count_ref.shape[1], lambda i, t: t + count_ref[0, i], jnp.int32(0)).astype(f32)
    flags = [is_chosen(order_ref, batch, pos * n_own + i) for i in range(n_own)]
    n_syn = functools.reduce(lambda a, b: a + b, flags)

    make_weights(plan, param_ref, ptap_ref, wl_ref, wl3_ref, sums_ref, chan_ref)
    for i in range(n_own):
        all_ref[n_pool + i] = syn_ref[i].astype(bf16)
    all_ref[0:n_pool] = pool_ref[...]
    part_ref[...] = jnp.zeros_like(part_ref)
    if KP > KU:
        now_ref[KU:KP, :] = jnp.zeros((KP - KU, plan.lanes), bf16)

    def image_of(i):
        syn_at = jnp.int32(n_pool + n_own - 1)
        before = n_syn
        for s in reversed(range(n_own)):
            before = before - flags[s]
            syn_at = jnp.where((flags[s] > 0) & (i == before), n_pool + s, syn_at)
        real_at = pick_ref[0, 0, jnp.clip(i - n_syn, 0, n_pool - 1)]
        return jnp.where(i < n_syn, syn_at, real_at), jnp.where(i < n_syn, 0.25 / batch, -0.25 / total)

    def begin(i):
        at, weight = image_of(i)
        planes = [all_ref[at, c] for c in range(C)]
        return Prepare(plan, planes, prow_ref[...], pcol_ref[...], wl3_ref, sums_ref, chan_ref), weight

    prep, weight = begin(jnp.int32(0))
    for _ in prep.stages(now_ref):
        pass
    thr_ref[...] = prep.thr
    coef_ref[...] = prep.scale * weight
    tile = 2 * LANES

    def step(i, base):
        prep, weight = begin(i + 1)
        ahead = prep.stages(next_ref)
        base = base + coef_ref[...] * thr_ref[...]
        for t in range(plan.lanes // tile):
            at = t * tile
            y = mm(wl_ref[...], now_ref[:, at : at + tile])
            next(ahead, None)
            for odd in range(2):
                for blk in range(D // 16):
                    r0 = (odd * (D // 16) + blk) * 64
                    thr = thr_ref[blk * 16 : (blk + 1) * 16, :]
                    coef = coef_ref[blk * 16 : (blk + 1) * 16, :]
                    out = slice(odd * D + blk * 16, odd * D + (blk + 1) * 16)
                    for half in range(2):
                        lanes = slice(half * LANES, (half + 1) * LANES)
                        ys = [jnp.maximum(y[r0 + p * 16 : r0 + (p + 1) * 16, lanes], thr) for p in range(4)]
                        here = slice(at + half * LANES, at + (half + 1) * LANES)
                        part_ref[out, here] += coef * ((ys[0] + ys[1]) + (ys[2] + ys[3]))
        for _ in ahead:
            pass
        now_ref[0:KU, :] = next_ref[0:KU, :]
        thr_ref[...] = prep.thr
        coef_ref[...] = prep.scale * weight
        return base

    base = lax.fori_loop(0, n_syn + own_count, step, jnp.zeros((D, LANES), f32))
    base = 4.0 * base
    for pair in range(plan.pairs):
        for odd in range(2):
            part_ref[odd * D : (odd + 1) * D, pair * LANES : (pair + 1) * LANES] -= base


def middle_kernel(
    plan, n_own, batch, own, where_ref, order_ref, syn_ref, prow_ref, pcol_ref, ptap_ref, param_ref,
    cols_ref, vsum_ref, hits_ref, stat_ref,
    wl_ref, wl3_ref, sums_ref, chan_ref,
):
    D, KP, KU, C = plan.depth, plan.deep, plan.used, plan.channels
    flag = is_chosen(order_ref, batch, where_ref[0] * n_own + own)
    tile = 2 * LANES

    @pl.when(flag > 0)
    def _():
        make_weights(plan, param_ref, ptap_ref, wl_ref, wl3_ref, sums_ref, chan_ref)
        if KP > KU:
            cols_ref[KU:KP, :] = jnp.zeros((KP - KU, plan.lanes), bf16)
        planes = [syn_ref[own, c].astype(bf16) for c in range(C)]
        prep = Prepare(plan, planes, prow_ref[...], pcol_ref[...], wl3_ref, sums_ref, chan_ref)
        for _ in prep.stages(cols_ref):
            pass
        for n, value in enumerate((prep.mean, prep.factor, prep.scale, prep.thr, chan_ref[0], chan_ref[1])):
            stat_ref[n] = value

        for t in range(plan.lanes // tile):
            at = t * tile
            y = mm(wl_ref[...], cols_ref[:, at : at + tile])
            for odd in range(2):
                for blk in range(D // 16):
                    r0 = (odd * (D // 16) + blk) * 64
                    thr = stat_ref[3, blk * 16 : (blk + 1) * 16, :]
                    out = slice(odd * D + blk * 16, odd * D + (blk + 1) * 16)
                    for half in range(2):
                        lanes = slice(half * LANES, (half + 1) * LANES)
                        yp = [y[r0 + p * 16 : r0 + (p + 1) * 16, lanes] for p in range(4)]
                        ys = [jnp.maximum(a, thr) for a in yp]
                        hs = [jnp.where(a > thr, 1.0, 0.0) for a in yp]
                        here = slice(at + half * LANES, at + (half + 1) * LANES)
                        vsum_ref[out, here] = (((ys[0] + ys[1]) + (ys[2] + ys[3])) - 4.0 * thr).astype(bf16)
                        hits_ref[out, here] = ((hs[0] + hs[1]) + (hs[2] + hs[3])).astype(bf16)


def backward_kernel(
    plan, n_own, batch, where_ref, order_ref, *refs,
):
    D, KU, blocks = plan.depth, plan.used, plan.depth // 16
    gap_ref = refs[0]
    owns = [refs[1 + 4 * i : 5 + 4 * i] for i in range(n_own)]
    (
        wl_ref, prow_ref, pcol_ref, syn_ref, first_ref, second_ref,
        new_syn_ref, new_first_ref, new_second_ref,
        grad_ref, dcols_ref, col_ref, wlt_ref,
    ) = refs[1 + 4 * n_own :]
    pos = where_ref[0]
    tile = 2 * LANES
    grad_factor = 2.0 * loss_scale / batch
    for g in range(plan.groups):
        wlt_ref[:, g * D : (g + 1) * D] = wl_ref[g * D : (g + 1) * D, :].astype(f32).T.astype(bf16)[0:KU, :]

    for i in range(n_own):
        cols_ref, vsum_ref, hits_ref, stat_ref = owns[i]
        flag = is_chosen(order_ref, batch, pos * n_own + i)

        @pl.when(flag == 0)
        def _():
            grad_ref[...] = jnp.zeros_like(grad_ref)

        @pl.when(flag > 0)
        def _():
            unit = grad_factor / (4.0 * plan.pixels)
            for blk in range(blocks):
                chan = slice(blk * 16, (blk + 1) * 16)
                one = two = jnp.zeros((16, LANES), f32)
                for pair in range(plan.pairs):
                    here = slice(pair * LANES, (pair + 1) * LANES)
                    for odd in range(2):
                        rows = slice(odd * D + blk * 16, odd * D + (blk + 1) * 16)
                        gap = gap_ref[rows, here]
                        one = one + gap * hits_ref[rows, here].astype(f32)
                        two = two + gap * vsum_ref[rows, here].astype(f32)
                one = jnp.broadcast_to(jnp.sum(one, axis=1, keepdims=True), (16, LANES)) * unit
                two = jnp.broadcast_to(jnp.sum(two, axis=1, keepdims=True), (16, LANES)) * unit
                mean, factor, scale, thr, gain, ratio = [stat_ref[n, chan, :] for n in range(6)]
                slope = factor * factor * (scale * two - one * (ratio * gain))
                col_ref[0, chan, :] = factor * gain * (0.25 * grad_factor)
                col_ref[1, chan, :] = slope
                col_ref[2, chan, :] = slope * mean - factor * (gain * one)

            for t in range(plan.lanes // tile):
                at = t * tile
                y = mm(wl_ref[...], cols_ref[:, at : at + tile])
                inner = []
                for odd in range(2):
                    for blk in range(blocks):
                        r0 = (odd * blocks + blk) * 64
                        chan = slice(blk * 16, (blk + 1) * 16)
                        thr_b, up_b, slope_b, off = stat_ref[3, chan, :], col_ref[0, chan, :], col_ref[1, chan, :], col_ref[2, chan, :]
                        ons = []
                        for half in range(2):
                            gap = gap_ref[odd * D + blk * 16 : odd * D + (blk + 1) * 16, at + half * LANES : at + (half + 1) * LANES]
                            ons.append(up_b * gap + off)
                        for p in range(4):
                            both = []
                            for half in range(2):
                                yp = y[r0 + p * 16 : r0 + (p + 1) * 16, half * LANES : (half + 1) * LANES]
                                both.append((jnp.where(yp > thr_b, ons[half], off) - slope_b * yp).astype(bf16))
                            inner.append(jnp.concatenate(both, axis=1))
                dcols_ref[:, at : at + tile] = mm(wlt_ref[...], jnp.concatenate(inner, axis=0))

            shifts = []
            for s in range(4):
                shifts.append(
                    jnp.concatenate(
                        [
                            dcols_ref[
                                (s * plan.channels + c) * SLOTS : (s * plan.channels + c + 1) * SLOTS,
                                pair * LANES : (pair + 1) * LANES,
                            ]
                            for c in range(plan.channels)
                            for pair in range(plan.pairs)
                        ],
                        axis=0,
                    )
                )
            high, low = split_two(jnp.concatenate(shifts, axis=1))
            back = (((1,), (1,)), ((), ()))
            pcol = pcol_ref[...]
            wide = lax.dot_general(high, pcol, back, preferred_element_type=f32) + lax.dot_general(
                low, pcol, back, preferred_element_type=f32
            )
            tall = jnp.concatenate(
                [
                    jnp.concatenate(
                        [
                            wide[c * plan.span : (c + 1) * plan.span, half * plan.width : (half + 1) * plan.width]
                            for c in range(plan.channels)
                        ],
                        axis=1,
                    )
                    for half in range(plan.halves)
                ],
                axis=0,
            )
            high, low = split_two(tall)
            prow = prow_ref[...].T
            image = mm(prow, high) + mm(prow, low)
            for c in range(plan.channels):
                grad_ref[c] = image[:, c * plan.width : (c + 1) * plan.width]

        for c in range(plan.channels):
            grad = grad_ref[c]
            first_new = beta_one * first_ref[i, c] + (1.0 - beta_one) * grad
            second_new = beta_two * second_ref[i, c] + (1.0 - beta_two) * grad * grad
            corrected = first_new / (1.0 - beta_one**adam_step)
            scale_hat = jnp.sqrt(second_new / (1.0 - beta_two**adam_step))
            new_syn_ref[i, c] = syn_ref[i, c] - learn_rate * corrected / (scale_hat + adam_eps)
            new_first_ref[i, c] = first_new
            new_second_ref[i, c] = second_new


def gather_params(conv_weight, norm_gain, norm_bias, taps_pad):
    taps, width = conv_weight.shape
    own = jnp.concatenate(
        [
            conv_weight,
            jnp.zeros((taps_pad - taps, width), conv_weight.dtype),
            norm_gain[None],
            norm_bias[None],
            jnp.zeros((14, width), conv_weight.dtype),
        ],
        axis=0,
    )
    if lax.axis_size("cls") == 2:
        other = lax.ppermute(own, "cls", [(0, 1), (1, 0)])
        low = lax.axis_index("cls") == 0
        return jnp.concatenate([jnp.where(low, own, other), jnp.where(low, other, own)], axis=1)
    return lax.all_gather(own, "cls", axis=1, tiled=True)


class Exchange:
    def __init__(self):
        self.n = lax.axis_size("wide")
        self.pos = lax.axis_index("wide")
        steps = []
        while 1 << (len(steps) + 1) <= self.n:
            steps.append(1 << len(steps))
        self.first, rest = steps[0], steps[1:]
        self.masks = [(self.first, self.first)] + list(zip(rest, rest[1:] + rest[:1]))

    def swap(self, x, masks):
        return lax.ppermute(x, "wide", [(i, i ^ masks[i & self.first]) for i in range(self.n)])

    def high(self, masks):
        return (self.pos & jnp.where((self.pos & self.first) > 0, masks[1], masks[0])) > 0

    def add(self, own, masks):
        high = self.high(masks)
        rows = own.shape[0] // 2
        kept = jnp.where(high, own[rows:], own[:rows])
        sent = jnp.where(high, own[:rows], own[rows:]).astype(jnp.float16)
        return kept, sent

    def join(self, own, other, masks):
        high = self.high(masks)
        return jnp.concatenate([jnp.where(high, other, own), jnp.where(high, own, other)], axis=0)


def exchange_sum(part, where, middle, n_own):
    ex = Exchange()
    rounds = [(masks, True) for masks in ex.masks] + [(masks, False) for masks in reversed(ex.masks)]
    at_round = [1 + (len(rounds) - 3) * i // max(n_own - 1, 1) for i in range(n_own)]
    own, made = part, []
    for n, (masks, adding) in enumerate(rounds):
        if adding:
            kept, sent = ex.add(own, masks)
        else:
            sent = own.astype(jnp.float16)
        todo = [i for i in range(n_own) if at_round[i] == n]
        if todo:
            sent, held = lax.optimization_barrier((sent, where))
        got = ex.swap(sent, masks)
        if todo:
            new = [middle(i, held) for i in todo]
            if n + 1 < len(rounds):
                got, new = lax.optimization_barrier((got, new))
            made += new
        own = kept + got.astype(f32) if adding else ex.join(sent, got, masks)
    return own.astype(f32), made


def body(
    syn_images, adam_first, adam_second, real_pool, real_pick, real_count, syn_order,
    conv_weight, norm_gain, norm_bias,
):
    _, n_own, channels, height, width = syn_images.shape
    batch = syn_order.shape[1] // 2
    depth = conv_weight.shape[1] * lax.axis_size("cls")
    plan = Plan(channels, height, width, depth)
    prow = jnp.asarray(plan.pick_rows(), bf16)
    pcol = jnp.asarray(plan.pick_cols(), bf16)
    ptap = jnp.asarray(plan.pick_taps(), bf16)
    params = gather_params(conv_weight, norm_gain, norm_bias, plan.taps_pad)
    where = lax.axis_index("wide").astype(jnp.int32)[None]

    smem = pl.BlockSpec(memory_space=pltpu.SMEM)
    vmem = pl.BlockSpec(memory_space=pltpu.VMEM)
    shape = jax.ShapeDtypeStruct
    rows = 2 * depth
    m_rows = plan.groups * depth
    weights = [
        pltpu.VMEM((m_rows, 3 * plan.deep), bf16),
        pltpu.VMEM((depth, plan.deep), f32),
        pltpu.VMEM((2 + channels, depth, LANES), f32),
    ]

    def within(mib):
        return pltpu.CompilerParams(vmem_limit_bytes=mib << 20)

    part, wl = pl.pallas_call(
        functools.partial(forward_kernel, plan, n_own, batch),
        in_specs=[smem] * 4 + [vmem] * 6,
        out_specs=[vmem] * 2,
        out_shape=[shape((rows, plan.lanes), f32), shape((m_rows, plan.deep), bf16)],
        scratch_shapes=[
            pltpu.VMEM((real_pool.shape[1] + n_own, channels, height, width), bf16),
            *weights,
            pltpu.VMEM((plan.deep, plan.lanes), bf16),
            pltpu.VMEM((plan.used, plan.lanes), bf16),
            *[pltpu.VMEM((depth, LANES), f32)] * 2,
        ],
        compiler_params=within(20),
        name="embed_sums",
    )(where, real_pick, real_count, syn_order, real_pool[0], syn_images[0], prow, pcol, ptap, params)

    def middle(own, held):
        return pl.pallas_call(
            functools.partial(middle_kernel, plan, n_own, batch, own),
            in_specs=[smem] * 2 + [vmem] * 5,
            out_specs=[vmem] * 4,
            out_shape=[
                shape((plan.deep, plan.lanes), bf16),
                shape((rows, plan.lanes), bf16),
                shape((rows, plan.lanes), bf16),
                shape((6, depth, LANES), f32),
            ],
            scratch_shapes=[pltpu.VMEM((m_rows, plan.deep), bf16), *weights],
            compiler_params=within(20),
            name="syn_features",
        )(held, syn_order, syn_images[0], prow, pcol, ptap, params)

    gap, made = exchange_sum(part, where, middle, n_own)

    img = shape((n_own, channels, height, width), f32)
    outs = pl.pallas_call(
        functools.partial(backward_kernel, plan, n_own, batch),
        in_specs=[smem] * 2 + [vmem] * (7 + 4 * n_own),
        out_specs=[vmem] * 3,
        out_shape=[img] * 3,
        scratch_shapes=[
            pltpu.VMEM((channels, height, width), f32),
            pltpu.VMEM((plan.used, plan.lanes), f32),
            pltpu.VMEM((3, depth, LANES), f32),
            pltpu.VMEM((plan.used, m_rows), bf16),
        ],
        compiler_params=within(28),
        name="image_grads",
    )(
        where, syn_order, gap, *[x for one in made for x in one], wl, prow, pcol,
        syn_images[0], adam_first[0], adam_second[0],
    )
    return tuple(out[None] for out in outs)


def solution(mesh):
    image = P("cls", "wide", None, None, None)
    return jax.shard_map(
        body,
        mesh=mesh,
        in_specs=(
            image, image, image, image, P("cls", "wide", None), P("cls", None), P("cls", None),
            P(None, "cls"), P("cls"), P("cls"),
        ),
        out_specs=(image, image, image),
        check_vma=False,
    )
```

```python
import functools

import jax
import jax.numpy as jnp
import numpy as np
from jax import lax
from jax.experimental import pallas as pl
from jax.experimental.pallas import tpu as pltpu
from jax.sharding import PartitionSpec as P

beta_one = 0.9
beta_two = 0.99
adam_step = 10.0
learn_rate = 0.1
adam_eps = 1e-08
loss_scale = 512.0
norm_eps = 1e-05

LANES = 128
SLOTS = 8
f32 = jnp.float32
bf16 = jnp.bfloat16


def mm(a, b):
    return lax.dot_general(a, b, (((1,), (0,)), ((), ())), preferred_element_type=f32)


class Plan:
    def __init__(self, channels, height, width, depth):
        self.channels, self.height, self.width, self.depth = channels, height, width, depth
        self.cols = width // 2
        self.halves = LANES // self.cols
        self.rows = height // self.halves
        self.pairs = self.rows // 4
        self.span = self.pairs * SLOTS
        self.lanes = self.pairs * LANES
        self.taps = 9 * channels
        self.taps_pad = -(-self.taps // 32) * 32
        self.used = 4 * channels * SLOTS
        self.deep = -(-self.used // LANES) * LANES
        self.groups = 8
        self.pixels = height * width

    def pick_rows(self):
        out = np.zeros((self.halves, self.pairs, SLOTS, self.height), np.float32)
        for half in range(self.halves):
            for pair in range(self.pairs):
                for slot in range(6):
                    row = half * self.rows + 4 * pair + slot - 1
                    if 0 <= row < self.height:
                        out[half, pair, slot, row] = 1.0
        return out.reshape(self.halves * self.span, self.height)

    def pick_cols(self):
        out = np.zeros((self.halves, self.width, 4, self.halves, self.cols), np.float32)
        for shift in range(4):
            for col in range(self.cols):
                src = 2 * col + shift - 1
                if 0 <= src < self.width:
                    for half in range(self.halves):
                        out[half, src, shift, half, col] = 1.0
        return out.reshape(self.halves * self.width, 4 * LANES)

    def pick_taps(self):
        out = np.zeros((2, 2, 2, self.deep, self.taps_pad), np.float32)
        for odd in range(2):
            for a in range(2):
                for b in range(2):
                    for i in range(3):
                        for j in range(3):
                            for c in range(self.channels):
                                k = ((b + j) * self.channels + c) * SLOTS + 2 * odd + a + i
                                out[odd, a, b, k, (i * 3 + j) * self.channels + c] = 1.0
        return out.reshape(self.groups * self.deep, self.taps_pad)


def spread(row):
    return jnp.broadcast_to(row, (LANES, row.shape[1])).T


def split_two(x):
    high = x.astype(bf16)
    return high, (x - high.astype(f32)).astype(bf16)


class Prepare:
    def __init__(self, plan, planes, prow, pcol, wl3_ref, sums_ref, chan_ref):
        self.plan, self.planes, self.prow, self.pcol = plan, planes, prow, pcol
        self.wl3_ref, self.sums_ref, self.chan_ref = wl3_ref, sums_ref, chan_ref

    def stages(self, cols_ref):
        plan = self.plan
        D, KU, KP, C = plan.depth, plan.used, plan.deep, plan.channels
        shifts = []
        for plane in self.planes:
            rows = plane.astype(f32)
            total = functools.reduce(lambda a, b: a + b, [rows[r : r + 8] for r in range(0, plan.height, 8)])
            total = jnp.sum(jnp.sum(total, axis=1, keepdims=True), axis=0, keepdims=True)
            shifts.append(jnp.round(total * (4.0 / plan.pixels)) * 0.25)
        picked = mm(self.prow, jnp.concatenate(self.planes, axis=1)).astype(bf16)
        yield
        blocks = []
        for c in range(C):
            blocks.append(
                jnp.concatenate(
                    [
                        picked[h * plan.span : (h + 1) * plan.span, c * plan.width : (c + 1) * plan.width]
                        for h in range(plan.halves)
                    ],
                    axis=1,
                )
            )
        moved = mm(jnp.concatenate(blocks, axis=0), self.pcol)
        yield
        tail = jnp.ones((KP - KU, LANES), bf16)
        gram = None
        for half in range(2):
            lean = []
            for pair in range(half * plan.pairs // 2, (half + 1) * plan.pairs // 2):
                parts = [
                    (c, moved[c * plan.span + pair * SLOTS : c * plan.span + (pair + 1) * SLOTS, s * LANES : (s + 1) * LANES])
                    for s in range(4)
                    for c in range(C)
                ]
                cols_ref[0:KU, pair * LANES : (pair + 1) * LANES] = jnp.concatenate([x for _, x in parts], axis=0).astype(bf16)
                own = jnp.concatenate([x - shifts[c] for c, x in parts], axis=0).astype(bf16)
                lean.append(jnp.concatenate([own, tail], axis=0))
            yield
            lean = jnp.concatenate(lean, axis=1)
            part = GRAM(lean)
            gram = part if gram is None else gram + part
            yield
        high = gram.astype(bf16)
        rest = gram - high.astype(f32)
        mid = rest.astype(bf16)
        low = (rest - mid.astype(f32)).astype(bf16)
        quad = mm(self.wl3_ref[...], jnp.concatenate([high, mid, low], axis=0))
        yield
        blocks = D // 16
        second = []
        for blk in range(blocks):
            rows = [slice(((odd * blocks + blk) * 4 + p) * 16, ((odd * blocks + blk) * 4 + p + 1) * 16) for odd in range(2) for p in range(4)]
            second.append(functools.reduce(lambda a, b: a + b, [quad[r] * self.wl3_ref[r, 0:KP].astype(f32) for r in rows]))
        second = jnp.sum(jnp.concatenate(second, axis=0), axis=1, keepdims=True) * (1.0 / plan.pixels)
        off = jnp.sum(self.sums_ref[...] * gram[KU : KU + 1, :], axis=1, keepdims=True) * (1.0 / plan.pixels)
        second = jnp.broadcast_to(second, (D, LANES))
        off = jnp.broadcast_to(off, (D, LANES))
        mean = off
        for c in range(C):
            mean = mean + shifts[c] * self.chan_ref[2 + c]
        var = jnp.maximum(second - off * off, 0.0) + norm_eps
        self.factor = lax.rsqrt(var)
        self.scale = self.chan_ref[0] * self.factor
        self.mean = mean
        self.thr = mean - self.chan_ref[1] * (var * self.factor)
        yield


def GRAM(lean):
    return lax.dot_general(lean, lean, (((1,), (1,)), ((), ())), preferred_element_type=f32)


def is_chosen(order_ref, batch, gid):
    return lax.fori_loop(0, batch, lambda j, t: t | (order_ref[0, j] == gid).astype(jnp.int32), jnp.int32(0))


def make_weights(plan, param_ref, ptap_ref, wl_ref, wl3_ref, sums_ref, chan_ref):
    D, KP, C = plan.depth, plan.deep, plan.channels
    spread_taps = mm(ptap_ref[...], param_ref[0 : plan.taps_pad, :])
    sums = None
    for g in range(plan.groups):
        odd, phase = divmod(g, 4)
        turned = spread_taps[g * KP : (g + 1) * KP, :].T
        sums = turned if sums is None else sums + turned
        turned = turned.astype(bf16)
        for blk in range(D // 16):
            at = ((odd * (D // 16) + blk) * 4 + phase) * 16
            rows = turned[blk * 16 : (blk + 1) * 16, :]
            wl_ref[at : at + 16, :] = rows
            for n in range(3):
                wl3_ref[at : at + 16, n * KP : (n + 1) * KP] = rows
    sums_ref[...] = sums
    gain = param_ref[plan.taps_pad : plan.taps_pad + 1, :].astype(f32)
    bias = param_ref[plan.taps_pad + 1 : plan.taps_pad + 2, :].astype(f32)
    chan_ref[0] = spread(gain)
    chan_ref[1] = spread(bias / gain)
    first = spread_taps[0:KP, :]
    for c in range(C):
        total = functools.reduce(lambda a, b: a + b, [first[(s * C + c) * SLOTS : (s * C + c + 1) * SLOTS] for s in range(4)])
        chan_ref[2 + c] = spread(jnp.sum(total, axis=0, keepdims=True))


def forward_kernel(
    plan, n_own, batch, where_ref, pick_ref, count_ref, order_ref,
    pool_ref, syn_ref, prow_ref, pcol_ref, ptap_ref, param_ref,
    part_ref, wl_ref,
    all_ref, wl3_ref, sums_ref, chan_ref, now_ref, next_ref, thr_ref, coef_ref,
):
    D, KP, KU, C = plan.depth, plan.deep, plan.used, plan.channels
    pos = where_ref[0]
    n_pool = pool_ref.shape[0]
    own_count = count_ref[0, pos]
    total = lax.fori_loop(0, count_ref.shape[1], lambda i, t: t + count_ref[0, i], jnp.int32(0)).astype(f32)
    flags = [is_chosen(order_ref, batch, pos * n_own + i) for i in range(n_own)]
    n_syn = functools.reduce(lambda a, b: a + b, flags)

    make_weights(plan, param_ref, ptap_ref, wl_ref, wl3_ref, sums_ref, chan_ref)
    for i in range(n_own):
        all_ref[n_pool + i] = syn_ref[i].astype(bf16)
    all_ref[0:n_pool] = pool_ref[...]
    part_ref[...] = jnp.zeros_like(part_ref)
    if KP > KU:
        now_ref[KU:KP, :] = jnp.zeros((KP - KU, plan.lanes), bf16)

    def image_of(i):
        syn_at = jnp.int32(n_pool + n_own - 1)
        before = n_syn
        for s in reversed(range(n_own)):
            before = before - flags[s]
            syn_at = jnp.where((flags[s] > 0) & (i == before), n_pool + s, syn_at)
        real_at = pick_ref[0, 0, jnp.clip(i - n_syn, 0, n_pool - 1)]
        return jnp.where(i < n_syn, syn_at, real_at), jnp.where(i < n_syn, 0.25 / batch, -0.25 / total)

    def begin(i):
        at, weight = image_of(i)
        planes = [all_ref[at, c] for c in range(C)]
        return Prepare(plan, planes, prow_ref[...], pcol_ref[...], wl3_ref, sums_ref, chan_ref), weight

    prep, weight = begin(jnp.int32(0))
    for _ in prep.stages(now_ref):
        pass
    thr_ref[...] = prep.thr
    coef_ref[...] = prep.scale * weight
    tile = 2 * LANES

    def step(i, base):
        prep, weight = begin(i + 1)
        ahead = prep.stages(next_ref)
        base = base + coef_ref[...] * thr_ref[...]
        for t in range(plan.lanes // tile):
            at = t * tile
            y = mm(wl_ref[...], now_ref[:, at : at + tile])
            next(ahead, None)
            for odd in range(2):
                for blk in range(D // 16):
                    r0 = (odd * (D // 16) + blk) * 64
                    thr = thr_ref[blk * 16 : (blk + 1) * 16, :]
                    coef = coef_ref[blk * 16 : (blk + 1) * 16, :]
                    out = slice(odd * D + blk * 16, odd * D + (blk + 1) * 16)
                    for half in range(2):
                        lanes = slice(half * LANES, (half + 1) * LANES)
                        ys = [jnp.maximum(y[r0 + p * 16 : r0 + (p + 1) * 16, lanes], thr) for p in range(4)]
                        here = slice(at + half * LANES, at + (half + 1) * LANES)
                        part_ref[out, here] += coef * ((ys[0] + ys[1]) + (ys[2] + ys[3]))
        for _ in ahead:
            pass
        now_ref[0:KU, :] = next_ref[0:KU, :]
        thr_ref[...] = prep.thr
        coef_ref[...] = prep.scale * weight
        return base

    base = lax.fori_loop(0, n_syn + own_count, step, jnp.zeros((D, LANES), f32))
    base = 4.0 * base
    for pair in range(plan.pairs):
        for odd in range(2):
            part_ref[odd * D : (odd + 1) * D, pair * LANES : (pair + 1) * LANES] -= base


def middle_kernel(
    plan, n_own, batch, own, where_ref, order_ref, syn_ref, prow_ref, pcol_ref, ptap_ref, param_ref,
    cols_ref, vsum_ref, hits_ref, stat_ref,
    wl_ref, wl3_ref, sums_ref, chan_ref,
):
    D, KP, KU, C = plan.depth, plan.deep, plan.used, plan.channels
    flag = is_chosen(order_ref, batch, where_ref[0] * n_own + own)
    tile = 2 * LANES

    @pl.when(flag > 0)
    def _():
        make_weights(plan, param_ref, ptap_ref, wl_ref, wl3_ref, sums_ref, chan_ref)
        if KP > KU:
            cols_ref[KU:KP, :] = jnp.zeros((KP - KU, plan.lanes), bf16)
        planes = [syn_ref[own, c].astype(bf16) for c in range(C)]
        prep = Prepare(plan, planes, prow_ref[...], pcol_ref[...], wl3_ref, sums_ref, chan_ref)
        for _ in prep.stages(cols_ref):
            pass
        for n, value in enumerate((prep.mean, prep.factor, prep.scale, prep.thr, chan_ref[0], chan_ref[1])):
            stat_ref[n] = value

        for t in range(plan.lanes // tile):
            at = t * tile
            y = mm(wl_ref[...], cols_ref[:, at : at + tile])
            for odd in range(2):
                for blk in range(D // 16):
                    r0 = (odd * (D // 16) + blk) * 64
                    thr = stat_ref[3, blk * 16 : (blk + 1) * 16, :]
                    out = slice(odd * D + blk * 16, odd * D + (blk + 1) * 16)
                    for half in range(2):
                        lanes = slice(half * LANES, (half + 1) * LANES)
                        yp = [y[r0 + p * 16 : r0 + (p + 1) * 16, lanes] for p in range(4)]
                        ys = [jnp.maximum(a, thr) for a in yp]
                        hs = [jnp.where(a > thr, 1.0, 0.0) for a in yp]
                        here = slice(at + half * LANES, at + (half + 1) * LANES)
                        vsum_ref[out, here] = (((ys[0] + ys[1]) + (ys[2] + ys[3])) - 4.0 * thr).astype(bf16)
                        hits_ref[out, here] = ((hs[0] + hs[1]) + (hs[2] + hs[3])).astype(bf16)


def backward_kernel(
    plan, n_own, batch, where_ref, order_ref, *refs,
):
    D, KU, blocks = plan.depth, plan.used, plan.depth // 16
    gap_ref = refs[0]
    owns = [refs[1 + 4 * i : 5 + 4 * i] for i in range(n_own)]
    (
        wl_ref, prow_ref, pcol_ref, syn_ref, first_ref, second_ref,
        new_syn_ref, new_first_ref, new_second_ref,
        grad_ref, dcols_ref, col_ref, wlt_ref,
    ) = refs[1 + 4 * n_own :]
    pos = where_ref[0]
    tile = 2 * LANES
    grad_factor = 2.0 * loss_scale / batch
    for g in range(plan.groups):
        wlt_ref[:, g * D : (g + 1) * D] = wl_ref[g * D : (g + 1) * D, :].astype(f32).T.astype(bf16)[0:KU, :]

    for i in range(n_own):
        cols_ref, vsum_ref, hits_ref, stat_ref = owns[i]
        flag = is_chosen(order_ref, batch, pos * n_own + i)

        @pl.when(flag == 0)
        def _():
            grad_ref[...] = jnp.zeros_like(grad_ref)

        @pl.when(flag > 0)
        def _():
            unit = grad_factor / (4.0 * plan.pixels)
            for blk in range(blocks):
                chan = slice(blk * 16, (blk + 1) * 16)
                one = two = jnp.zeros((16, LANES), f32)
                for pair in range(plan.pairs):
                    here = slice(pair * LANES, (pair + 1) * LANES)
                    for odd in range(2):
                        rows = slice(odd * D + blk * 16, odd * D + (blk + 1) * 16)
                        gap = gap_ref[rows, here]
                        one = one + gap * hits_ref[rows, here].astype(f32)
                        two = two + gap * vsum_ref[rows, here].astype(f32)
                one = jnp.broadcast_to(jnp.sum(one, axis=1, keepdims=True), (16, LANES)) * unit
                two = jnp.broadcast_to(jnp.sum(two, axis=1, keepdims=True), (16, LANES)) * unit
                mean, factor, scale, thr, gain, ratio = [stat_ref[n, chan, :] for n in range(6)]
                slope = factor * factor * (scale * two - one * (ratio * gain))
                col_ref[0, chan, :] = factor * gain * (0.25 * grad_factor)
                col_ref[1, chan, :] = slope
                col_ref[2, chan, :] = slope * mean - factor * (gain * one)

            for t in range(plan.lanes // tile):
                at = t * tile
                y = mm(wl_ref[...], cols_ref[:, at : at + tile])
                inner = []
                for odd in range(2):
                    for blk in range(blocks):
                        r0 = (odd * blocks + blk) * 64
                        chan = slice(blk * 16, (blk + 1) * 16)
                        thr_b, up_b, slope_b, off = stat_ref[3, chan, :], col_ref[0, chan, :], col_ref[1, chan, :], col_ref[2, chan, :]
                        ons = []
                        for half in range(2):
                            gap = gap_ref[odd * D + blk * 16 : odd * D + (blk + 1) * 16, at + half * LANES : at + (half + 1) * LANES]
                            ons.append(up_b * gap + off)
                        for p in range(4):
                            both = []
                            for half in range(2):
                                yp = y[r0 + p * 16 : r0 + (p + 1) * 16, half * LANES : (half + 1) * LANES]
                                both.append((jnp.where(yp > thr_b, ons[half], off) - slope_b * yp).astype(bf16))
                            inner.append(jnp.concatenate(both, axis=1))
                dcols_ref[:, at : at + tile] = mm(wlt_ref[...], jnp.concatenate(inner, axis=0))

            shifts = []
            for s in range(4):
                shifts.append(
                    jnp.concatenate(
                        [
                            dcols_ref[
                                (s * plan.channels + c) * SLOTS : (s * plan.channels + c + 1) * SLOTS,
                                pair * LANES : (pair + 1) * LANES,
                            ]
                            for c in range(plan.channels)
                            for pair in range(plan.pairs)
                        ],
                        axis=0,
                    )
                )
            high, low = split_two(jnp.concatenate(shifts, axis=1))
            back = (((1,), (1,)), ((), ()))
            pcol = pcol_ref[...]
            wide = lax.dot_general(high, pcol, back, preferred_element_type=f32) + lax.dot_general(
                low, pcol, back, preferred_element_type=f32
            )
            tall = jnp.concatenate(
                [
                    jnp.concatenate(
                        [
                            wide[c * plan.span : (c + 1) * plan.span, half * plan.width : (half + 1) * plan.width]
                            for c in range(plan.channels)
                        ],
                        axis=1,
                    )
                    for half in range(plan.halves)
                ],
                axis=0,
            )
            high, low = split_two(tall)
            prow = prow_ref[...].T
            image = mm(prow, high) + mm(prow, low)
            for c in range(plan.channels):
                grad_ref[c] = image[:, c * plan.width : (c + 1) * plan.width]

        for c in range(plan.channels):
            grad = grad_ref[c]
            first_new = beta_one * first_ref[i, c] + (1.0 - beta_one) * grad
            second_new = beta_two * second_ref[i, c] + (1.0 - beta_two) * grad * grad
            corrected = first_new / (1.0 - beta_one**adam_step)
            scale_hat = jnp.sqrt(second_new / (1.0 - beta_two**adam_step))
            new_syn_ref[i, c] = syn_ref[i, c] - learn_rate * corrected / (scale_hat + adam_eps)
            new_first_ref[i, c] = first_new
            new_second_ref[i, c] = second_new


def gather_params(conv_weight, norm_gain, norm_bias, taps_pad):
    taps, width = conv_weight.shape
    own = jnp.concatenate(
        [
            conv_weight,
            jnp.zeros((taps_pad - taps, width), conv_weight.dtype),
            norm_gain[None],
            norm_bias[None],
            jnp.zeros((14, width), conv_weight.dtype),
        ],
        axis=0,
    )
    if lax.axis_size("cls") == 2:
        other = lax.ppermute(own, "cls", [(0, 1), (1, 0)])
        low = lax.axis_index("cls") == 0
        return jnp.concatenate([jnp.where(low, own, other), jnp.where(low, other, own)], axis=1)
    return lax.all_gather(own, "cls", axis=1, tiled=True)


class Exchange:
    def __init__(self):
        self.n = lax.axis_size("wide")
        self.pos = lax.axis_index("wide")
        steps = []
        while 1 << (len(steps) + 1) <= self.n:
            steps.append(1 << len(steps))
        self.first, rest = steps[0], steps[1:]
        self.masks = [(self.first, self.first)] + list(zip(rest, rest[1:] + rest[:1]))

    def swap(self, x, masks):
        return lax.ppermute(x, "wide", [(i, i ^ masks[i & self.first]) for i in range(self.n)])

    def high(self, masks):
        return (self.pos & jnp.where((self.pos & self.first) > 0, masks[1], masks[0])) > 0

    def add(self, own, masks):
        high = self.high(masks)
        rows = own.shape[0] // 2
        kept = jnp.where(high, own[rows:], own[:rows])
        sent = jnp.where(high, own[:rows], own[rows:]).astype(jnp.float16)
        return kept, sent

    def join(self, own, other, masks):
        high = self.high(masks)
        return jnp.concatenate([jnp.where(high, other, own), jnp.where(high, own, other)], axis=0)


def exchange_sum(part, where, middle, n_own):
    ex = Exchange()
    halved = ex.masks[:2]
    whole = ex.masks[2:]
    rounds = [(m, "halve") for m in halved] + [(m, "whole") for m in whole] + [(m, "join") for m in reversed(halved)]
    at_round = [1 + (len(rounds) - 3) * i // max(n_own - 1, 1) for i in range(n_own)]
    own, made = part, []
    for n, (masks, kind) in enumerate(rounds):
        if kind == "halve":
            own, sent = ex.add(own, masks)
        else:
            sent = own.astype(jnp.float16)
        todo = [i for i in range(n_own) if at_round[i] == n]
        if todo:
            sent, held = lax.optimization_barrier((sent, where))
        got = ex.swap(sent, masks)
        if todo:
            new = [middle(i, held) for i in todo]
            if n + 1 < len(rounds):
                got, new = lax.optimization_barrier((got, new))
            made += new
        own = ex.join(sent, got, masks) if kind == "join" else own + got.astype(f32)
    return own.astype(f32), made


def body(
    syn_images, adam_first, adam_second, real_pool, real_pick, real_count, syn_order,
    conv_weight, norm_gain, norm_bias,
):
    _, n_own, channels, height, width = syn_images.shape
    batch = syn_order.shape[1] // 2
    depth = conv_weight.shape[1] * lax.axis_size("cls")
    plan = Plan(channels, height, width, depth)
    prow = jnp.asarray(plan.pick_rows(), bf16)
    pcol = jnp.asarray(plan.pick_cols(), bf16)
    ptap = jnp.asarray(plan.pick_taps(), bf16)
    params = gather_params(conv_weight, norm_gain, norm_bias, plan.taps_pad)
    where = lax.axis_index("wide").astype(jnp.int32)[None]

    smem = pl.BlockSpec(memory_space=pltpu.SMEM)
    vmem = pl.BlockSpec(memory_space=pltpu.VMEM)
    shape = jax.ShapeDtypeStruct
    rows = 2 * depth
    m_rows = plan.groups * depth
    weights = [
        pltpu.VMEM((m_rows, 3 * plan.deep), bf16),
        pltpu.VMEM((depth, plan.deep), f32),
        pltpu.VMEM((2 + channels, depth, LANES), f32),
    ]

    def within(mib):
        return pltpu.CompilerParams(vmem_limit_bytes=mib << 20)

    part, wl = pl.pallas_call(
        functools.partial(forward_kernel, plan, n_own, batch),
        in_specs=[smem] * 4 + [vmem] * 6,
        out_specs=[vmem] * 2,
        out_shape=[shape((rows, plan.lanes), f32), shape((m_rows, plan.deep), bf16)],
        scratch_shapes=[
            pltpu.VMEM((real_pool.shape[1] + n_own, channels, height, width), bf16),
            *weights,
            pltpu.VMEM((plan.deep, plan.lanes), bf16),
            pltpu.VMEM((plan.used, plan.lanes), bf16),
            *[pltpu.VMEM((depth, LANES), f32)] * 2,
        ],
        compiler_params=within(60),
        name="embed_sums",
    )(where, real_pick, real_count, syn_order, real_pool[0], syn_images[0], prow, pcol, ptap, params)

    def middle(own, held):
        return pl.pallas_call(
            functools.partial(middle_kernel, plan, n_own, batch, own),
            in_specs=[smem] * 2 + [vmem] * 5,
            out_specs=[vmem] * 4,
            out_shape=[
                shape((plan.deep, plan.lanes), bf16),
                shape((rows, plan.lanes), bf16),
                shape((rows, plan.lanes), bf16),
                shape((6, depth, LANES), f32),
            ],
            scratch_shapes=[pltpu.VMEM((m_rows, plan.deep), bf16), *weights],
            compiler_params=within(14),
            name="syn_features",
        )(held, syn_order, syn_images[0], prow, pcol, ptap, params)

    gap, made = exchange_sum(part, where, middle, n_own)

    img = shape((n_own, channels, height, width), f32)
    outs = pl.pallas_call(
        functools.partial(backward_kernel, plan, n_own, batch),
        in_specs=[smem] * 2 + [vmem] * (7 + 4 * n_own),
        out_specs=[vmem] * 3,
        out_shape=[img] * 3,
        scratch_shapes=[
            pltpu.VMEM((channels, height, width), f32),
            pltpu.VMEM((plan.used, plan.lanes), f32),
            pltpu.VMEM((3, depth, LANES), f32),
            pltpu.VMEM((plan.used, m_rows), bf16),
        ],
        compiler_params=within(24),
        name="image_grads",
    )(
        where, syn_order, gap, *[x for one in made for x in one], wl, prow, pcol,
        syn_images[0], adam_first[0], adam_second[0],
    )
    return tuple(out[None] for out in outs)


def solution(mesh):
    image = P("cls", "wide", None, None, None)
    return jax.shard_map(
        body,
        mesh=mesh,
        in_specs=(
            image, image, image, image, P("cls", "wide", None), P("cls", None), P("cls", None),
            P(None, "cls"), P("cls"), P("cls"),
        ),
        out_specs=(image, image, image),
        check_vma=False,
    )
```

```python
import functools

import jax
import jax.numpy as jnp
import numpy as np
from jax import lax
from jax.experimental import pallas as pl
from jax.experimental.pallas import tpu as pltpu
from jax.sharding import PartitionSpec as P

beta_one = 0.9
beta_two = 0.99
adam_step = 10.0
learn_rate = 0.1
adam_eps = 1e-08
loss_scale = 512.0
norm_eps = 1e-05

LANES = 128
SLOTS = 8
f32 = jnp.float32
bf16 = jnp.bfloat16


def mm(a, b):
    return lax.dot_general(a, b, (((1,), (0,)), ((), ())), preferred_element_type=f32)


class Plan:
    def __init__(self, channels, height, width, depth):
        self.channels, self.height, self.width, self.depth = channels, height, width, depth
        self.cols = width // 2
        self.halves = LANES // self.cols
        self.rows = height // self.halves
        self.pairs = self.rows // 4
        self.tall = self.rows + 16
        self.span = self.pairs * SLOTS
        self.lanes = self.pairs * LANES
        self.taps = 9 * channels
        self.taps_pad = -(-self.taps // 32) * 32
        self.used = 4 * channels * SLOTS
        self.deep = -(-self.used // LANES) * LANES
        self.groups = 8
        self.pixels = height * width

    def pick_rows(self):
        out = np.zeros((self.halves, self.pairs, SLOTS, self.height), np.float32)
        for half in range(self.halves):
            for pair in range(self.pairs):
                for slot in range(6):
                    row = half * self.rows + 4 * pair + slot - 1
                    if 0 <= row < self.height:
                        out[half, pair, slot, row] = 1.0
        return out.reshape(self.halves * self.span, self.height)

    def pick_cols(self):
        out = np.zeros((self.halves, self.width, 4, self.halves, self.cols), np.float32)
        for shift in range(4):
            for col in range(self.cols):
                src = 2 * col + shift - 1
                if 0 <= src < self.width:
                    for half in range(self.halves):
                        out[half, src, shift, half, col] = 1.0
        return out.reshape(self.halves * self.width, 4 * LANES)

    def pick_taps(self):
        out = np.zeros((2, 2, 2, self.deep, self.taps_pad), np.float32)
        for odd in range(2):
            for a in range(2):
                for b in range(2):
                    for i in range(3):
                        for j in range(3):
                            for c in range(self.channels):
                                k = ((b + j) * self.channels + c) * SLOTS + 2 * odd + a + i
                                out[odd, a, b, k, (i * 3 + j) * self.channels + c] = 1.0
        return out.reshape(self.groups * self.deep, self.taps_pad)


def spread(row):
    return jnp.broadcast_to(row, (LANES, row.shape[1])).T


def split_two(x):
    high = x.astype(bf16)
    return high, (x - high.astype(f32)).astype(bf16)


class Prepare:
    def __init__(self, plan, planes, pcol, rows_ref, deep_ref, sums_ref, chan_ref):
        self.plan, self.planes, self.pcol, self.rows_ref = plan, planes, pcol, rows_ref
        self.deep_ref, self.sums_ref, self.chan_ref = deep_ref, sums_ref, chan_ref

    def stages(self, cols_ref):
        plan = self.plan
        D, KU, KP, C, tall = plan.depth, plan.used, plan.deep, plan.channels, plan.tall
        shifts, blocks = [], []
        for plane in self.planes:
            rows = plane.astype(f32)
            total = functools.reduce(lambda a, b: a + b, [rows[r : r + 8] for r in range(0, plan.height, 8)])
            total = jnp.sum(jnp.sum(total, axis=1, keepdims=True), axis=0, keepdims=True)
            shifts.append(jnp.round(total * (4.0 / plan.pixels)) * 0.25)
            rows = jnp.concatenate([jnp.zeros((1, plan.width), f32), rows, jnp.zeros((15, plan.width), f32)], axis=0)
            blocks.append(
                jnp.concatenate([rows[h * plan.rows : h * plan.rows + tall] for h in range(plan.halves)], axis=1).astype(bf16)
            )
        yield
        self.rows_ref[...] = mm(jnp.concatenate(blocks, axis=0), self.pcol)
        yield
        tail = jnp.ones((KP - KU, LANES), bf16)
        gram = None
        for half in range(2):
            lean = []
            for pair in range(half * plan.pairs // 2, (half + 1) * plan.pairs // 2):
                parts = [
                    (c, self.rows_ref[c * tall + 4 * pair : c * tall + 4 * pair + SLOTS, s * LANES : (s + 1) * LANES])
                    for s in range(4)
                    for c in range(C)
                ]
                cols_ref[0:KU, pair * LANES : (pair + 1) * LANES] = jnp.concatenate([x for _, x in parts], axis=0).astype(bf16)
                own = jnp.concatenate([x - shifts[c] for c, x in parts], axis=0).astype(bf16)
                lean.append(jnp.concatenate([own, tail], axis=0))
            yield
            lean = jnp.concatenate(lean, axis=1)
            part = lax.dot_general(lean, lean, (((1,), (1,)), ((), ())), preferred_element_type=f32)
            gram = part if gram is None else gram + part
            yield
        moved = gram
        for step in (1, 2, C * SLOTS):
            moved = moved + pltpu.roll(pltpu.roll(moved, KP - step, 0), KP - step, 1)
        high = moved.astype(bf16)
        rest = moved - high.astype(f32)
        mid = rest.astype(bf16)
        low = (rest - mid.astype(f32)).astype(bf16)
        quad = mm(self.deep_ref[...], jnp.concatenate([high, mid, low], axis=0))
        yield
        first = self.deep_ref[:, 0:KP].astype(f32)
        second = jnp.sum(quad * first, axis=1, keepdims=True) * (1.0 / plan.pixels)
        off = jnp.sum(self.sums_ref[...] * gram[KU : KU + 1, :], axis=1, keepdims=True) * (1.0 / plan.pixels)
        second = jnp.broadcast_to(second, (D, LANES))
        off = jnp.broadcast_to(off, (D, LANES))
        mean = off
        for c in range(C):
            mean = mean + shifts[c] * self.chan_ref[2 + c]
        var = jnp.maximum(second - off * off, 0.0) + norm_eps
        self.factor = lax.rsqrt(var)
        self.scale = self.chan_ref[0] * self.factor
        self.mean = mean
        self.thr = mean - self.chan_ref[1] * (var * self.factor)
        yield


def is_chosen(order_ref, batch, gid):
    return lax.fori_loop(0, batch, lambda j, t: t | (order_ref[0, j] == gid).astype(jnp.int32), jnp.int32(0))


def make_weights(plan, param_ref, ptap_ref, wl_ref, deep_ref, sums_ref, chan_ref):
    D, KP, C = plan.depth, plan.deep, plan.channels
    spread_taps = mm(ptap_ref[...], param_ref[0 : plan.taps_pad, :])
    sums = None
    for g in range(plan.groups):
        odd, phase = divmod(g, 4)
        turned = spread_taps[g * KP : (g + 1) * KP, :].T
        sums = turned if sums is None else sums + turned
        turned = turned.astype(bf16)
        if g == 0:
            for n in range(3):
                deep_ref[:, n * KP : (n + 1) * KP] = turned
        for blk in range(D // 16):
            at = ((odd * (D // 16) + blk) * 4 + phase) * 16
            rows = turned[blk * 16 : (blk + 1) * 16, :]
            wl_ref[at : at + 16, :] = rows
    sums_ref[...] = sums
    gain = param_ref[plan.taps_pad : plan.taps_pad + 1, :].astype(f32)
    bias = param_ref[plan.taps_pad + 1 : plan.taps_pad + 2, :].astype(f32)
    chan_ref[0] = spread(gain)
    chan_ref[1] = spread(bias / gain)
    first = spread_taps[0:KP, :]
    for c in range(C):
        total = functools.reduce(lambda a, b: a + b, [first[(s * C + c) * SLOTS : (s * C + c + 1) * SLOTS] for s in range(4)])
        chan_ref[2 + c] = spread(jnp.sum(total, axis=0, keepdims=True))


def forward_kernel(
    plan, n_own, batch, where_ref, pick_ref, count_ref, order_ref,
    pool_ref, syn_ref, pcol_ref, ptap_ref, param_ref,
    part_ref, wl_ref,
    all_ref, rows_ref, deep_ref, sums_ref, chan_ref, now_ref, next_ref, thr_ref, coef_ref,
):
    D, KP, KU, C = plan.depth, plan.deep, plan.used, plan.channels
    pos = where_ref[0]
    n_pool = pool_ref.shape[0]
    own_count = count_ref[0, pos]
    total = lax.fori_loop(0, count_ref.shape[1], lambda i, t: t + count_ref[0, i], jnp.int32(0)).astype(f32)
    flags = [is_chosen(order_ref, batch, pos * n_own + i) for i in range(n_own)]
    n_syn = functools.reduce(lambda a, b: a + b, flags)

    make_weights(plan, param_ref, ptap_ref, wl_ref, deep_ref, sums_ref, chan_ref)
    for i in range(n_own):
        all_ref[n_pool + i] = syn_ref[i].astype(bf16)
    all_ref[0:n_pool] = pool_ref[...]
    part_ref[...] = jnp.zeros_like(part_ref)
    if KP > KU:
        now_ref[KU:KP, :] = jnp.zeros((KP - KU, plan.lanes), bf16)

    def image_of(i):
        syn_at = jnp.int32(n_pool + n_own - 1)
        before = n_syn
        for s in reversed(range(n_own)):
            before = before - flags[s]
            syn_at = jnp.where((flags[s] > 0) & (i == before), n_pool + s, syn_at)
        real_at = pick_ref[0, 0, jnp.clip(i - n_syn, 0, n_pool - 1)]
        return jnp.where(i < n_syn, syn_at, real_at), jnp.where(i < n_syn, 0.25 / batch, -0.25 / total)

    def begin(i):
        at, weight = image_of(i)
        planes = [all_ref[at, c] for c in range(C)]
        return Prepare(plan, planes, pcol_ref[...], rows_ref, deep_ref, sums_ref, chan_ref), weight

    prep, weight = begin(jnp.int32(0))
    for _ in prep.stages(now_ref):
        pass
    thr_ref[...] = prep.thr
    coef_ref[...] = prep.scale * weight
    tile = 2 * LANES

    def step(i, base):
        prep, weight = begin(i + 1)
        ahead = prep.stages(next_ref)
        base = base + coef_ref[...] * thr_ref[...]
        wide = 2 * tile
        for t in range(plan.lanes // wide):
            at = t * wide
            y = mm(wl_ref[...], now_ref[:, at : at + wide])
            for _ in range((3, 3, 2, 0)[min(t, 3)]):
                next(ahead, None)
            for odd in range(2):
                for blk in range(D // 16):
                    r0 = (odd * (D // 16) + blk) * 64
                    thr = thr_ref[blk * 16 : (blk + 1) * 16, :]
                    coef = coef_ref[blk * 16 : (blk + 1) * 16, :]
                    out = slice(odd * D + blk * 16, odd * D + (blk + 1) * 16)
                    for half in range(wide // LANES):
                        lanes = slice(half * LANES, (half + 1) * LANES)
                        ys = [jnp.maximum(y[r0 + p * 16 : r0 + (p + 1) * 16, lanes], thr) for p in range(4)]
                        here = slice(at + half * LANES, at + (half + 1) * LANES)
                        part_ref[out, here] += coef * ((ys[0] + ys[1]) + (ys[2] + ys[3]))
        for _ in ahead:
            pass
        now_ref[0:KU, :] = next_ref[0:KU, :]
        thr_ref[...] = prep.thr
        coef_ref[...] = prep.scale * weight
        return base

    base = lax.fori_loop(0, n_syn + own_count, step, jnp.zeros((D, LANES), f32))
    base = 4.0 * base
    for pair in range(plan.pairs):
        for odd in range(2):
            part_ref[odd * D : (odd + 1) * D, pair * LANES : (pair + 1) * LANES] -= base


def middle_kernel(
    plan, n_own, batch, own, where_ref, order_ref, syn_ref, pcol_ref, ptap_ref, param_ref,
    cols_ref, vsum_ref, hits_ref, stat_ref,
    wl_ref, rows_ref, deep_ref, sums_ref, chan_ref,
):
    D, KP, KU, C = plan.depth, plan.deep, plan.used, plan.channels
    flag = is_chosen(order_ref, batch, where_ref[0] * n_own + own)
    tile = 2 * LANES

    @pl.when(flag > 0)
    def _():
        make_weights(plan, param_ref, ptap_ref, wl_ref, deep_ref, sums_ref, chan_ref)
        if KP > KU:
            cols_ref[KU:KP, :] = jnp.zeros((KP - KU, plan.lanes), bf16)
        planes = [syn_ref[own, c].astype(bf16) for c in range(C)]
        prep = Prepare(plan, planes, pcol_ref[...], rows_ref, deep_ref, sums_ref, chan_ref)
        for _ in prep.stages(cols_ref):
            pass
        for n, value in enumerate((prep.mean, prep.factor, prep.scale, prep.thr, chan_ref[0], chan_ref[1])):
            stat_ref[n] = value

        for t in range(plan.lanes // tile):
            at = t * tile
            y = mm(wl_ref[...], cols_ref[:, at : at + tile])
            for odd in range(2):
                for blk in range(D // 16):
                    r0 = (odd * (D // 16) + blk) * 64
                    thr = stat_ref[3, blk * 16 : (blk + 1) * 16, :]
                    out = slice(odd * D + blk * 16, odd * D + (blk + 1) * 16)
                    for half in range(2):
                        lanes = slice(half * LANES, (half + 1) * LANES)
                        yp = [y[r0 + p * 16 : r0 + (p + 1) * 16, lanes] for p in range(4)]
                        ys = [jnp.maximum(a, thr) for a in yp]
                        hs = [jnp.where(a > thr, 1.0, 0.0) for a in yp]
                        here = slice(at + half * LANES, at + (half + 1) * LANES)
                        vsum_ref[out, here] = ((ys[0] + ys[1]) + (ys[2] + ys[3])) - 4.0 * thr
                        hits_ref[out, here] = (hs[0] + hs[1]) + (hs[2] + hs[3])


def backward_kernel(
    plan, n_own, batch, where_ref, order_ref, *refs,
):
    D, KU, blocks = plan.depth, plan.used, plan.depth // 16
    gap_ref = refs[0]
    owns = [refs[1 + 4 * i : 5 + 4 * i] for i in range(n_own)]
    (
        wl_ref, prow_ref, pcol_ref, syn_ref, first_ref, second_ref,
        new_syn_ref, new_first_ref, new_second_ref,
        grad_ref, dcols_ref, col_ref, wlt_ref,
    ) = refs[1 + 4 * n_own :]
    pos = where_ref[0]
    tile = 2 * LANES
    grad_factor = 2.0 * loss_scale / batch
    for g in range(plan.groups):
        wlt_ref[:, g * D : (g + 1) * D] = wl_ref[g * D : (g + 1) * D, :].astype(f32).T.astype(bf16)[0:KU, :]

    for i in range(n_own):
        cols_ref, vsum_ref, hits_ref, stat_ref = owns[i]
        flag = is_chosen(order_ref, batch, pos * n_own + i)

        @pl.when(flag == 0)
        def _():
            grad_ref[...] = jnp.zeros_like(grad_ref)

        @pl.when(flag > 0)
        def _():
            unit = grad_factor / (4.0 * plan.pixels)
            for blk in range(blocks):
                chan = slice(blk * 16, (blk + 1) * 16)
                one = two = jnp.zeros((16, LANES), f32)
                for pair in range(plan.pairs):
                    here = slice(pair * LANES, (pair + 1) * LANES)
                    for odd in range(2):
                        rows = slice(odd * D + blk * 16, odd * D + (blk + 1) * 16)
                        gap = gap_ref[rows, here]
                        one = one + gap * hits_ref[rows, here]
                        two = two + gap * vsum_ref[rows, here]
                one = jnp.broadcast_to(jnp.sum(one, axis=1, keepdims=True), (16, LANES)) * unit
                two = jnp.broadcast_to(jnp.sum(two, axis=1, keepdims=True), (16, LANES)) * unit
                mean, factor, scale, thr, gain, ratio = [stat_ref[n, chan, :] for n in range(6)]
                slope = factor * factor * (scale * two - one * (ratio * gain))
                col_ref[0, chan, :] = factor * gain * (0.25 * grad_factor)
                col_ref[1, chan, :] = slope
                col_ref[2, chan, :] = slope * mean - factor * (gain * one)

            for t in range(plan.lanes // tile):
                at = t * tile
                y = mm(wl_ref[...], cols_ref[:, at : at + tile])
                inner = []
                for odd in range(2):
                    for blk in range(blocks):
                        r0 = (odd * blocks + blk) * 64
                        chan = slice(blk * 16, (blk + 1) * 16)
                        thr_b, up_b, slope_b, off = stat_ref[3, chan, :], col_ref[0, chan, :], col_ref[1, chan, :], col_ref[2, chan, :]
                        ons = []
                        for half in range(2):
                            gap = gap_ref[odd * D + blk * 16 : odd * D + (blk + 1) * 16, at + half * LANES : at + (half + 1) * LANES]
                            ons.append(up_b * gap + off)
                        for p in range(4):
                            both = []
                            for half in range(2):
                                yp = y[r0 + p * 16 : r0 + (p + 1) * 16, half * LANES : (half + 1) * LANES]
                                both.append((jnp.where(yp > thr_b, ons[half], off) - slope_b * yp).astype(bf16))
                            inner.append(jnp.concatenate(both, axis=1))
                dcols_ref[:, at : at + tile] = mm(wlt_ref[...], jnp.concatenate(inner, axis=0))

            shifts = []
            for s in range(4):
                shifts.append(
                    jnp.concatenate(
                        [
                            dcols_ref[
                                (s * plan.channels + c) * SLOTS : (s * plan.channels + c + 1) * SLOTS,
                                pair * LANES : (pair + 1) * LANES,
                            ]
                            for c in range(plan.channels)
                            for pair in range(plan.pairs)
                        ],
                        axis=0,
                    )
                )
            high, low = split_two(jnp.concatenate(shifts, axis=1))
            back = (((1,), (1,)), ((), ()))
            pcol = pcol_ref[...]
            wide = lax.dot_general(high, pcol, back, preferred_element_type=f32) + lax.dot_general(
                low, pcol, back, preferred_element_type=f32
            )
            tall = jnp.concatenate(
                [
                    jnp.concatenate(
                        [
                            wide[c * plan.span : (c + 1) * plan.span, half * plan.width : (half + 1) * plan.width]
                            for c in range(plan.channels)
                        ],
                        axis=1,
                    )
                    for half in range(plan.halves)
                ],
                axis=0,
            )
            high, low = split_two(tall)
            prow = prow_ref[...].T
            image = mm(prow, high) + mm(prow, low)
            for c in range(plan.channels):
                grad_ref[c] = image[:, c * plan.width : (c + 1) * plan.width]

        for c in range(plan.channels):
            grad = grad_ref[c]
            first_new = beta_one * first_ref[i, c] + (1.0 - beta_one) * grad
            second_new = beta_two * second_ref[i, c] + (1.0 - beta_two) * grad * grad
            corrected = first_new / (1.0 - beta_one**adam_step)
            scale_hat = jnp.sqrt(second_new / (1.0 - beta_two**adam_step))
            new_syn_ref[i, c] = syn_ref[i, c] - learn_rate * corrected / (scale_hat + adam_eps)
            new_first_ref[i, c] = first_new
            new_second_ref[i, c] = second_new


def gather_params(conv_weight, norm_gain, norm_bias, taps_pad):
    taps, width = conv_weight.shape
    own = jnp.concatenate(
        [
            conv_weight,
            jnp.zeros((taps_pad - taps, width), conv_weight.dtype),
            norm_gain[None],
            norm_bias[None],
            jnp.zeros((14, width), conv_weight.dtype),
        ],
        axis=0,
    )
    if lax.axis_size("cls") == 2:
        other = lax.ppermute(own, "cls", [(0, 1), (1, 0)])
        low = lax.axis_index("cls") == 0
        return jnp.concatenate([jnp.where(low, own, other), jnp.where(low, other, own)], axis=1)
    return lax.all_gather(own, "cls", axis=1, tiled=True)


class Exchange:
    def __init__(self):
        self.n = lax.axis_size("wide")
        self.pos = lax.axis_index("wide")
        steps = []
        while 1 << (len(steps) + 1) <= self.n:
            steps.append(1 << len(steps))
        self.first, rest = steps[0], steps[1:]
        self.masks = [(self.first, self.first)] + list(zip(rest, rest[1:] + rest[:1]))

    def swap(self, x, masks):
        return lax.ppermute(x, "wide", [(i, i ^ masks[i & self.first]) for i in range(self.n)])

    def high(self, masks):
        return (self.pos & jnp.where((self.pos & self.first) > 0, masks[1], masks[0])) > 0

    def add(self, own, masks):
        high = self.high(masks)
        rows = own.shape[0] // 2
        kept = jnp.where(high, own[rows:], own[:rows])
        sent = jnp.where(high, own[:rows], own[rows:]).astype(jnp.float16)
        return kept, sent

    def join(self, own, other, masks):
        high = self.high(masks)
        return jnp.concatenate([jnp.where(high, other, own), jnp.where(high, own, other)], axis=0)


def exchange_sum(part, where, middle, n_own):
    ex = Exchange()
    halved = ex.masks[:2]
    whole = ex.masks[2:]
    rounds = [(m, "halve") for m in halved] + [(m, "whole") for m in whole] + [(m, "join") for m in reversed(halved)]
    at_round = [1 + (len(rounds) - 3) * i // max(n_own - 1, 1) for i in range(n_own)]
    own, made = part, []
    for n, (masks, kind) in enumerate(rounds):
        if kind == "halve":
            own, sent = ex.add(own, masks)
        else:
            sent = own.astype(jnp.float16)
        todo = [i for i in range(n_own) if at_round[i] == n]
        if todo:
            sent, held = lax.optimization_barrier((sent, where))
        got = ex.swap(sent, masks)
        if todo:
            new = [middle(i, held) for i in todo]
            if n + 1 < len(rounds):
                got, new = lax.optimization_barrier((got, new))
            made += new
        own = ex.join(sent, got, masks) if kind == "join" else own + got.astype(f32)
    return own.astype(f32), made


def body(
    syn_images, adam_first, adam_second, real_pool, real_pick, real_count, syn_order,
    conv_weight, norm_gain, norm_bias,
):
    _, n_own, channels, height, width = syn_images.shape
    batch = syn_order.shape[1] // 2
    depth = conv_weight.shape[1] * lax.axis_size("cls")
    plan = Plan(channels, height, width, depth)
    prow = jnp.asarray(plan.pick_rows(), bf16)
    pcol = jnp.asarray(plan.pick_cols(), bf16)
    ptap = jnp.asarray(plan.pick_taps(), bf16)
    params = gather_params(conv_weight, norm_gain, norm_bias, plan.taps_pad)
    where = lax.axis_index("wide").astype(jnp.int32)[None]

    smem = pl.BlockSpec(memory_space=pltpu.SMEM)
    vmem = pl.BlockSpec(memory_space=pltpu.VMEM)
    shape = jax.ShapeDtypeStruct
    rows = 2 * depth
    m_rows = plan.groups * depth
    weights = [
        pltpu.VMEM((channels * plan.tall, 4 * LANES), f32),
        pltpu.VMEM((depth, 3 * plan.deep), bf16),
        pltpu.VMEM((depth, plan.deep), f32),
        pltpu.VMEM((2 + channels, depth, LANES), f32),
    ]

    def within(mib):
        return pltpu.CompilerParams(vmem_limit_bytes=mib << 20)

    part, wl = pl.pallas_call(
        functools.partial(forward_kernel, plan, n_own, batch),
        in_specs=[smem] * 4 + [vmem] * 5,
        out_specs=[vmem] * 2,
        out_shape=[shape((rows, plan.lanes), f32), shape((m_rows, plan.deep), bf16)],
        scratch_shapes=[
            pltpu.VMEM((real_pool.shape[1] + n_own, channels, height, width), bf16),
            *weights,
            pltpu.VMEM((plan.deep, plan.lanes), bf16),
            pltpu.VMEM((plan.used, plan.lanes), bf16),
            *[pltpu.VMEM((depth, LANES), f32)] * 2,
        ],
        compiler_params=within(60),
        name="embed_sums",
    )(where, real_pick, real_count, syn_order, real_pool[0], syn_images[0], pcol, ptap, params)

    def middle(own, held):
        return pl.pallas_call(
            functools.partial(middle_kernel, plan, n_own, batch, own),
            in_specs=[smem] * 2 + [vmem] * 4,
            out_specs=[vmem] * 4,
            out_shape=[
                shape((plan.deep, plan.lanes), bf16),
                shape((rows, plan.lanes), f32),
                shape((rows, plan.lanes), f32),
                shape((6, depth, LANES), f32),
            ],
            scratch_shapes=[pltpu.VMEM((m_rows, plan.deep), bf16), *weights],
            compiler_params=within(18),
            name="syn_features",
        )(held, syn_order, syn_images[0], pcol, ptap, params)

    gap, made = exchange_sum(part, where, middle, n_own)

    img = shape((n_own, channels, height, width), f32)
    outs = pl.pallas_call(
        functools.partial(backward_kernel, plan, n_own, batch),
        in_specs=[smem] * 2 + [vmem] * (7 + 4 * n_own),
        out_specs=[vmem] * 3,
        out_shape=[img] * 3,
        scratch_shapes=[
            pltpu.VMEM((channels, height, width), f32),
            pltpu.VMEM((plan.used, plan.lanes), f32),
            pltpu.VMEM((3, depth, LANES), f32),
            pltpu.VMEM((plan.used, m_rows), bf16),
        ],
        compiler_params=within(24),
        name="image_grads",
    )(
        where, syn_order, gap, *[x for one in made for x in one], wl, prow, pcol,
        syn_images[0], adam_first[0], adam_second[0],
    )
    return tuple(out[None] for out in outs)


def solution(mesh):
    image = P("cls", "wide", None, None, None)
    return jax.shard_map(
        body,
        mesh=mesh,
        in_specs=(
            image, image, image, image, P("cls", "wide", None), P("cls", None), P("cls", None),
            P(None, "cls"), P("cls"), P("cls"),
        ),
        out_specs=(image, image, image),
        check_vma=False,
    )
```

```python
import functools

import jax
import jax.numpy as jnp
import numpy as np
from jax import lax
from jax.experimental import pallas as pl
from jax.experimental.pallas import tpu as pltpu
from jax.sharding import PartitionSpec as P

beta_one = 0.9
beta_two = 0.99
adam_step = 10.0
learn_rate = 0.1
adam_eps = 1e-08
loss_scale = 512.0
norm_eps = 1e-05

LANES = 128
SLOTS = 8
f32 = jnp.float32
bf16 = jnp.bfloat16


def mm(a, b):
    return lax.dot_general(a, b, (((1,), (0,)), ((), ())), preferred_element_type=f32)


class Plan:
    def __init__(self, channels, height, width, depth):
        self.channels, self.height, self.width, self.depth = channels, height, width, depth
        self.cols = width // 2
        self.halves = LANES // self.cols
        self.rows = height // self.halves
        self.pairs = self.rows // 4
        self.tall = self.rows + 16
        self.span = self.pairs * SLOTS
        self.lanes = self.pairs * LANES
        self.taps = 9 * channels
        self.taps_pad = -(-self.taps // 32) * 32
        self.used = 4 * channels * SLOTS
        self.deep = -(-self.used // LANES) * LANES
        self.groups = 8
        self.pixels = height * width

    def pick_rows(self):
        out = np.zeros((self.halves, self.pairs, SLOTS, self.height), np.float32)
        for half in range(self.halves):
            for pair in range(self.pairs):
                for slot in range(6):
                    row = half * self.rows + 4 * pair + slot - 1
                    if 0 <= row < self.height:
                        out[half, pair, slot, row] = 1.0
        return out.reshape(self.halves * self.span, self.height)

    def pick_cols(self):
        out = np.zeros((self.halves, self.width, 4, self.halves, self.cols), np.float32)
        for shift in range(4):
            for col in range(self.cols):
                src = 2 * col + shift - 1
                if 0 <= src < self.width:
                    for half in range(self.halves):
                        out[half, src, shift, half, col] = 1.0
        return out.reshape(self.halves * self.width, 4 * LANES)

    def pick_taps(self):
        out = np.zeros((2, 2, 2, self.deep, self.taps_pad), np.float32)
        for odd in range(2):
            for a in range(2):
                for b in range(2):
                    for i in range(3):
                        for j in range(3):
                            for c in range(self.channels):
                                k = ((b + j) * self.channels + c) * SLOTS + 2 * odd + a + i
                                out[odd, a, b, k, (i * 3 + j) * self.channels + c] = 1.0
        return out.reshape(self.groups * self.deep, self.taps_pad)


def spread(row):
    return jnp.broadcast_to(row, (LANES, row.shape[1])).T


def split_two(x):
    high = x.astype(bf16)
    return high, (x - high.astype(f32)).astype(bf16)


class Prepare:
    def __init__(self, plan, planes, pcol, rows_ref, deep_ref, sums_ref, chan_ref):
        self.plan, self.planes, self.pcol, self.rows_ref = plan, planes, pcol, rows_ref
        self.deep_ref, self.sums_ref, self.chan_ref = deep_ref, sums_ref, chan_ref

    def stages(self, cols_ref):
        plan = self.plan
        D, KU, KP, C, tall = plan.depth, plan.used, plan.deep, plan.channels, plan.tall
        shifts, blocks = [], []
        for plane in self.planes:
            rows = plane.astype(f32)
            total = functools.reduce(lambda a, b: a + b, [rows[r : r + 8] for r in range(0, plan.height, 8)])
            total = jnp.sum(jnp.sum(total, axis=1, keepdims=True), axis=0, keepdims=True)
            shifts.append(jnp.round(total * (4.0 / plan.pixels)) * 0.25)
            rows = jnp.concatenate([jnp.zeros((1, plan.width), f32), rows, jnp.zeros((15, plan.width), f32)], axis=0)
            blocks.append(
                jnp.concatenate([rows[h * plan.rows : h * plan.rows + tall] for h in range(plan.halves)], axis=1).astype(bf16)
            )
        yield
        self.rows_ref[...] = mm(jnp.concatenate(blocks, axis=0), self.pcol)
        yield
        tail = jnp.ones((KP - KU, LANES), bf16)
        gram = None
        for half in range(2):
            lean = []
            for pair in range(half * plan.pairs // 2, (half + 1) * plan.pairs // 2):
                parts = [
                    (c, self.rows_ref[c * tall + 4 * pair : c * tall + 4 * pair + SLOTS, s * LANES : (s + 1) * LANES])
                    for s in range(4)
                    for c in range(C)
                ]
                cols_ref[0:KU, pair * LANES : (pair + 1) * LANES] = jnp.concatenate([x for _, x in parts], axis=0).astype(bf16)
                own = jnp.concatenate([x - shifts[c] for c, x in parts], axis=0).astype(bf16)
                lean.append(jnp.concatenate([own, tail], axis=0))
            yield
            lean = jnp.concatenate(lean, axis=1)
            part = lax.dot_general(lean, lean, (((1,), (1,)), ((), ())), preferred_element_type=f32)
            gram = part if gram is None else gram + part
            yield
        moved = gram
        for step in (1, 2, C * SLOTS):
            moved = moved + pltpu.roll(pltpu.roll(moved, KP - step, 0), KP - step, 1)
        high = moved.astype(bf16)
        rest = moved - high.astype(f32)
        mid = rest.astype(bf16)
        low = (rest - mid.astype(f32)).astype(bf16)
        quad = mm(self.deep_ref[...], jnp.concatenate([high, mid, low], axis=0))
        yield
        first = self.deep_ref[:, 0:KP].astype(f32)
        second = jnp.sum(quad * first, axis=1, keepdims=True) * (1.0 / plan.pixels)
        off = jnp.sum(self.sums_ref[...] * gram[KU : KU + 1, :], axis=1, keepdims=True) * (1.0 / plan.pixels)
        second = jnp.broadcast_to(second, (D, LANES))
        off = jnp.broadcast_to(off, (D, LANES))
        mean = off
        for c in range(C):
            mean = mean + shifts[c] * self.chan_ref[2 + c]
        var = jnp.maximum(second - off * off, 0.0) + norm_eps
        self.factor = lax.rsqrt(var)
        self.scale = self.chan_ref[0] * self.factor
        self.mean = mean
        self.thr = mean - self.chan_ref[1] * (var * self.factor)
        yield


def is_chosen(order_ref, batch, gid):
    return lax.fori_loop(0, batch, lambda j, t: t | (order_ref[0, j] == gid).astype(jnp.int32), jnp.int32(0))


def make_weights(plan, param_ref, ptap_ref, wl_ref, deep_ref, sums_ref, chan_ref):
    D, KP, C = plan.depth, plan.deep, plan.channels
    spread_taps = mm(ptap_ref[...], param_ref[0 : plan.taps_pad, :])
    sums = None
    for g in range(plan.groups):
        odd, phase = divmod(g, 4)
        turned = spread_taps[g * KP : (g + 1) * KP, :].T
        sums = turned if sums is None else sums + turned
        turned = turned.astype(bf16)
        if g == 0:
            for n in range(3):
                deep_ref[:, n * KP : (n + 1) * KP] = turned
        for blk in range(D // 16):
            at = ((odd * (D // 16) + blk) * 4 + phase) * 16
            rows = turned[blk * 16 : (blk + 1) * 16, :]
            wl_ref[at : at + 16, :] = rows
    sums_ref[...] = sums
    gain = param_ref[plan.taps_pad : plan.taps_pad + 1, :].astype(f32)
    bias = param_ref[plan.taps_pad + 1 : plan.taps_pad + 2, :].astype(f32)
    chan_ref[0] = spread(gain)
    chan_ref[1] = spread(bias / gain)
    first = spread_taps[0:KP, :]
    for c in range(C):
        total = functools.reduce(lambda a, b: a + b, [first[(s * C + c) * SLOTS : (s * C + c + 1) * SLOTS] for s in range(4)])
        chan_ref[2 + c] = spread(jnp.sum(total, axis=0, keepdims=True))


def forward_kernel(
    plan, n_own, batch, where_ref, pick_hbm, count_hbm, order_hbm,
    pool_hbm, sent_hbm, syn_hbm, pcol_hbm, ptap_hbm, param_ref,
    part_ref, wl_ref,
    all_ref, rows_ref, deep_ref, sums_ref, chan_ref, now_ref, next_ref, thr_ref, coef_ref,
    pick_ref, count_ref, order_ref, syn_ref, pcol_ref, ptap_ref, sems,
):
    D, KP, KU, C = plan.depth, plan.deep, plan.used, plan.channels
    n_pool, n_sent = pool_hbm.shape[0], sent_hbm.shape[0]
    copies = [
        pltpu.make_async_copy(src, dst, sems.at[n])
        for n, (src, dst) in enumerate(
            (
                (ptap_hbm, ptap_ref),
                (pick_hbm, pick_ref),
                (count_hbm, count_ref),
                (order_hbm, order_ref),
                (pcol_hbm, pcol_ref),
                (syn_hbm, syn_ref),
                (pool_hbm, all_ref.at[pl.ds(0, n_pool)]),
                (sent_hbm, all_ref.at[pl.ds(n_pool, n_sent)]),
            )
        )
    ]
    for copy in copies:
        copy.start()
    part_ref[...] = jnp.zeros_like(part_ref)
    if KP > KU:
        now_ref[KU:KP, :] = jnp.zeros((KP - KU, plan.lanes), bf16)
    for copy in copies:
        copy.wait()

    pos = where_ref[0]
    mate_count = count_ref[0, pos ^ 1]
    own_count = count_ref[0, pos]
    own_count = own_count - jnp.where(own_count == n_pool, n_sent, 0)
    mate_count = jnp.where(mate_count == n_pool, n_sent, 0)
    total = lax.fori_loop(0, count_ref.shape[1], lambda i, t: t + count_ref[0, i], jnp.int32(0)).astype(f32)
    flags = [is_chosen(order_ref, batch, pos * n_own + i) for i in range(n_own)]
    n_syn = functools.reduce(lambda a, b: a + b, flags)

    make_weights(plan, param_ref, ptap_ref, wl_ref, deep_ref, sums_ref, chan_ref)
    n_real = n_pool + n_sent
    for i in range(n_own):
        all_ref[n_real + i] = syn_ref[i].astype(bf16)

    def image_of(i):
        syn_at = jnp.int32(n_real + n_own - 1)
        before = n_syn
        for s in reversed(range(n_own)):
            before = before - flags[s]
            syn_at = jnp.where((flags[s] > 0) & (i == before), n_real + s, syn_at)
        own_at = pick_ref[0, 0, jnp.clip(i - n_syn, 0, n_pool - 1)]
        sent_at = n_pool + jnp.clip(i - n_syn - own_count, 0, n_sent - 1)
        real_at = jnp.where(i - n_syn < own_count, own_at, sent_at)
        return jnp.where(i < n_syn, syn_at, real_at), jnp.where(i < n_syn, 0.25 / batch, -0.25 / total)

    def begin(i):
        at, weight = image_of(i)
        planes = [all_ref[at, c] for c in range(C)]
        return Prepare(plan, planes, pcol_ref[...], rows_ref, deep_ref, sums_ref, chan_ref), weight

    prep, weight = begin(jnp.int32(0))
    for _ in prep.stages(now_ref):
        pass
    thr_ref[...] = prep.thr
    coef_ref[...] = prep.scale * weight
    tile = 2 * LANES

    def step(i, base):
        prep, weight = begin(i + 1)
        ahead = prep.stages(next_ref)
        base = base + coef_ref[...] * thr_ref[...]
        wide = 2 * tile
        for t in range(plan.lanes // wide):
            at = t * wide
            y = mm(wl_ref[...], now_ref[:, at : at + wide])
            for _ in range((3, 3, 2, 0)[min(t, 3)]):
                next(ahead, None)
            for odd in range(2):
                for blk in range(D // 16):
                    r0 = (odd * (D // 16) + blk) * 64
                    thr = thr_ref[blk * 16 : (blk + 1) * 16, :]
                    coef = coef_ref[blk * 16 : (blk + 1) * 16, :]
                    out = slice(odd * D + blk * 16, odd * D + (blk + 1) * 16)
                    for half in range(wide // LANES):
                        lanes = slice(half * LANES, (half + 1) * LANES)
                        ys = [jnp.maximum(y[r0 + p * 16 : r0 + (p + 1) * 16, lanes], thr) for p in range(4)]
                        here = slice(at + half * LANES, at + (half + 1) * LANES)
                        part_ref[out, here] += coef * ((ys[0] + ys[1]) + (ys[2] + ys[3]))
        for _ in ahead:
            pass
        now_ref[0:KU, :] = next_ref[0:KU, :]
        thr_ref[...] = prep.thr
        coef_ref[...] = prep.scale * weight
        return base

    base = lax.fori_loop(0, n_syn + own_count + mate_count, step, jnp.zeros((D, LANES), f32))
    base = 4.0 * base
    for pair in range(plan.pairs):
        for odd in range(2):
            part_ref[odd * D : (odd + 1) * D, pair * LANES : (pair + 1) * LANES] -= base


def middle_kernel(
    plan, n_own, batch, own, where_ref, order_ref, syn_ref, pcol_ref, ptap_ref, param_ref,
    cols_ref, vsum_ref, hits_ref, stat_ref,
    wl_ref, rows_ref, deep_ref, sums_ref, chan_ref,
):
    D, KP, KU, C = plan.depth, plan.deep, plan.used, plan.channels
    flag = is_chosen(order_ref, batch, where_ref[0] * n_own + own)
    tile = 2 * LANES

    @pl.when(flag > 0)
    def _():
        make_weights(plan, param_ref, ptap_ref, wl_ref, deep_ref, sums_ref, chan_ref)
        if KP > KU:
            cols_ref[KU:KP, :] = jnp.zeros((KP - KU, plan.lanes), bf16)
        planes = [syn_ref[own, c].astype(bf16) for c in range(C)]
        prep = Prepare(plan, planes, pcol_ref[...], rows_ref, deep_ref, sums_ref, chan_ref)
        for _ in prep.stages(cols_ref):
            pass
        for n, value in enumerate((prep.mean, prep.factor, prep.scale, prep.thr, chan_ref[0], chan_ref[1])):
            stat_ref[n] = value

        for t in range(plan.lanes // tile):
            at = t * tile
            y = mm(wl_ref[...], cols_ref[:, at : at + tile])
            for odd in range(2):
                for blk in range(D // 16):
                    r0 = (odd * (D // 16) + blk) * 64
                    thr = stat_ref[3, blk * 16 : (blk + 1) * 16, :]
                    out = slice(odd * D + blk * 16, odd * D + (blk + 1) * 16)
                    for half in range(2):
                        lanes = slice(half * LANES, (half + 1) * LANES)
                        yp = [y[r0 + p * 16 : r0 + (p + 1) * 16, lanes] for p in range(4)]
                        ys = [jnp.maximum(a, thr) for a in yp]
                        hs = [jnp.where(a > thr, 1.0, 0.0) for a in yp]
                        here = slice(at + half * LANES, at + (half + 1) * LANES)
                        vsum_ref[out, here] = ((ys[0] + ys[1]) + (ys[2] + ys[3])) - 4.0 * thr
                        hits_ref[out, here] = (hs[0] + hs[1]) + (hs[2] + hs[3])


def backward_kernel(
    plan, n_own, batch, where_ref, order_ref, *refs,
):
    D, KU, blocks = plan.depth, plan.used, plan.depth // 16
    gap_ref = refs[0]
    owns = [refs[1 + 4 * i : 5 + 4 * i] for i in range(n_own)]
    (
        wl_ref, prow_ref, pcol_ref, syn_ref, first_hbm, second_hbm,
        new_syn_ref, new_first_ref, new_second_ref,
        grad_ref, dcols_ref, col_ref, wlt_ref, first_ref, second_ref, sems,
    ) = refs[1 + 4 * n_own :]
    moments = [
        pltpu.make_async_copy(first_hbm, first_ref, sems.at[0]),
        pltpu.make_async_copy(second_hbm, second_ref, sems.at[1]),
    ]
    for copy in moments:
        copy.start()
    pos = where_ref[0]
    tile = 2 * LANES
    grad_factor = 2.0 * loss_scale / batch
    for g in range(plan.groups):
        wlt_ref[:, g * D : (g + 1) * D] = wl_ref[g * D : (g + 1) * D, :].astype(f32).T.astype(bf16)[0:KU, :]

    for i in range(n_own):
        cols_ref, vsum_ref, hits_ref, stat_ref = owns[i]
        flag = is_chosen(order_ref, batch, pos * n_own + i)

        @pl.when(flag == 0)
        def _():
            grad_ref[...] = jnp.zeros_like(grad_ref)

        @pl.when(flag > 0)
        def _():
            unit = grad_factor / (4.0 * plan.pixels)
            for blk in range(blocks):
                chan = slice(blk * 16, (blk + 1) * 16)
                one = two = jnp.zeros((16, LANES), f32)
                for pair in range(plan.pairs):
                    here = slice(pair * LANES, (pair + 1) * LANES)
                    for odd in range(2):
                        rows = slice(odd * D + blk * 16, odd * D + (blk + 1) * 16)
                        gap = gap_ref[rows, here]
                        one = one + gap * hits_ref[rows, here]
                        two = two + gap * vsum_ref[rows, here]
                one = jnp.broadcast_to(jnp.sum(one, axis=1, keepdims=True), (16, LANES)) * unit
                two = jnp.broadcast_to(jnp.sum(two, axis=1, keepdims=True), (16, LANES)) * unit
                mean, factor, scale, thr, gain, ratio = [stat_ref[n, chan, :] for n in range(6)]
                slope = factor * factor * (scale * two - one * (ratio * gain))
                col_ref[0, chan, :] = factor * gain * (0.25 * grad_factor)
                col_ref[1, chan, :] = slope
                col_ref[2, chan, :] = slope * mean - factor * (gain * one)

            wide = 2 * tile
            for t in range(plan.lanes // wide):
                at = t * wide
                y = mm(wl_ref[...], cols_ref[:, at : at + wide])
                inner = []
                for odd in range(2):
                    for blk in range(blocks):
                        r0 = (odd * blocks + blk) * 64
                        chan = slice(blk * 16, (blk + 1) * 16)
                        thr_b, up_b, slope_b, off = stat_ref[3, chan, :], col_ref[0, chan, :], col_ref[1, chan, :], col_ref[2, chan, :]
                        ons = []
                        for half in range(wide // LANES):
                            gap = gap_ref[odd * D + blk * 16 : odd * D + (blk + 1) * 16, at + half * LANES : at + (half + 1) * LANES]
                            ons.append(up_b * gap + off)
                        for p in range(4):
                            both = []
                            for half in range(wide // LANES):
                                yp = y[r0 + p * 16 : r0 + (p + 1) * 16, half * LANES : (half + 1) * LANES]
                                both.append((jnp.where(yp > thr_b, ons[half], off) - slope_b * yp).astype(bf16))
                            inner.append(jnp.concatenate(both, axis=1))
                dcols_ref[:, at : at + wide] = mm(wlt_ref[...], jnp.concatenate(inner, axis=0))

            shifts = []
            for s in range(4):
                shifts.append(
                    jnp.concatenate(
                        [
                            dcols_ref[
                                (s * plan.channels + c) * SLOTS : (s * plan.channels + c + 1) * SLOTS,
                                pair * LANES : (pair + 1) * LANES,
                            ]
                            for c in range(plan.channels)
                            for pair in range(plan.pairs)
                        ],
                        axis=0,
                    )
                )
            high, low = split_two(jnp.concatenate(shifts, axis=1))
            back = (((1,), (1,)), ((), ()))
            pcol = pcol_ref[...]
            wide = lax.dot_general(high, pcol, back, preferred_element_type=f32) + lax.dot_general(
                low, pcol, back, preferred_element_type=f32
            )
            tall = jnp.concatenate(
                [
                    jnp.concatenate(
                        [
                            wide[c * plan.span : (c + 1) * plan.span, half * plan.width : (half + 1) * plan.width]
                            for c in range(plan.channels)
                        ],
                        axis=1,
                    )
                    for half in range(plan.halves)
                ],
                axis=0,
            )
            high, low = split_two(tall)
            prow = prow_ref[...].T
            image = mm(prow, high) + mm(prow, low)
            for c in range(plan.channels):
                grad_ref[c] = image[:, c * plan.width : (c + 1) * plan.width]

        if i == 0:
            for copy in moments:
                copy.wait()
        for c in range(plan.channels):
            grad = grad_ref[c]
            first_new = beta_one * first_ref[i, c] + (1.0 - beta_one) * grad
            second_new = beta_two * second_ref[i, c] + (1.0 - beta_two) * grad * grad
            corrected = first_new / (1.0 - beta_one**adam_step)
            scale_hat = jnp.sqrt(second_new / (1.0 - beta_two**adam_step))
            new_syn_ref[i, c] = syn_ref[i, c] - learn_rate * corrected / (scale_hat + adam_eps)
            new_first_ref[i, c] = first_new
            new_second_ref[i, c] = second_new


def gather_params(conv_weight, norm_gain, norm_bias, taps_pad):
    taps, width = conv_weight.shape
    own = jnp.concatenate(
        [
            conv_weight,
            jnp.zeros((taps_pad - taps, width), conv_weight.dtype),
            norm_gain[None],
            norm_bias[None],
            jnp.zeros((14, width), conv_weight.dtype),
        ],
        axis=0,
    )
    if lax.axis_size("cls") == 2:
        other = lax.ppermute(own, "cls", [(0, 1), (1, 0)])
        low = lax.axis_index("cls") == 0
        return jnp.concatenate([jnp.where(low, own, other), jnp.where(low, other, own)], axis=1)
    return lax.all_gather(own, "cls", axis=1, tiled=True)


class Exchange:
    def __init__(self):
        self.n = lax.axis_size("wide")
        self.pos = lax.axis_index("wide")
        steps = []
        while 1 << (len(steps) + 1) <= self.n:
            steps.append(1 << len(steps))
        self.first, rest = steps[0], steps[1:]
        self.masks = [(self.first, self.first)] + list(zip(rest, rest[1:] + rest[:1]))

    def swap(self, x, masks):
        return lax.ppermute(x, "wide", [(i, i ^ masks[i & self.first]) for i in range(self.n)])

    def high(self, masks):
        return (self.pos & jnp.where((self.pos & self.first) > 0, masks[1], masks[0])) > 0

    def add(self, own, masks):
        high = self.high(masks)
        rows = own.shape[0] // 2
        kept = jnp.where(high, own[rows:], own[:rows])
        sent = jnp.where(high, own[:rows], own[rows:]).astype(jnp.float16)
        return kept, sent

    def join(self, own, other, masks):
        high = self.high(masks)
        return jnp.concatenate([jnp.where(high, other, own), jnp.where(high, own, other)], axis=0)


def exchange_sum(part, where, middle, n_own):
    ex = Exchange()
    halved = ex.masks[:2]
    whole = ex.masks[2:]
    rounds = [(m, "halve") for m in halved] + [(m, "whole") for m in whole] + [(m, "join") for m in reversed(halved)]
    at_round = [1 + (len(rounds) - 3) * i // max(n_own - 1, 1) for i in range(n_own)]
    own, made = part, []
    for n, (masks, kind) in enumerate(rounds):
        if kind == "halve":
            own, sent = ex.add(own, masks)
        else:
            sent = own.astype(jnp.float16)
        todo = [i for i in range(n_own) if at_round[i] == n]
        if todo:
            sent, held = lax.optimization_barrier((sent, where))
        got = ex.swap(sent, masks)
        if todo:
            new = [middle(i, held) for i in todo]
            if n + 1 < len(rounds):
                got, new = lax.optimization_barrier((got, new))
            made += new
        own = ex.join(sent, got, masks) if kind == "join" else own + got.astype(f32)
    return own.astype(f32), made


def body(
    syn_images, adam_first, adam_second, real_pool, real_pick, real_count, syn_order,
    conv_weight, norm_gain, norm_bias,
):
    _, n_own, channels, height, width = syn_images.shape
    batch = syn_order.shape[1] // 2
    depth = conv_weight.shape[1] * lax.axis_size("cls")
    plan = Plan(channels, height, width, depth)
    prow = jnp.asarray(plan.pick_rows(), bf16)
    pcol = jnp.asarray(plan.pick_cols(), bf16)
    ptap = jnp.asarray(plan.pick_taps(), bf16)
    n_pool = real_pool.shape[1]
    sent = jnp.stack(
        [lax.dynamic_index_in_dim(real_pool[0], real_pick[0, 0, n], 0, False) for n in range(n_pool - n_pool // 4, n_pool)]
    )
    got = lax.ppermute(sent, "wide", [(i, i ^ 1) for i in range(lax.axis_size("wide"))])
    params = gather_params(conv_weight, norm_gain, norm_bias, plan.taps_pad)
    where = lax.axis_index("wide").astype(jnp.int32)[None]

    smem = pl.BlockSpec(memory_space=pltpu.SMEM)
    vmem = pl.BlockSpec(memory_space=pltpu.VMEM)
    shape = jax.ShapeDtypeStruct
    rows = 2 * depth
    m_rows = plan.groups * depth
    weights = [
        pltpu.VMEM((channels * plan.tall, 4 * LANES), f32),
        pltpu.VMEM((depth, 3 * plan.deep), bf16),
        pltpu.VMEM((depth, plan.deep), f32),
        pltpu.VMEM((2 + channels, depth, LANES), f32),
    ]

    def within(mib):
        return pltpu.CompilerParams(vmem_limit_bytes=mib << 20)

    hbm = pl.BlockSpec(memory_space=pltpu.HBM)
    part, wl = pl.pallas_call(
        functools.partial(forward_kernel, plan, n_own, batch),
        in_specs=[smem] + [hbm] * 8 + [vmem],
        out_specs=[vmem] * 2,
        out_shape=[shape((rows, plan.lanes), f32), shape((m_rows, plan.deep), bf16)],
        scratch_shapes=[
            pltpu.VMEM((n_pool + sent.shape[0] + n_own, channels, height, width), bf16),
            *weights,
            pltpu.VMEM((plan.deep, plan.lanes), bf16),
            pltpu.VMEM((plan.used, plan.lanes), bf16),
            *[pltpu.VMEM((depth, LANES), f32)] * 2,
            pltpu.SMEM(real_pick.shape, jnp.int32),
            pltpu.SMEM(real_count.shape, jnp.int32),
            pltpu.SMEM(syn_order.shape, jnp.int32),
            pltpu.VMEM(syn_images.shape[1:], f32),
            pltpu.VMEM(pcol.shape, bf16),
            pltpu.VMEM(ptap.shape, bf16),
            pltpu.SemaphoreType.DMA((8,)),
        ],
        compiler_params=within(60),
        name="embed_sums",
    )(where, real_pick, real_count, syn_order, real_pool[0], got, syn_images[0], pcol, ptap, params)

    def middle(own, held):
        return pl.pallas_call(
            functools.partial(middle_kernel, plan, n_own, batch, own),
            in_specs=[smem] * 2 + [vmem] * 4,
            out_specs=[vmem] * 4,
            out_shape=[
                shape((plan.deep, plan.lanes), bf16),
                shape((rows, plan.lanes), f32),
                shape((rows, plan.lanes), f32),
                shape((6, depth, LANES), f32),
            ],
            scratch_shapes=[pltpu.VMEM((m_rows, plan.deep), bf16), *weights],
            compiler_params=within(18),
            name="syn_features",
        )(held, syn_order, syn_images[0], pcol, ptap, params)

    gap, made = exchange_sum(part, where, middle, n_own)

    img = shape((n_own, channels, height, width), f32)
    outs = pl.pallas_call(
        functools.partial(backward_kernel, plan, n_own, batch),
        in_specs=[smem] * 2 + [vmem] * (5 + 4 * n_own) + [hbm] * 2,
        out_specs=[vmem] * 3,
        out_shape=[img] * 3,
        scratch_shapes=[
            pltpu.VMEM((channels, height, width), f32),
            pltpu.VMEM((plan.used, plan.lanes), f32),
            pltpu.VMEM((3, depth, LANES), f32),
            pltpu.VMEM((plan.used, m_rows), bf16),
            pltpu.VMEM(img.shape, f32),
            pltpu.VMEM(img.shape, f32),
            pltpu.SemaphoreType.DMA((2,)),
        ],
        compiler_params=within(24),
        name="image_grads",
    )(
        where, syn_order, gap, *[x for one in made for x in one], wl, prow, pcol,
        syn_images[0], adam_first[0], adam_second[0],
    )
    return tuple(out[None] for out in outs)


def solution(mesh):
    image = P("cls", "wide", None, None, None)
    return jax.shard_map(
        body,
        mesh=mesh,
        in_specs=(
            image, image, image, image, P("cls", "wide", None), P("cls", None), P("cls", None),
            P(None, "cls"), P("cls"), P("cls"),
        ),
        out_specs=(image, image, image),
        check_vma=False,
    )
```

```python
import functools

import jax
import jax.numpy as jnp
import numpy as np
from jax import lax
from jax.experimental import pallas as pl
from jax.experimental.pallas import tpu as pltpu
from jax.sharding import PartitionSpec as P

beta_one = 0.9
beta_two = 0.99
adam_step = 10.0
learn_rate = 0.1
adam_eps = 1e-08
loss_scale = 512.0
norm_eps = 1e-05

LANES = 128
SLOTS = 8
f32 = jnp.float32
bf16 = jnp.bfloat16


def mm(a, b):
    return lax.dot_general(a, b, (((1,), (0,)), ((), ())), preferred_element_type=f32)


class Plan:
    def __init__(self, channels, height, width, depth):
        self.channels, self.height, self.width, self.depth = channels, height, width, depth
        self.cols = width // 2
        self.halves = LANES // self.cols
        self.rows = height // self.halves
        self.pairs = self.rows // 4
        self.tall = self.rows + 16
        self.span = self.pairs * SLOTS
        self.lanes = self.pairs * LANES
        self.taps = 9 * channels
        self.taps_pad = -(-self.taps // 32) * 32
        self.used = 4 * channels * SLOTS
        self.deep = -(-self.used // LANES) * LANES
        self.groups = 8
        self.pixels = height * width

    def pick_rows(self):
        out = np.zeros((self.halves, self.pairs, SLOTS, self.height), np.float32)
        for half in range(self.halves):
            for pair in range(self.pairs):
                for slot in range(6):
                    row = half * self.rows + 4 * pair + slot - 1
                    if 0 <= row < self.height:
                        out[half, pair, slot, row] = 1.0
        return out.reshape(self.halves * self.span, self.height)

    def pick_cols(self):
        out = np.zeros((self.halves, self.width, 4, self.halves, self.cols), np.float32)
        for shift in range(4):
            for col in range(self.cols):
                src = 2 * col + shift - 1
                if 0 <= src < self.width:
                    for half in range(self.halves):
                        out[half, src, shift, half, col] = 1.0
        return out.reshape(self.halves * self.width, 4 * LANES)

    def pick_taps(self):
        out = np.zeros((2, 2, 2, self.deep, self.taps_pad), np.float32)
        for odd in range(2):
            for a in range(2):
                for b in range(2):
                    for i in range(3):
                        for j in range(3):
                            for c in range(self.channels):
                                k = ((b + j) * self.channels + c) * SLOTS + 2 * odd + a + i
                                out[odd, a, b, k, (i * 3 + j) * self.channels + c] = 1.0
        return out.reshape(self.groups * self.deep, self.taps_pad)


def spread(row):
    return jnp.broadcast_to(row, (LANES, row.shape[1])).T


def split_two(x):
    high = x.astype(bf16)
    return high, (x - high.astype(f32)).astype(bf16)


class Prepare:
    def __init__(self, plan, planes, pcol, rows_ref, deep_ref, sums_ref, chan_ref):
        self.plan, self.planes, self.pcol, self.rows_ref = plan, planes, pcol, rows_ref
        self.deep_ref, self.sums_ref, self.chan_ref = deep_ref, sums_ref, chan_ref

    def stages(self, cols_ref):
        plan = self.plan
        D, KU, KP, C, tall = plan.depth, plan.used, plan.deep, plan.channels, plan.tall
        shifts, blocks = [], []
        for plane in self.planes:
            rows = plane.astype(f32)
            total = functools.reduce(lambda a, b: a + b, [rows[r : r + 8] for r in range(0, plan.height, 8)])
            total = jnp.sum(jnp.sum(total, axis=1, keepdims=True), axis=0, keepdims=True)
            shifts.append(jnp.round(total * (4.0 / plan.pixels)) * 0.25)
            rows = jnp.concatenate([jnp.zeros((1, plan.width), f32), rows, jnp.zeros((15, plan.width), f32)], axis=0)
            blocks.append(
                jnp.concatenate([rows[h * plan.rows : h * plan.rows + tall] for h in range(plan.halves)], axis=1).astype(bf16)
            )
        yield
        self.rows_ref[...] = mm(jnp.concatenate(blocks, axis=0), self.pcol)
        yield
        tail = jnp.ones((KP - KU, LANES), bf16)
        gram = None
        for half in range(2):
            lean = []
            for pair in range(half * plan.pairs // 2, (half + 1) * plan.pairs // 2):
                parts = [
                    (c, self.rows_ref[c * tall + 4 * pair : c * tall + 4 * pair + SLOTS, s * LANES : (s + 1) * LANES])
                    for s in range(4)
                    for c in range(C)
                ]
                cols_ref[0:KU, pair * LANES : (pair + 1) * LANES] = jnp.concatenate([x for _, x in parts], axis=0).astype(bf16)
                own = jnp.concatenate([x - shifts[c] for c, x in parts], axis=0).astype(bf16)
                lean.append(jnp.concatenate([own, tail], axis=0))
            yield
            lean = jnp.concatenate(lean, axis=1)
            part = lax.dot_general(lean, lean, (((1,), (1,)), ((), ())), preferred_element_type=f32)
            gram = part if gram is None else gram + part
            yield
        moved = gram
        for step in (1, 2, C * SLOTS):
            moved = moved + pltpu.roll(pltpu.roll(moved, KP - step, 0), KP - step, 1)
        high = moved.astype(bf16)
        rest = moved - high.astype(f32)
        mid = rest.astype(bf16)
        low = (rest - mid.astype(f32)).astype(bf16)
        quad = mm(self.deep_ref[...], jnp.concatenate([high, mid, low], axis=0))
        yield
        first = self.deep_ref[:, 0:KP].astype(f32)
        second = jnp.sum(quad * first, axis=1, keepdims=True) * (1.0 / plan.pixels)
        off = jnp.sum(self.sums_ref[...] * gram[KU : KU + 1, :], axis=1, keepdims=True) * (1.0 / plan.pixels)
        second = jnp.broadcast_to(second, (D, LANES))
        off = jnp.broadcast_to(off, (D, LANES))
        mean = off
        for c in range(C):
            mean = mean + shifts[c] * self.chan_ref[2 + c]
        var = jnp.maximum(second - off * off, 0.0) + norm_eps
        self.factor = lax.rsqrt(var)
        self.scale = self.chan_ref[0] * self.factor
        self.mean = mean
        self.thr = mean - self.chan_ref[1] * (var * self.factor)
        yield


def is_chosen(order_ref, batch, gid):
    return lax.fori_loop(0, batch, lambda j, t: t | (order_ref[0, j] == gid).astype(jnp.int32), jnp.int32(0))


def make_weights(plan, param_ref, ptap_ref, wl_ref, deep_ref, sums_ref, chan_ref):
    D, KP, C = plan.depth, plan.deep, plan.channels
    spread_taps = mm(ptap_ref[...], param_ref[0 : plan.taps_pad, :])
    sums = None
    for g in range(plan.groups):
        odd, phase = divmod(g, 4)
        turned = spread_taps[g * KP : (g + 1) * KP, :].T
        sums = turned if sums is None else sums + turned
        turned = turned.astype(bf16)
        if g == 0:
            for n in range(3):
                deep_ref[:, n * KP : (n + 1) * KP] = turned
        for blk in range(D // 16):
            at = ((odd * (D // 16) + blk) * 4 + phase) * 16
            rows = turned[blk * 16 : (blk + 1) * 16, :]
            wl_ref[at : at + 16, :] = rows
    sums_ref[...] = sums
    gain = param_ref[plan.taps_pad : plan.taps_pad + 1, :].astype(f32)
    bias = param_ref[plan.taps_pad + 1 : plan.taps_pad + 2, :].astype(f32)
    chan_ref[0] = spread(gain)
    chan_ref[1] = spread(bias / gain)
    first = spread_taps[0:KP, :]
    for c in range(C):
        total = functools.reduce(lambda a, b: a + b, [first[(s * C + c) * SLOTS : (s * C + c + 1) * SLOTS] for s in range(4)])
        chan_ref[2 + c] = spread(jnp.sum(total, axis=0, keepdims=True))


def forward_kernel(
    plan, n_own, batch, where_ref, pick_hbm, count_hbm, order_hbm,
    pool_hbm, sent_hbm, syn_hbm, pcol_hbm, ptap_hbm, param_ref,
    part_ref,
    all_ref, wl_ref, rows_ref, deep_ref, sums_ref, chan_ref, now_ref, next_ref, thr_ref, coef_ref,
    pick_ref, count_ref, order_ref, syn_ref, pcol_ref, ptap_ref, sems,
):
    D, KP, KU, C = plan.depth, plan.deep, plan.used, plan.channels
    n_pool, n_sent = pool_hbm.shape[0], sent_hbm.shape[0]
    copies = [
        pltpu.make_async_copy(src, dst, sems.at[n])
        for n, (src, dst) in enumerate(
            (
                (ptap_hbm, ptap_ref),
                (pick_hbm, pick_ref),
                (count_hbm, count_ref),
                (order_hbm, order_ref),
                (pcol_hbm, pcol_ref),
                (syn_hbm, syn_ref),
                (pool_hbm, all_ref.at[pl.ds(0, n_pool)]),
                (sent_hbm, all_ref.at[pl.ds(n_pool, n_sent)]),
            )
        )
    ]
    for copy in copies:
        copy.start()
    part_ref[...] = jnp.zeros_like(part_ref)
    if KP > KU:
        now_ref[KU:KP, :] = jnp.zeros((KP - KU, plan.lanes), bf16)
    copies[0].wait()
    make_weights(plan, param_ref, ptap_ref, wl_ref, deep_ref, sums_ref, chan_ref)
    for copy in copies[1:]:
        copy.wait()

    pos = where_ref[0]
    mate_count = count_ref[0, pos ^ 1]
    own_count = count_ref[0, pos]
    full = own_count == n_pool
    own_count = own_count - jnp.where(full, n_sent, 0)
    mate_count = jnp.where(mate_count == n_pool, n_sent, 0)
    total = lax.fori_loop(0, count_ref.shape[1], lambda i, t: t + count_ref[0, i], jnp.int32(0)).astype(f32)
    flags = [is_chosen(order_ref, batch, pos * n_own + i) for i in range(n_own)]
    n_syn = functools.reduce(lambda a, b: a + b, flags)
    n_real = n_pool + n_sent
    for i in range(n_own):
        all_ref[n_real + i] = syn_ref[i].astype(bf16)

    def image_of(i):
        syn_at = jnp.int32(n_real + n_own - 1)
        before = n_syn
        for s in reversed(range(n_own)):
            before = before - flags[s]
            syn_at = jnp.where((flags[s] > 0) & (i == before), n_real + s, syn_at)
        own_at = jnp.clip(i - n_syn, 0, n_pool - 1)
        own_at = jnp.where(full, own_at, pick_ref[0, 0, own_at])
        sent_at = n_pool + jnp.clip(i - n_syn - own_count, 0, n_sent - 1)
        real_at = jnp.where(i - n_syn < own_count, own_at, sent_at)
        return jnp.where(i < n_syn, syn_at, real_at), jnp.where(i < n_syn, 0.25 / batch, -0.25 / total)

    def begin(i):
        at, weight = image_of(i)
        planes = [all_ref[at, c] for c in range(C)]
        return Prepare(plan, planes, pcol_ref[...], rows_ref, deep_ref, sums_ref, chan_ref), weight

    prep, weight = begin(jnp.int32(0))
    for _ in prep.stages(now_ref):
        pass
    thr_ref[...] = prep.thr
    coef_ref[...] = prep.scale * weight
    tile = 2 * LANES

    def step(i, base):
        prep, weight = begin(i + 1)
        ahead = prep.stages(next_ref)
        base = base + coef_ref[...] * thr_ref[...]
        wide = 2 * tile
        for t in range(plan.lanes // wide):
            at = t * wide
            y = mm(wl_ref[...], now_ref[:, at : at + wide])
            for _ in range((3, 3, 2, 0)[min(t, 3)]):
                next(ahead, None)
            for odd in range(2):
                for blk in range(D // 16):
                    r0 = (odd * (D // 16) + blk) * 64
                    thr = thr_ref[blk * 16 : (blk + 1) * 16, :]
                    coef = coef_ref[blk * 16 : (blk + 1) * 16, :]
                    out = slice(odd * D + blk * 16, odd * D + (blk + 1) * 16)
                    for half in range(wide // LANES):
                        lanes = slice(half * LANES, (half + 1) * LANES)
                        ys = [jnp.maximum(y[r0 + p * 16 : r0 + (p + 1) * 16, lanes], thr) for p in range(4)]
                        here = slice(at + half * LANES, at + (half + 1) * LANES)
                        part_ref[out, here] += coef * ((ys[0] + ys[1]) + (ys[2] + ys[3]))
        for _ in ahead:
            pass
        now_ref[0:KU, :] = next_ref[0:KU, :]
        thr_ref[...] = prep.thr
        coef_ref[...] = prep.scale * weight
        return base

    base = lax.fori_loop(0, n_syn + own_count + mate_count, step, jnp.zeros((D, LANES), f32))
    base = 4.0 * base
    for pair in range(plan.pairs):
        for odd in range(2):
            part_ref[odd * D : (odd + 1) * D, pair * LANES : (pair + 1) * LANES] -= base


def middle_kernel(
    plan, n_own, batch, own, where_ref, order_ref, syn_ref, first_ref, second_ref, pcol_ref, ptap_ref, param_ref,
    cols_ref, vsum_ref, hits_ref, stat_ref, wl_ref, wlt_ref, decay_ref,
    rows_ref, deep_ref, sums_ref, chan_ref,
):
    D, KP, KU, C = plan.depth, plan.deep, plan.used, plan.channels
    flag = is_chosen(order_ref, batch, where_ref[0] * n_own + own)
    tile = 2 * LANES
    decay_ref[0] = beta_one * first_ref[own]
    decay_ref[1] = beta_two * second_ref[own]

    @pl.when(flag > 0)
    def _():
        make_weights(plan, param_ref, ptap_ref, wl_ref, deep_ref, sums_ref, chan_ref)
        for g in range(plan.groups):
            wlt_ref[:, g * D : (g + 1) * D] = wl_ref[g * D : (g + 1) * D, :].astype(f32).T.astype(bf16)[0:KU, :]
        if KP > KU:
            cols_ref[KU:KP, :] = jnp.zeros((KP - KU, plan.lanes), bf16)
        planes = [syn_ref[own, c].astype(bf16) for c in range(C)]
        prep = Prepare(plan, planes, pcol_ref[...], rows_ref, deep_ref, sums_ref, chan_ref)
        for _ in prep.stages(cols_ref):
            pass
        for n, value in enumerate((prep.mean, prep.factor, prep.scale, prep.thr, chan_ref[0], chan_ref[1])):
            stat_ref[n] = value

        for t in range(plan.lanes // tile):
            at = t * tile
            y = mm(wl_ref[...], cols_ref[:, at : at + tile])
            for odd in range(2):
                for blk in range(D // 16):
                    r0 = (odd * (D // 16) + blk) * 64
                    thr = stat_ref[3, blk * 16 : (blk + 1) * 16, :]
                    out = slice(odd * D + blk * 16, odd * D + (blk + 1) * 16)
                    for half in range(2):
                        lanes = slice(half * LANES, (half + 1) * LANES)
                        yp = [y[r0 + p * 16 : r0 + (p + 1) * 16, lanes] for p in range(4)]
                        ys = [jnp.maximum(a, thr) for a in yp]
                        hs = [jnp.where(a > thr, 1.0, 0.0) for a in yp]
                        here = slice(at + half * LANES, at + (half + 1) * LANES)
                        vsum_ref[out, here] = ((ys[0] + ys[1]) + (ys[2] + ys[3])) - 4.0 * thr
                        hits_ref[out, here] = (hs[0] + hs[1]) + (hs[2] + hs[3])


def backward_kernel(
    plan, n_own, batch, where_ref, order_ref, *refs,
):
    D, KU, blocks = plan.depth, plan.used, plan.depth // 16
    gap_ref = refs[0]
    owns = [refs[1 + 7 * i : 8 + 7 * i] for i in range(n_own)]
    (
        prow_ref, pcol_ref, syn_ref, new_syn_ref, new_first_ref, new_second_ref,
        grad_ref, dcols_ref, col_ref,
    ) = refs[1 + 7 * n_own :]
    pos = where_ref[0]
    tile = 2 * LANES
    grad_factor = 2.0 * loss_scale / batch

    for i in range(n_own):
        cols_ref, vsum_ref, hits_ref, stat_ref, wl_ref, wlt_ref, decay_ref = owns[i]
        flag = is_chosen(order_ref, batch, pos * n_own + i)

        @pl.when(flag == 0)
        def _():
            grad_ref[...] = jnp.zeros_like(grad_ref)

        @pl.when(flag > 0)
        def _():
            unit = grad_factor / (4.0 * plan.pixels)
            for blk in range(blocks):
                chan = slice(blk * 16, (blk + 1) * 16)
                one = two = jnp.zeros((16, LANES), f32)
                for pair in range(plan.pairs):
                    here = slice(pair * LANES, (pair + 1) * LANES)
                    for odd in range(2):
                        rows = slice(odd * D + blk * 16, odd * D + (blk + 1) * 16)
                        gap = gap_ref[rows, here]
                        one = one + gap * hits_ref[rows, here]
                        two = two + gap * vsum_ref[rows, here]
                one = jnp.broadcast_to(jnp.sum(one, axis=1, keepdims=True), (16, LANES)) * unit
                two = jnp.broadcast_to(jnp.sum(two, axis=1, keepdims=True), (16, LANES)) * unit
                mean, factor, scale, thr, gain, ratio = [stat_ref[n, chan, :] for n in range(6)]
                slope = factor * factor * (scale * two - one * (ratio * gain))
                col_ref[0, chan, :] = factor * gain * (0.25 * grad_factor)
                col_ref[1, chan, :] = slope
                col_ref[2, chan, :] = slope * mean - factor * (gain * one)

            wide = 2 * tile
            for t in range(plan.lanes // wide):
                at = t * wide
                y = mm(wl_ref[...], cols_ref[:, at : at + wide])
                inner = []
                for odd in range(2):
                    for blk in range(blocks):
                        r0 = (odd * blocks + blk) * 64
                        chan = slice(blk * 16, (blk + 1) * 16)
                        thr_b, up_b, slope_b, off = stat_ref[3, chan, :], col_ref[0, chan, :], col_ref[1, chan, :], col_ref[2, chan, :]
                        ons = []
                        for half in range(wide // LANES):
                            gap = gap_ref[odd * D + blk * 16 : odd * D + (blk + 1) * 16, at + half * LANES : at + (half + 1) * LANES]
                            ons.append(up_b * gap + off)
                        for p in range(4):
                            both = []
                            for half in range(wide // LANES):
                                yp = y[r0 + p * 16 : r0 + (p + 1) * 16, half * LANES : (half + 1) * LANES]
                                both.append((jnp.where(yp > thr_b, ons[half], off) - slope_b * yp).astype(bf16))
                            inner.append(jnp.concatenate(both, axis=1))
                dcols_ref[:, at : at + wide] = mm(wlt_ref[...], jnp.concatenate(inner, axis=0))

            shifts = []
            for s in range(4):
                shifts.append(
                    jnp.concatenate(
                        [
                            dcols_ref[
                                (s * plan.channels + c) * SLOTS : (s * plan.channels + c + 1) * SLOTS,
                                pair * LANES : (pair + 1) * LANES,
                            ]
                            for c in range(plan.channels)
                            for pair in range(plan.pairs)
                        ],
                        axis=0,
                    )
                )
            high, low = split_two(jnp.concatenate(shifts, axis=1))
            back = (((1,), (1,)), ((), ()))
            pcol = pcol_ref[...]
            wide = lax.dot_general(high, pcol, back, preferred_element_type=f32) + lax.dot_general(
                low, pcol, back, preferred_element_type=f32
            )
            tall = jnp.concatenate(
                [
                    jnp.concatenate(
                        [
                            wide[c * plan.span : (c + 1) * plan.span, half * plan.width : (half + 1) * plan.width]
                            for c in range(plan.channels)
                        ],
                        axis=1,
                    )
                    for half in range(plan.halves)
                ],
                axis=0,
            )
            high, low = split_two(tall)
            prow = prow_ref[...].T
            image = mm(prow, high) + mm(prow, low)
            for c in range(plan.channels):
                grad_ref[c] = image[:, c * plan.width : (c + 1) * plan.width]

        for c in range(plan.channels):
            grad = grad_ref[c]
            first_new = decay_ref[0, c] + (1.0 - beta_one) * grad
            second_new = decay_ref[1, c] + (1.0 - beta_two) * grad * grad
            corrected = first_new / (1.0 - beta_one**adam_step)
            scale_hat = jnp.sqrt(second_new / (1.0 - beta_two**adam_step))
            new_syn_ref[i, c] = syn_ref[i, c] - learn_rate * corrected / (scale_hat + adam_eps)
            new_first_ref[i, c] = first_new
            new_second_ref[i, c] = second_new


def gather_params(conv_weight, norm_gain, norm_bias, taps_pad):
    taps = conv_weight.shape[0]
    tall = taps_pad + 16
    own = (
        jnp.pad(conv_weight, ((0, tall - taps), (0, 0)))
        + jnp.pad(norm_gain[None], ((taps_pad, tall - taps_pad - 1), (0, 0)))
        + jnp.pad(norm_bias[None], ((taps_pad + 1, tall - taps_pad - 2), (0, 0)))
    )
    if lax.axis_size("cls") == 2:
        other = lax.ppermute(own, "cls", [(0, 1), (1, 0)])
        low = lax.axis_index("cls") == 0
        return jnp.concatenate([jnp.where(low, own, other), jnp.where(low, other, own)], axis=1)
    return lax.all_gather(own, "cls", axis=1, tiled=True)


class Exchange:
    def __init__(self):
        self.n = lax.axis_size("wide")
        self.pos = lax.axis_index("wide")
        steps = []
        while 1 << (len(steps) + 1) <= self.n:
            steps.append(1 << len(steps))
        self.first, rest = steps[0], steps[1:]
        self.masks = [(self.first, self.first)] + list(zip(rest, rest[1:] + rest[:1]))

    def swap(self, x, masks):
        return lax.ppermute(x, "wide", [(i, i ^ masks[i & self.first]) for i in range(self.n)])

    def high(self, masks):
        return (self.pos & jnp.where((self.pos & self.first) > 0, masks[1], masks[0])) > 0

    def add(self, own, masks):
        high = self.high(masks)
        rows = own.shape[0] // 2
        kept = jnp.where(high, own[rows:], own[:rows])
        sent = jnp.where(high, own[:rows], own[rows:]).astype(jnp.float16)
        return kept, sent

    def join(self, own, other, masks):
        high = self.high(masks)
        return jnp.concatenate([jnp.where(high, other, own), jnp.where(high, own, other)], axis=0)


def exchange_sum(part, where, middle, n_own):
    ex = Exchange()
    halved = ex.masks[:2]
    whole = ex.masks[2:]
    rounds = [(m, "halve") for m in halved] + [(m, "whole") for m in whole] + [(m, "join") for m in reversed(halved)]
    at_round = [1 + (len(rounds) - 3) * i // max(n_own - 1, 1) for i in range(n_own)]
    own, made = part, []
    for n, (masks, kind) in enumerate(rounds):
        if kind == "halve":
            own, sent = ex.add(own, masks)
        else:
            sent = own.astype(jnp.float16)
        todo = [i for i in range(n_own) if at_round[i] == n]
        if todo:
            sent, held = lax.optimization_barrier((sent, where))
        got = ex.swap(sent, masks)
        if todo:
            new = [middle(i, held) for i in todo]
            if n + 1 < len(rounds):
                got, new = lax.optimization_barrier((got, new))
            made += new
        own = ex.join(sent, got, masks) if kind == "join" else own + got.astype(f32)
    return own.astype(f32), made


def body(
    syn_images, adam_first, adam_second, real_pool, real_pick, real_count, syn_order,
    conv_weight, norm_gain, norm_bias,
):
    _, n_own, channels, height, width = syn_images.shape
    batch = syn_order.shape[1] // 2
    depth = conv_weight.shape[1] * lax.axis_size("cls")
    plan = Plan(channels, height, width, depth)
    prow = jnp.asarray(plan.pick_rows(), bf16)
    pcol = jnp.asarray(plan.pick_cols(), bf16)
    ptap = jnp.asarray(plan.pick_taps(), bf16)
    n_pool = real_pool.shape[1]
    sent = real_pool[0, n_pool - n_pool // 4 :]
    got = lax.ppermute(sent, "wide", [(i, i ^ 1) for i in range(lax.axis_size("wide"))])
    params = gather_params(conv_weight, norm_gain, norm_bias, plan.taps_pad)
    where = lax.axis_index("wide").astype(jnp.int32)[None]

    smem = pl.BlockSpec(memory_space=pltpu.SMEM)
    vmem = pl.BlockSpec(memory_space=pltpu.VMEM)
    shape = jax.ShapeDtypeStruct
    rows = 2 * depth
    m_rows = plan.groups * depth
    weights = [
        pltpu.VMEM((channels * plan.tall, 4 * LANES), f32),
        pltpu.VMEM((depth, 3 * plan.deep), bf16),
        pltpu.VMEM((depth, plan.deep), f32),
        pltpu.VMEM((2 + channels, depth, LANES), f32),
    ]

    def within(mib):
        return pltpu.CompilerParams(vmem_limit_bytes=mib << 20)

    hbm = pl.BlockSpec(memory_space=pltpu.HBM)
    part = pl.pallas_call(
        functools.partial(forward_kernel, plan, n_own, batch),
        in_specs=[smem] + [hbm] * 4 + [pl.BlockSpec(memory_space=pl.ANY)] + [hbm] * 3 + [vmem],
        out_specs=vmem,
        out_shape=shape((rows, plan.lanes), f32),
        scratch_shapes=[
            pltpu.VMEM((n_pool + sent.shape[0] + n_own, channels, height, width), bf16),
            pltpu.VMEM((m_rows, plan.deep), bf16),
            *weights,
            pltpu.VMEM((plan.deep, plan.lanes), bf16),
            pltpu.VMEM((plan.used, plan.lanes), bf16),
            *[pltpu.VMEM((depth, LANES), f32)] * 2,
            pltpu.SMEM(real_pick.shape, jnp.int32),
            pltpu.SMEM(real_count.shape, jnp.int32),
            pltpu.SMEM(syn_order.shape, jnp.int32),
            pltpu.VMEM(syn_images.shape[1:], f32),
            pltpu.VMEM(pcol.shape, bf16),
            pltpu.VMEM(ptap.shape, bf16),
            pltpu.SemaphoreType.DMA((8,)),
        ],
        compiler_params=within(60),
        name="embed_sums",
    )(where, real_pick, real_count, syn_order, real_pool[0], got, syn_images[0], pcol, ptap, params)

    def middle(own, held):
        return pl.pallas_call(
            functools.partial(middle_kernel, plan, n_own, batch, own),
            in_specs=[smem] * 2 + [vmem] * 6,
            out_specs=[vmem] * 7,
            out_shape=[
                shape((plan.deep, plan.lanes), bf16),
                shape((rows, plan.lanes), f32),
                shape((rows, plan.lanes), f32),
                shape((6, depth, LANES), f32),
                shape((m_rows, plan.deep), bf16),
                shape((plan.used, m_rows), bf16),
                shape((2, channels, height, width), f32),
            ],
            scratch_shapes=weights,
            compiler_params=within(18),
            name="syn_features",
        )(held, syn_order, syn_images[0], adam_first[0], adam_second[0], pcol, ptap, params)

    gap, made = exchange_sum(part, where, middle, n_own)

    img = shape((n_own, channels, height, width), f32)
    outs = pl.pallas_call(
        functools.partial(backward_kernel, plan, n_own, batch),
        in_specs=[smem] * 2 + [vmem] * (4 + 7 * n_own),
        out_specs=[vmem] * 3,
        out_shape=[img] * 3,
        scratch_shapes=[
            pltpu.VMEM((channels, height, width), f32),
            pltpu.VMEM((plan.used, plan.lanes), f32),
            pltpu.VMEM((3, depth, LANES), f32),
        ],
        compiler_params=within(24),
        name="image_grads",
    )(
        where, syn_order, gap, *[x for one in made for x in one], prow, pcol, syn_images[0],
    )
    return tuple(out[None] for out in outs)


def solution(mesh):
    image = P("cls", "wide", None, None, None)
    return jax.shard_map(
        body,
        mesh=mesh,
        in_specs=(
            image, image, image, image, P("cls", "wide", None), P("cls", None), P("cls", None),
            P(None, "cls"), P("cls"), P("cls"),
        ),
        out_specs=(image, image, image),
        check_vma=False,
    )
```

```python
import functools

import jax
import jax.numpy as jnp
import numpy as np
from jax import lax
from jax.experimental import pallas as pl
from jax.experimental.pallas import tpu as pltpu
from jax.sharding import PartitionSpec as P

beta_one = 0.9
beta_two = 0.99
adam_step = 10.0
learn_rate = 0.1
adam_eps = 1e-08
loss_scale = 512.0
norm_eps = 1e-05

LANES = 128
SLOTS = 8
f32 = jnp.float32
bf16 = jnp.bfloat16


def mm(a, b):
    return lax.dot_general(a, b, (((1,), (0,)), ((), ())), preferred_element_type=f32)


class Plan:
    def __init__(self, channels, height, width, depth):
        self.channels, self.height, self.width, self.depth = channels, height, width, depth
        self.cols = width // 2
        self.halves = LANES // self.cols
        self.rows = height // self.halves
        self.pairs = self.rows // 4
        self.tall = self.rows + 16
        self.span = self.pairs * SLOTS
        self.lanes = self.pairs * LANES
        self.taps = 9 * channels
        self.taps_pad = -(-self.taps // 32) * 32
        self.used = 4 * channels * SLOTS
        self.deep = -(-self.used // LANES) * LANES
        self.groups = 8
        self.pixels = height * width

    def pick_cols(self):
        out = np.zeros((self.halves, self.width, 4, self.halves, self.cols), np.float32)
        for shift in range(4):
            for col in range(self.cols):
                src = 2 * col + shift - 1
                if 0 <= src < self.width:
                    for half in range(self.halves):
                        out[half, src, shift, half, col] = 1.0
        return out.reshape(self.halves * self.width, 4 * LANES)

    def pick_taps(self):
        out = np.zeros((2, 2, 2, self.deep, self.taps_pad), np.float32)
        for odd in range(2):
            for a in range(2):
                for b in range(2):
                    for i in range(3):
                        for j in range(3):
                            for c in range(self.channels):
                                k = ((b + j) * self.channels + c) * SLOTS + 2 * odd + a + i
                                out[odd, a, b, k, (i * 3 + j) * self.channels + c] = 1.0
        return out.reshape(self.groups * self.deep, self.taps_pad)


def spread(row):
    return jnp.broadcast_to(row, (LANES, row.shape[1])).T


def split_two(x):
    high = x.astype(bf16)
    return high, (x - high.astype(f32)).astype(bf16)


class Prepare:
    def __init__(self, plan, planes, pcol, rows_ref, deep_ref, sums_ref, chan_ref):
        self.plan, self.planes, self.pcol, self.rows_ref = plan, planes, pcol, rows_ref
        self.deep_ref, self.sums_ref, self.chan_ref = deep_ref, sums_ref, chan_ref

    def stages(self, cols_ref):
        plan = self.plan
        D, KU, KP, C, tall = plan.depth, plan.used, plan.deep, plan.channels, plan.tall
        shifts, blocks = [], []
        for plane in self.planes:
            rows = plane.astype(f32)
            total = functools.reduce(lambda a, b: a + b, [rows[r : r + 8] for r in range(0, plan.height, 8)])
            total = jnp.sum(jnp.sum(total, axis=1, keepdims=True), axis=0, keepdims=True)
            shifts.append(jnp.round(total * (4.0 / plan.pixels)) * 0.25)
            rows = jnp.concatenate([jnp.zeros((1, plan.width), f32), rows, jnp.zeros((15, plan.width), f32)], axis=0)
            blocks.append(
                jnp.concatenate([rows[h * plan.rows : h * plan.rows + tall] for h in range(plan.halves)], axis=1).astype(bf16)
            )
        yield
        self.rows_ref[...] = mm(jnp.concatenate(blocks, axis=0), self.pcol)
        yield
        tail = jnp.ones((KP - KU, LANES), bf16)
        gram = None
        for half in range(2):
            lean = []
            for pair in range(half * plan.pairs // 2, (half + 1) * plan.pairs // 2):
                parts = [
                    (c, self.rows_ref[c * tall + 4 * pair : c * tall + 4 * pair + SLOTS, s * LANES : (s + 1) * LANES])
                    for s in range(4)
                    for c in range(C)
                ]
                cols_ref[0:KU, pair * LANES : (pair + 1) * LANES] = jnp.concatenate([x for _, x in parts], axis=0).astype(bf16)
                own = jnp.concatenate([x - shifts[c] for c, x in parts], axis=0).astype(bf16)
                lean.append(jnp.concatenate([own, tail], axis=0))
            yield
            lean = jnp.concatenate(lean, axis=1)
            part = lax.dot_general(lean, lean, (((1,), (1,)), ((), ())), preferred_element_type=f32)
            gram = part if gram is None else gram + part
            yield
        moved = gram
        for step in (1, 2, C * SLOTS):
            moved = moved + pltpu.roll(pltpu.roll(moved, KP - step, 0), KP - step, 1)
        high = moved.astype(bf16)
        rest = moved - high.astype(f32)
        mid = rest.astype(bf16)
        low = (rest - mid.astype(f32)).astype(bf16)
        quad = mm(self.deep_ref[...], jnp.concatenate([high, mid, low], axis=0))
        yield
        first = self.deep_ref[:, 0:KP].astype(f32)
        second = jnp.sum(quad * first, axis=1, keepdims=True) * (1.0 / plan.pixels)
        off = jnp.sum(self.sums_ref[...] * gram[KU : KU + 1, :], axis=1, keepdims=True) * (1.0 / plan.pixels)
        second = jnp.broadcast_to(second, (D, LANES))
        off = jnp.broadcast_to(off, (D, LANES))
        mean = off
        for c in range(C):
            mean = mean + shifts[c] * self.chan_ref[2 + c]
        var = jnp.maximum(second - off * off, 0.0) + norm_eps
        self.factor = lax.rsqrt(var)
        self.scale = self.chan_ref[0] * self.factor
        self.mean = mean
        self.thr = mean - self.chan_ref[1] * (var * self.factor)
        yield


def join_params(low_ref, near_ref, far_ref, param_ref):
    near, far = near_ref[...].astype(f32), far_ref[...].astype(f32)
    low = low_ref[0] > 0
    param_ref[...] = jnp.concatenate([jnp.where(low, near, far), jnp.where(low, far, near)], axis=1).astype(bf16)


def is_chosen(order_ref, batch, gid):
    return lax.fori_loop(0, batch, lambda j, t: t | (order_ref[0, j] == gid).astype(jnp.int32), jnp.int32(0))


def make_weights(plan, param_ref, ptap_ref, wl_ref, deep_ref, sums_ref, chan_ref):
    D, KP, C = plan.depth, plan.deep, plan.channels
    spread_taps = mm(ptap_ref[...], param_ref[0 : plan.taps_pad, :])
    sums = None
    for g in range(plan.groups):
        odd, phase = divmod(g, 4)
        turned = spread_taps[g * KP : (g + 1) * KP, :].T
        sums = turned if sums is None else sums + turned
        turned = turned.astype(bf16)
        if g == 0:
            for n in range(3):
                deep_ref[:, n * KP : (n + 1) * KP] = turned
        for blk in range(D // 16):
            at = ((odd * (D // 16) + blk) * 4 + phase) * 16
            rows = turned[blk * 16 : (blk + 1) * 16, :]
            wl_ref[at : at + 16, :] = rows
    sums_ref[...] = sums
    gain = param_ref[plan.taps_pad : plan.taps_pad + 1, :].astype(f32)
    bias = param_ref[plan.taps_pad + 1 : plan.taps_pad + 2, :].astype(f32)
    chan_ref[0] = spread(gain)
    chan_ref[1] = spread(bias / gain)
    first = spread_taps[0:KP, :]
    for c in range(C):
        total = functools.reduce(lambda a, b: a + b, [first[(s * C + c) * SLOTS : (s * C + c + 1) * SLOTS] for s in range(4)])
        chan_ref[2 + c] = spread(jnp.sum(total, axis=0, keepdims=True))


def forward_kernel(
    plan, n_own, batch, where_ref, pick_hbm, count_hbm, order_hbm,
    pool_hbm, sent_hbm, syn_hbm, pcol_hbm, ptap_hbm, low_ref, near_ref, far_ref,
    kept_ref, other_ref,
    part_ref, param_ref, all_ref, wl_ref, rows_ref, deep_ref, sums_ref, chan_ref, now_ref, next_ref, thr_ref, coef_ref,
    pick_ref, count_ref, order_ref, syn_ref, pcol_ref, ptap_ref, sems,
):
    D, KP, KU, C = plan.depth, plan.deep, plan.used, plan.channels
    n_pool, n_sent = pool_hbm.shape[0], sent_hbm.shape[0]
    copies = [
        pltpu.make_async_copy(src, dst, sems.at[n])
        for n, (src, dst) in enumerate(
            (
                (ptap_hbm, ptap_ref),
                (pick_hbm, pick_ref),
                (count_hbm, count_ref),
                (order_hbm, order_ref),
                (pcol_hbm, pcol_ref),
                (syn_hbm, syn_ref),
                (pool_hbm, all_ref.at[pl.ds(0, n_pool)]),
                (sent_hbm, all_ref.at[pl.ds(n_pool, n_sent)]),
            )
        )
    ]
    for copy in copies:
        copy.start()
    part_ref[...] = jnp.zeros_like(part_ref)
    if KP > KU:
        now_ref[KU:KP, :] = jnp.zeros((KP - KU, plan.lanes), bf16)
    join_params(low_ref, near_ref, far_ref, param_ref)
    copies[0].wait()
    make_weights(plan, param_ref, ptap_ref, wl_ref, deep_ref, sums_ref, chan_ref)
    for copy in copies[1:]:
        copy.wait()

    pos = where_ref[0]
    mate_count = count_ref[0, pos ^ 1]
    own_count = count_ref[0, pos]
    full = own_count == n_pool
    own_count = own_count - jnp.where(full, n_sent, 0)
    mate_count = jnp.where(mate_count == n_pool, n_sent, 0)
    total = lax.fori_loop(0, count_ref.shape[1], lambda i, t: t + count_ref[0, i], jnp.int32(0)).astype(f32)
    flags = [is_chosen(order_ref, batch, pos * n_own + i) for i in range(n_own)]
    n_syn = functools.reduce(lambda a, b: a + b, flags)
    n_real = n_pool + n_sent
    for i in range(n_own):
        all_ref[n_real + i] = syn_ref[i].astype(bf16)

    def image_of(i):
        syn_at = jnp.int32(n_real + n_own - 1)
        before = n_syn
        for s in reversed(range(n_own)):
            before = before - flags[s]
            syn_at = jnp.where((flags[s] > 0) & (i == before), n_real + s, syn_at)
        own_at = jnp.clip(i - n_syn, 0, n_pool - 1)
        own_at = jnp.where(full, own_at, pick_ref[0, 0, own_at])
        sent_at = n_pool + jnp.clip(i - n_syn - own_count, 0, n_sent - 1)
        real_at = jnp.where(i - n_syn < own_count, own_at, sent_at)
        return jnp.where(i < n_syn, syn_at, real_at), jnp.where(i < n_syn, 0.25 / batch, -0.25 / total)

    def begin(i):
        at, weight = image_of(i)
        planes = [all_ref[at, c] for c in range(C)]
        return Prepare(plan, planes, pcol_ref[...], rows_ref, deep_ref, sums_ref, chan_ref), weight

    prep, weight = begin(jnp.int32(0))
    for _ in prep.stages(now_ref):
        pass
    thr_ref[...] = prep.thr
    coef_ref[...] = prep.scale * weight
    tile = 2 * LANES

    def step(i, base):
        prep, weight = begin(i + 1)
        ahead = prep.stages(next_ref)
        base = base + coef_ref[...] * thr_ref[...]
        wide = 2 * tile
        for t in range(plan.lanes // wide):
            at = t * wide
            y = mm(wl_ref[...], now_ref[:, at : at + wide])
            for _ in range((3, 3, 2, 0)[min(t, 3)]):
                next(ahead, None)
            for odd in range(2):
                for blk in range(D // 16):
                    r0 = (odd * (D // 16) + blk) * 64
                    thr = thr_ref[blk * 16 : (blk + 1) * 16, :]
                    coef = coef_ref[blk * 16 : (blk + 1) * 16, :]
                    out = slice(odd * D + blk * 16, odd * D + (blk + 1) * 16)
                    for half in range(wide // LANES):
                        lanes = slice(half * LANES, (half + 1) * LANES)
                        ys = [jnp.maximum(y[r0 + p * 16 : r0 + (p + 1) * 16, lanes], thr) for p in range(4)]
                        here = slice(at + half * LANES, at + (half + 1) * LANES)
                        part_ref[out, here] += coef * ((ys[0] + ys[1]) + (ys[2] + ys[3]))
        for _ in ahead:
            pass
        now_ref[0:KU, :] = next_ref[0:KU, :]
        thr_ref[...] = prep.thr
        coef_ref[...] = prep.scale * weight
        return base

    base = lax.fori_loop(0, n_syn + own_count + mate_count, step, jnp.zeros((D, LANES), f32))
    base = 4.0 * base
    mine = pl.multiple_of((pos & 1) * D, D)
    for pair in range(plan.pairs):
        here = slice(pair * LANES, (pair + 1) * LANES)
        other_ref[:, here] = part_ref[pl.ds(D - mine, D), here] - base
        kept_ref[:, here] = part_ref[pl.ds(mine, D), here] - base


def middle_kernel(
    plan, n_own, batch, own, where_ref, order_ref, syn_ref, first_ref, second_ref, pcol_ref, ptap_ref, low_ref, near_ref, far_ref,
    cols_ref, vsum_ref, hits_ref, stat_ref, wl_ref, wlt_ref, decay_ref,
    param_ref, rows_ref, deep_ref, sums_ref, chan_ref,
):
    D, KP, KU, C = plan.depth, plan.deep, plan.used, plan.channels
    flag = is_chosen(order_ref, batch, where_ref[0] * n_own + own)
    tile = 2 * LANES
    decay_ref[0] = beta_one * first_ref[own]
    decay_ref[1] = beta_two * second_ref[own]

    @pl.when(flag > 0)
    def _():
        join_params(low_ref, near_ref, far_ref, param_ref)
        make_weights(plan, param_ref, ptap_ref, wl_ref, deep_ref, sums_ref, chan_ref)
        for g in range(plan.groups):
            wlt_ref[:, g * D : (g + 1) * D] = wl_ref[g * D : (g + 1) * D, :].astype(f32).T.astype(bf16)[0:KU, :]
        if KP > KU:
            cols_ref[KU:KP, :] = jnp.zeros((KP - KU, plan.lanes), bf16)
        planes = [syn_ref[own, c].astype(bf16) for c in range(C)]
        prep = Prepare(plan, planes, pcol_ref[...], rows_ref, deep_ref, sums_ref, chan_ref)
        for _ in prep.stages(cols_ref):
            pass
        for n, value in enumerate((prep.mean, prep.factor, prep.scale, prep.thr, chan_ref[0], chan_ref[1])):
            stat_ref[n] = value

        for t in range(plan.lanes // tile):
            at = t * tile
            y = mm(wl_ref[...], cols_ref[:, at : at + tile])
            for odd in range(2):
                for blk in range(D // 16):
                    r0 = (odd * (D // 16) + blk) * 64
                    thr = stat_ref[3, blk * 16 : (blk + 1) * 16, :]
                    out = slice(odd * D + blk * 16, odd * D + (blk + 1) * 16)
                    for half in range(2):
                        lanes = slice(half * LANES, (half + 1) * LANES)
                        yp = [y[r0 + p * 16 : r0 + (p + 1) * 16, lanes] for p in range(4)]
                        ys = [jnp.maximum(a, thr) for a in yp]
                        hs = [jnp.where(a > thr, 1.0, 0.0) for a in yp]
                        here = slice(at + half * LANES, at + (half + 1) * LANES)
                        vsum_ref[out, here] = ((ys[0] + ys[1]) + (ys[2] + ys[3])) - 4.0 * thr
                        hits_ref[out, here] = (hs[0] + hs[1]) + (hs[2] + hs[3])


def backward_kernel(
    plan, n_own, batch, where_ref, order_ref, *refs,
):
    D, KU, blocks = plan.depth, plan.used, plan.depth // 16
    gap_ref = refs[0]
    owns = [refs[1 + 7 * i : 8 + 7 * i] for i in range(n_own)]
    (
        pcol_ref, syn_ref, new_syn_ref, new_first_ref, new_second_ref,
        grads_ref, shared_dcols, shared_col,
    ) = refs[1 + 7 * n_own :]
    pos = where_ref[0]
    tile = 2 * LANES
    grad_factor = 2.0 * loss_scale / batch
    shape = (plan.height, plan.halves * plan.span)
    spot = lax.broadcasted_iota(jnp.int32, shape, 1)
    slot = lax.rem(spot, SLOTS)
    row = lax.div(spot, plan.span) * plan.rows + lax.div(lax.rem(spot, plan.span), SLOTS) * 4 + slot - 1
    prow = jnp.where((lax.broadcasted_iota(jnp.int32, shape, 0) == row) & (slot < 6), 1.0, 0.0).astype(bf16)
    flags = [is_chosen(order_ref, batch, pos * n_own + i) for i in range(n_own)]

    def gradient(i):
        grad_ref, dcols_ref, col_ref = grads_ref.at[i], shared_dcols.at[i], shared_col.at[i]
        cols_ref, vsum_ref, hits_ref, stat_ref, wl_ref, wlt_ref, decay_ref = owns[i]
        unit = grad_factor / (4.0 * plan.pixels)
        for blk in range(blocks):
            chan = slice(blk * 16, (blk + 1) * 16)
            one = two = jnp.zeros((16, LANES), f32)
            for pair in range(plan.pairs):
                here = slice(pair * LANES, (pair + 1) * LANES)
                for odd in range(2):
                    rows = slice(odd * D + blk * 16, odd * D + (blk + 1) * 16)
                    gap = gap_ref[rows, here]
                    one = one + gap * hits_ref[rows, here]
                    two = two + gap * vsum_ref[rows, here]
            one = jnp.broadcast_to(jnp.sum(one, axis=1, keepdims=True), (16, LANES)) * unit
            two = jnp.broadcast_to(jnp.sum(two, axis=1, keepdims=True), (16, LANES)) * unit
            mean, factor, scale, thr, gain, ratio = [stat_ref[n, chan, :] for n in range(6)]
            slope = factor * factor * (scale * two - one * (ratio * gain))
            col_ref[0, chan, :] = factor * gain * (0.25 * grad_factor)
            col_ref[1, chan, :] = slope
            col_ref[2, chan, :] = slope * mean - factor * (gain * one)

        wide = 2 * tile
        for t in range(plan.lanes // wide):
            at = t * wide
            y = mm(wl_ref[...], cols_ref[:, at : at + wide])
            inner = []
            for odd in range(2):
                for blk in range(blocks):
                    r0 = (odd * blocks + blk) * 64
                    chan = slice(blk * 16, (blk + 1) * 16)
                    thr_b, up_b, slope_b, off = stat_ref[3, chan, :], col_ref[0, chan, :], col_ref[1, chan, :], col_ref[2, chan, :]
                    ons = []
                    for half in range(wide // LANES):
                        gap = gap_ref[odd * D + blk * 16 : odd * D + (blk + 1) * 16, at + half * LANES : at + (half + 1) * LANES]
                        ons.append(up_b * gap + off)
                    for p in range(4):
                        both = []
                        for half in range(wide // LANES):
                            yp = y[r0 + p * 16 : r0 + (p + 1) * 16, half * LANES : (half + 1) * LANES]
                            both.append((jnp.where(yp > thr_b, ons[half], off) - slope_b * yp).astype(bf16))
                        inner.append(jnp.concatenate(both, axis=1))
            dcols_ref[:, at : at + wide] = mm(wlt_ref[...], jnp.concatenate(inner, axis=0))

        shifts = []
        for s in range(4):
            shifts.append(
                jnp.concatenate(
                    [
                        dcols_ref[
                            (s * plan.channels + c) * SLOTS : (s * plan.channels + c + 1) * SLOTS,
                            pair * LANES : (pair + 1) * LANES,
                        ]
                        for c in range(plan.channels)
                        for pair in range(plan.pairs)
                    ],
                    axis=0,
                )
            )
        high, low = split_two(jnp.concatenate(shifts, axis=1))
        back = (((1,), (1,)), ((), ()))
        pcol = pcol_ref[...]
        wide = lax.dot_general(high, pcol, back, preferred_element_type=f32) + lax.dot_general(
            low, pcol, back, preferred_element_type=f32
        )
        tall = jnp.concatenate(
            [
                jnp.concatenate(
                    [
                        wide[c * plan.span : (c + 1) * plan.span, half * plan.width : (half + 1) * plan.width]
                        for c in range(plan.channels)
                    ],
                    axis=1,
                )
                for half in range(plan.halves)
            ],
            axis=0,
        )
        high, low = split_two(tall)
        image = mm(prow, high) + mm(prow, low)
        for c in range(plan.channels):
            grad_ref[c] = image[:, c * plan.width : (c + 1) * plan.width]

    for i in range(n_own):

        @pl.when(flags[i] > 0)
        def _():
            gradient(i)

        @pl.when(flags[i] == 0)
        def _():
            grads_ref[i] = jnp.zeros(grads_ref.shape[1:], f32)

    for i in range(n_own):
        decay_ref = owns[i][6]
        for c in range(plan.channels):
            grad = grads_ref[i, c]
            first_new = decay_ref[0, c] + (1.0 - beta_one) * grad
            second_new = decay_ref[1, c] + (1.0 - beta_two) * grad * grad
            corrected = first_new / (1.0 - beta_one**adam_step)
            scale_hat = jnp.sqrt(second_new / (1.0 - beta_two**adam_step))
            new_syn_ref[i, c] = syn_ref[i, c] - learn_rate * corrected / (scale_hat + adam_eps)
            new_first_ref[i, c] = first_new
            new_second_ref[i, c] = second_new


def gather_params(conv_weight, norm_gain, norm_bias, taps_pad):
    taps = conv_weight.shape[0]
    tall = taps_pad + 16
    own = (
        jnp.pad(conv_weight, ((0, tall - taps), (0, 0)))
        + jnp.pad(norm_gain[None], ((taps_pad, tall - taps_pad - 1), (0, 0)))
        + jnp.pad(norm_bias[None], ((taps_pad + 1, tall - taps_pad - 2), (0, 0)))
    )
    if lax.axis_size("cls") == 2:
        other = lax.ppermute(own, "cls", [(0, 1), (1, 0)])
        return (1 - lax.axis_index("cls")).astype(jnp.int32)[None], own, other
    whole = lax.all_gather(own, "cls", axis=1, tiled=True)
    half = whole.shape[1] // 2
    return jnp.ones((1,), jnp.int32), whole[:, :half], whole[:, half:]


class Exchange:
    def __init__(self):
        self.n = lax.axis_size("wide")
        self.pos = lax.axis_index("wide")
        steps = []
        while 1 << (len(steps) + 1) <= self.n:
            steps.append(1 << len(steps))
        self.first, rest = steps[0], steps[1:]
        self.masks = [(self.first, self.first)] + list(zip(rest, rest[1:] + rest[:1]))

    def swap(self, x, masks):
        return lax.ppermute(x, "wide", [(i, i ^ masks[i & self.first]) for i in range(self.n)])

    def high(self, masks):
        return (self.pos & jnp.where((self.pos & self.first) > 0, masks[1], masks[0])) > 0

    def add(self, own, masks):
        high = self.high(masks)
        rows = own.shape[0] // 2
        kept = jnp.where(high, own[rows:], own[:rows])
        sent = jnp.where(high, own[:rows], own[rows:]).astype(jnp.float16)
        return kept, sent

    def join(self, own, other, masks):
        high = self.high(masks)
        return jnp.concatenate([jnp.where(high, other, own), jnp.where(high, own, other)], axis=0)


def exchange_sum(kept, away, where, middle, n_own):
    ex = Exchange()
    halved = ex.masks[:2]
    whole = ex.masks[2:]
    rounds = [(m, "halve") for m in halved] + [(m, "whole") for m in whole] + [(m, "join") for m in reversed(halved)]
    at_round = [min(1 + i, len(rounds) - 2) for i in range(n_own)]
    own, made = None, []
    for n, (masks, kind) in enumerate(rounds):
        if n == 0:
            own, sent = kept, away.astype(jnp.float16)
        elif kind == "halve":
            own, sent = ex.add(own, masks)
        else:
            sent = own.astype(jnp.float16)
        todo = [i for i in range(n_own) if at_round[i] == n]
        if todo:
            sent, held = lax.optimization_barrier((sent, where))
        got = ex.swap(sent, masks)
        if todo:
            new = [middle(i, held) for i in todo]
            if n + 1 < len(rounds):
                got, new = lax.optimization_barrier((got, new))
            made += new
        own = ex.join(sent, got, masks) if kind == "join" else own + got.astype(f32)
    return own.astype(f32), made


def body(
    syn_images, adam_first, adam_second, real_pool, real_pick, real_count, syn_order,
    conv_weight, norm_gain, norm_bias,
):
    _, n_own, channels, height, width = syn_images.shape
    batch = syn_order.shape[1] // 2
    depth = conv_weight.shape[1] * lax.axis_size("cls")
    plan = Plan(channels, height, width, depth)
    pcol = jnp.asarray(plan.pick_cols(), bf16)
    ptap = jnp.asarray(plan.pick_taps(), bf16)
    n_pool = real_pool.shape[1]
    got = lax.ppermute(real_pool[0, n_pool - n_pool // 4 :], "wide", [(i, i ^ 1) for i in range(lax.axis_size("wide"))])
    low, near, far = gather_params(conv_weight, norm_gain, norm_bias, plan.taps_pad)
    where = lax.axis_index("wide").astype(jnp.int32)[None]

    smem = pl.BlockSpec(memory_space=pltpu.SMEM)
    vmem = pl.BlockSpec(memory_space=pltpu.VMEM)
    shape = jax.ShapeDtypeStruct
    rows = 2 * depth
    m_rows = plan.groups * depth
    weights = [
        pltpu.VMEM((channels * plan.tall, 4 * LANES), f32),
        pltpu.VMEM((depth, 3 * plan.deep), bf16),
        pltpu.VMEM((depth, plan.deep), f32),
        pltpu.VMEM((2 + channels, depth, LANES), f32),
    ]

    def within(mib):
        return pltpu.CompilerParams(vmem_limit_bytes=mib << 20)

    hbm = pl.BlockSpec(memory_space=pltpu.HBM)
    kept, sent = pl.pallas_call(
        functools.partial(forward_kernel, plan, n_own, batch),
        in_specs=[smem] + [hbm] * 4 + [pl.BlockSpec(memory_space=pl.ANY)] + [hbm] * 3 + [smem] + [vmem] * 2,
        out_specs=[vmem] * 2,
        out_shape=[shape((depth, plan.lanes), f32)] * 2,
        scratch_shapes=[
            pltpu.VMEM((rows, plan.lanes), f32),
            pltpu.VMEM((near.shape[0], depth), bf16),
            pltpu.VMEM((n_pool + got.shape[0] + n_own, channels, height, width), bf16),
            pltpu.VMEM((m_rows, plan.deep), bf16),
            *weights,
            pltpu.VMEM((plan.deep, plan.lanes), bf16),
            pltpu.VMEM((plan.used, plan.lanes), bf16),
            *[pltpu.VMEM((depth, LANES), f32)] * 2,
            pltpu.SMEM(real_pick.shape, jnp.int32),
            pltpu.SMEM(real_count.shape, jnp.int32),
            pltpu.SMEM(syn_order.shape, jnp.int32),
            pltpu.VMEM(syn_images.shape[1:], f32),
            pltpu.VMEM(pcol.shape, bf16),
            pltpu.VMEM(ptap.shape, bf16),
            pltpu.SemaphoreType.DMA((8,)),
        ],
        compiler_params=within(60),
        name="embed_sums",
    )(where, real_pick, real_count, syn_order, real_pool[0], got, syn_images[0], pcol, ptap, low, near, far)

    def middle(own, held):
        return pl.pallas_call(
            functools.partial(middle_kernel, plan, n_own, batch, own),
            in_specs=[smem] * 2 + [vmem] * 5 + [smem] + [vmem] * 2,
            out_specs=[vmem] * 7,
            out_shape=[
                shape((plan.deep, plan.lanes), bf16),
                shape((rows, plan.lanes), f32),
                shape((rows, plan.lanes), f32),
                shape((6, depth, LANES), f32),
                shape((m_rows, plan.deep), bf16),
                shape((plan.used, m_rows), bf16),
                shape((2, channels, height, width), f32),
            ],
            scratch_shapes=[pltpu.VMEM((near.shape[0], depth), bf16), *weights],
            compiler_params=within(18),
            name="syn_features",
        )(held, syn_order, syn_images[0], adam_first[0], adam_second[0], pcol, ptap, low, near, far)

    gap, made = exchange_sum(kept, sent, where, middle, n_own)

    img = shape((n_own, channels, height, width), f32)
    outs = pl.pallas_call(
        functools.partial(backward_kernel, plan, n_own, batch),
        in_specs=[smem] * 2 + [vmem] * (3 + 7 * n_own),
        out_specs=[vmem] * 3,
        out_shape=[img] * 3,
        scratch_shapes=[
            pltpu.VMEM((n_own, channels, height, width), f32),
            pltpu.VMEM((n_own, plan.used, plan.lanes), f32),
            pltpu.VMEM((n_own, 3, depth, LANES), f32),
        ],
        compiler_params=within(24),
        name="image_grads",
    )(
        where, syn_order, gap, *[x for one in made for x in one], pcol, syn_images[0],
    )
    return tuple(out[None] for out in outs)


def solution(mesh):
    image = P("cls", "wide", None, None, None)
    return jax.shard_map(
        body,
        mesh=mesh,
        in_specs=(
            image, image, image, image, P("cls", "wide", None), P("cls", None), P("cls", None),
            P(None, "cls"), P("cls"), P("cls"),
        ),
        out_specs=(image, image, image),
        check_vma=False,
    )
```

```python
import functools

import jax
import jax.numpy as jnp
import numpy as np
from jax import lax
from jax.experimental import pallas as pl
from jax.experimental.pallas import tpu as pltpu
from jax.sharding import PartitionSpec as P

beta_one = 0.9
beta_two = 0.99
adam_step = 10.0
learn_rate = 0.1
adam_eps = 1e-08
loss_scale = 512.0
norm_eps = 1e-05

LANES = 128
SLOTS = 8
f32 = jnp.float32
bf16 = jnp.bfloat16


def mm(a, b):
    return lax.dot_general(a, b, (((1,), (0,)), ((), ())), preferred_element_type=f32)


class Plan:
    def __init__(self, channels, height, width, depth):
        self.channels, self.height, self.width, self.depth = channels, height, width, depth
        self.cols = width // 2
        self.halves = LANES // self.cols
        self.rows = height // self.halves
        self.pairs = self.rows // 4
        self.tall = self.rows + 16
        self.span = self.pairs * SLOTS
        self.lanes = self.pairs * LANES
        self.taps = 9 * channels
        self.taps_pad = -(-self.taps // 32) * 32
        self.used = 4 * channels * SLOTS
        self.deep = -(-self.used // LANES) * LANES
        self.groups = 8
        self.pixels = height * width

    def pick_cols(self):
        out = np.zeros((self.halves, self.width, 4, self.halves, self.cols), np.float32)
        for shift in range(4):
            for col in range(self.cols):
                src = 2 * col + shift - 1
                if 0 <= src < self.width:
                    for half in range(self.halves):
                        out[half, src, shift, half, col] = 1.0
        return out.reshape(self.halves * self.width, 4 * LANES)

    def pick_taps(self):
        out = np.zeros((2, 2, 2, self.deep, self.taps_pad), np.float32)
        for odd in range(2):
            for a in range(2):
                for b in range(2):
                    for i in range(3):
                        for j in range(3):
                            for c in range(self.channels):
                                k = ((b + j) * self.channels + c) * SLOTS + 2 * odd + a + i
                                out[odd, a, b, k, (i * 3 + j) * self.channels + c] = 1.0
        return out.reshape(self.groups * self.deep, self.taps_pad)


def spread(row):
    return jnp.broadcast_to(row, (LANES, row.shape[1])).T


def split_two(x):
    high = x.astype(bf16)
    return high, (x - high.astype(f32)).astype(bf16)


class Prepare:
    def __init__(self, plan, planes, pcol, rows_ref, deep_ref, sums_ref, chan_ref):
        self.plan, self.planes, self.pcol, self.rows_ref = plan, planes, pcol, rows_ref
        self.deep_ref, self.sums_ref, self.chan_ref = deep_ref, sums_ref, chan_ref

    def stages(self, cols_ref):
        plan = self.plan
        D, KU, KP, C, tall = plan.depth, plan.used, plan.deep, plan.channels, plan.tall
        shifts, blocks = [], []
        for plane in self.planes:
            rows = plane.astype(f32)
            total = functools.reduce(lambda a, b: a + b, [rows[r : r + 8] for r in range(0, plan.height, 8)])
            total = jnp.sum(jnp.sum(total, axis=1, keepdims=True), axis=0, keepdims=True)
            shifts.append(jnp.round(total * (4.0 / plan.pixels)) * 0.25)
            rows = jnp.concatenate([jnp.zeros((1, plan.width), f32), rows, jnp.zeros((15, plan.width), f32)], axis=0)
            blocks.append(
                jnp.concatenate([rows[h * plan.rows : h * plan.rows + tall] for h in range(plan.halves)], axis=1).astype(bf16)
            )
        yield
        self.rows_ref[...] = mm(jnp.concatenate(blocks, axis=0), self.pcol)
        yield
        tail = jnp.ones((KP - KU, LANES), bf16)
        gram = None
        for half in range(2):
            lean = []
            for pair in range(half * plan.pairs // 2, (half + 1) * plan.pairs // 2):
                parts = [
                    (c, self.rows_ref[c * tall + 4 * pair : c * tall + 4 * pair + SLOTS, s * LANES : (s + 1) * LANES])
                    for s in range(4)
                    for c in range(C)
                ]
                cols_ref[0:KU, pair * LANES : (pair + 1) * LANES] = jnp.concatenate([x for _, x in parts], axis=0).astype(bf16)
                own = jnp.concatenate([x - shifts[c] for c, x in parts], axis=0).astype(bf16)
                lean.append(jnp.concatenate([own, tail], axis=0))
            yield
            lean = jnp.concatenate(lean, axis=1)
            part = lax.dot_general(lean, lean, (((1,), (1,)), ((), ())), preferred_element_type=f32)
            gram = part if gram is None else gram + part
            yield
        moved = gram
        for step in (1, 2, C * SLOTS):
            moved = moved + pltpu.roll(pltpu.roll(moved, KP - step, 0), KP - step, 1)
        high = moved.astype(bf16)
        rest = moved - high.astype(f32)
        mid = rest.astype(bf16)
        low = (rest - mid.astype(f32)).astype(bf16)
        quad = mm(self.deep_ref[...], jnp.concatenate([high, mid, low], axis=0))
        yield
        first = self.deep_ref[:, 0:KP].astype(f32)
        second = jnp.sum(quad * first, axis=1, keepdims=True) * (1.0 / plan.pixels)
        off = jnp.sum(self.sums_ref[...] * gram[KU : KU + 1, :], axis=1, keepdims=True) * (1.0 / plan.pixels)
        second = jnp.broadcast_to(second, (D, LANES))
        off = jnp.broadcast_to(off, (D, LANES))
        mean = off
        for c in range(C):
            mean = mean + shifts[c] * self.chan_ref[2 + c]
        var = jnp.maximum(second - off * off, 0.0) + norm_eps
        self.factor = lax.rsqrt(var)
        self.scale = self.chan_ref[0] * self.factor
        self.mean = mean
        self.thr = mean - self.chan_ref[1] * (var * self.factor)
        yield


def join_params(low_ref, near_ref, far_ref, param_ref):
    near, far = near_ref[...].astype(f32), far_ref[...].astype(f32)
    low = low_ref[0] > 0
    param_ref[...] = jnp.concatenate([jnp.where(low, near, far), jnp.where(low, far, near)], axis=1).astype(bf16)


def is_chosen(order_ref, batch, gid):
    return lax.fori_loop(0, batch, lambda j, t: t | (order_ref[0, j] == gid).astype(jnp.int32), jnp.int32(0))


def make_weights(plan, param_ref, ptap_ref, wl_ref, deep_ref, sums_ref, chan_ref):
    D, KP, C = plan.depth, plan.deep, plan.channels
    spread_taps = mm(ptap_ref[...], param_ref[0 : plan.taps_pad, :])
    sums = None
    for g in range(plan.groups):
        odd, phase = divmod(g, 4)
        turned = spread_taps[g * KP : (g + 1) * KP, :].T
        sums = turned if sums is None else sums + turned
        turned = turned.astype(bf16)
        if g == 0:
            for n in range(3):
                deep_ref[:, n * KP : (n + 1) * KP] = turned
        for blk in range(D // 16):
            at = ((odd * (D // 16) + blk) * 4 + phase) * 16
            rows = turned[blk * 16 : (blk + 1) * 16, :]
            wl_ref[at : at + 16, :] = rows
    sums_ref[...] = sums
    gain = param_ref[plan.taps_pad : plan.taps_pad + 1, :].astype(f32)
    bias = param_ref[plan.taps_pad + 1 : plan.taps_pad + 2, :].astype(f32)
    chan_ref[0] = spread(gain)
    chan_ref[1] = spread(bias / gain)
    first = spread_taps[0:KP, :]
    for c in range(C):
        total = functools.reduce(lambda a, b: a + b, [first[(s * C + c) * SLOTS : (s * C + c + 1) * SLOTS] for s in range(4)])
        chan_ref[2 + c] = spread(jnp.sum(total, axis=0, keepdims=True))


def forward_kernel(
    plan, n_own, batch, where_ref, pick_hbm, count_hbm, order_hbm,
    pool_hbm, sent_hbm, syn_hbm, pcol_hbm, ptap_hbm, low_ref, near_ref, far_ref,
    kept_ref, other_ref,
    part_ref, param_ref, all_ref, wl_ref, rows_ref, deep_ref, sums_ref, chan_ref, now_ref, next_ref, thr_ref, coef_ref,
    pick_ref, count_ref, order_ref, syn_ref, pcol_ref, ptap_ref, sems,
):
    D, KP, KU, C = plan.depth, plan.deep, plan.used, plan.channels
    n_pool, n_sent = pool_hbm.shape[0], sent_hbm.shape[0]
    copies = [
        pltpu.make_async_copy(src, dst, sems.at[n])
        for n, (src, dst) in enumerate(
            (
                (ptap_hbm, ptap_ref),
                (pick_hbm, pick_ref),
                (count_hbm, count_ref),
                (order_hbm, order_ref),
                (pcol_hbm, pcol_ref),
                (syn_hbm, syn_ref),
                (pool_hbm, all_ref.at[pl.ds(0, n_pool)]),
                (sent_hbm, all_ref.at[pl.ds(n_pool, n_sent)]),
            )
        )
    ]
    for copy in copies:
        copy.start()
    part_ref[...] = jnp.zeros_like(part_ref)
    if KP > KU:
        now_ref[KU:KP, :] = jnp.zeros((KP - KU, plan.lanes), bf16)
    join_params(low_ref, near_ref, far_ref, param_ref)
    copies[0].wait()
    make_weights(plan, param_ref, ptap_ref, wl_ref, deep_ref, sums_ref, chan_ref)
    for copy in copies[1:]:
        copy.wait()

    pos = where_ref[0]
    mate_count = count_ref[0, pos ^ 1]
    own_count = count_ref[0, pos]
    full = own_count == n_pool
    own_count = own_count - jnp.where(full, n_sent, 0)
    mate_count = jnp.where(mate_count == n_pool, n_sent, 0)
    total = lax.fori_loop(0, count_ref.shape[1], lambda i, t: t + count_ref[0, i], jnp.int32(0)).astype(f32)
    flags = [is_chosen(order_ref, batch, pos * n_own + i) for i in range(n_own)]
    n_syn = functools.reduce(lambda a, b: a + b, flags)
    n_real = n_pool + n_sent
    for i in range(n_own):
        all_ref[n_real + i] = syn_ref[i].astype(bf16)

    def image_of(i):
        syn_at = jnp.int32(n_real + n_own - 1)
        before = n_syn
        for s in reversed(range(n_own)):
            before = before - flags[s]
            syn_at = jnp.where((flags[s] > 0) & (i == before), n_real + s, syn_at)
        own_at = jnp.clip(i - n_syn, 0, n_pool - 1)
        own_at = jnp.where(full, own_at, pick_ref[0, 0, own_at])
        sent_at = n_pool + jnp.clip(i - n_syn - own_count, 0, n_sent - 1)
        real_at = jnp.where(i - n_syn < own_count, own_at, sent_at)
        return jnp.where(i < n_syn, syn_at, real_at), jnp.where(i < n_syn, 0.25 / batch, -0.25 / total)

    def begin(i):
        at, weight = image_of(i)
        planes = [all_ref[at, c] for c in range(C)]
        return Prepare(plan, planes, pcol_ref[...], rows_ref, deep_ref, sums_ref, chan_ref), weight

    prep, weight = begin(jnp.int32(0))
    for _ in prep.stages(now_ref):
        pass
    thr_ref[...] = prep.thr
    coef_ref[...] = prep.scale * weight
    tile = 2 * LANES

    def step(i, base):
        prep, weight = begin(i + 1)
        ahead = prep.stages(next_ref)
        base = base + coef_ref[...] * thr_ref[...]
        wide = 2 * tile
        for t in range(plan.lanes // wide):
            at = t * wide
            y = mm(wl_ref[...], now_ref[:, at : at + wide])
            for _ in range((3, 3, 2, 0)[min(t, 3)]):
                next(ahead, None)
            for odd in range(2):
                for blk in range(D // 16):
                    r0 = (odd * (D // 16) + blk) * 64
                    thr = thr_ref[blk * 16 : (blk + 1) * 16, :]
                    coef = coef_ref[blk * 16 : (blk + 1) * 16, :]
                    out = slice(odd * D + blk * 16, odd * D + (blk + 1) * 16)
                    for half in range(wide // LANES):
                        lanes = slice(half * LANES, (half + 1) * LANES)
                        ys = [jnp.maximum(y[r0 + p * 16 : r0 + (p + 1) * 16, lanes], thr) for p in range(4)]
                        here = slice(at + half * LANES, at + (half + 1) * LANES)
                        part_ref[out, here] += coef * ((ys[0] + ys[1]) + (ys[2] + ys[3]))
        for _ in ahead:
            pass
        now_ref[0:KU, :] = next_ref[0:KU, :]
        thr_ref[...] = prep.thr
        coef_ref[...] = prep.scale * weight
        return base

    base = lax.fori_loop(0, n_syn + own_count + mate_count, step, jnp.zeros((D, LANES), f32))
    base = 4.0 * base
    mine = pl.multiple_of((pos & 1) * D, D)
    for pair in range(plan.pairs):
        here = slice(pair * LANES, (pair + 1) * LANES)
        other_ref[:, here] = part_ref[pl.ds(D - mine, D), here] - base
        kept_ref[:, here] = part_ref[pl.ds(mine, D), here] - base


def middle_kernel(
    plan, n_own, batch, own, where_ref, order_ref, syn_ref, first_ref, second_ref, pcol_ref, ptap_ref, low_ref, near_ref, far_ref,
    cols_ref, vsum_ref, hits_ref, stat_ref, wl_ref, wlt_ref, decay_ref,
    param_ref, rows_ref, deep_ref, sums_ref, chan_ref,
):
    D, KP, KU, C = plan.depth, plan.deep, plan.used, plan.channels
    flag = is_chosen(order_ref, batch, where_ref[0] * n_own + own)
    tile = 2 * LANES
    decay_ref[0] = beta_one * first_ref[own]
    decay_ref[1] = beta_two * second_ref[own]

    @pl.when(flag > 0)
    def _():
        join_params(low_ref, near_ref, far_ref, param_ref)
        make_weights(plan, param_ref, ptap_ref, wl_ref, deep_ref, sums_ref, chan_ref)
        for g in range(plan.groups):
            wlt_ref[:, g * D : (g + 1) * D] = wl_ref[g * D : (g + 1) * D, :].astype(f32).T.astype(bf16)[0:KU, :]
        if KP > KU:
            cols_ref[KU:KP, :] = jnp.zeros((KP - KU, plan.lanes), bf16)
        planes = [syn_ref[own, c].astype(bf16) for c in range(C)]
        prep = Prepare(plan, planes, pcol_ref[...], rows_ref, deep_ref, sums_ref, chan_ref)
        for _ in prep.stages(cols_ref):
            pass
        for n, value in enumerate((prep.mean, prep.factor, prep.scale, prep.thr, chan_ref[0], chan_ref[1])):
            stat_ref[n] = value

        for t in range(plan.lanes // tile):
            at = t * tile
            y = mm(wl_ref[...], cols_ref[:, at : at + tile])
            for odd in range(2):
                for blk in range(D // 16):
                    r0 = (odd * (D // 16) + blk) * 64
                    thr = stat_ref[3, blk * 16 : (blk + 1) * 16, :]
                    out = slice(odd * D + blk * 16, odd * D + (blk + 1) * 16)
                    for half in range(2):
                        lanes = slice(half * LANES, (half + 1) * LANES)
                        yp = [y[r0 + p * 16 : r0 + (p + 1) * 16, lanes] for p in range(4)]
                        ys = [jnp.maximum(a, thr) for a in yp]
                        hs = [jnp.where(a > thr, 1.0, 0.0) for a in yp]
                        here = slice(at + half * LANES, at + (half + 1) * LANES)
                        vsum_ref[out, here] = ((ys[0] + ys[1]) + (ys[2] + ys[3])) - 4.0 * thr
                        hits_ref[out, here] = (hs[0] + hs[1]) + (hs[2] + hs[3])


def backward_kernel(
    plan, n_own, batch, where_ref, order_ref, *refs,
):
    D, KU, blocks = plan.depth, plan.used, plan.depth // 16
    gap_ref = refs[0]
    owns = [refs[1 + 7 * i : 8 + 7 * i] for i in range(n_own)]
    (
        pcol_ref, syn_ref, new_syn_ref, new_first_ref, new_second_ref,
        grads_ref, shared_dcols, shared_col,
    ) = refs[1 + 7 * n_own :]
    pos = where_ref[0]
    tile = 2 * LANES
    grad_factor = 2.0 * loss_scale / batch
    shape = (plan.height, plan.halves * plan.span)
    spot = lax.broadcasted_iota(jnp.int32, shape, 1)
    slot = lax.rem(spot, SLOTS)
    row = lax.div(spot, plan.span) * plan.rows + lax.div(lax.rem(spot, plan.span), SLOTS) * 4 + slot - 1
    prow = jnp.where((lax.broadcasted_iota(jnp.int32, shape, 0) == row) & (slot < 6), 1.0, 0.0).astype(bf16)
    flags = [is_chosen(order_ref, batch, pos * n_own + i) for i in range(n_own)]

    def gradient(i):
        grad_ref, dcols_ref, col_ref = grads_ref.at[i], shared_dcols.at[i], shared_col.at[i]
        cols_ref, vsum_ref, hits_ref, stat_ref, wl_ref, wlt_ref, decay_ref = owns[i]
        unit = grad_factor / (4.0 * plan.pixels)
        for blk in range(blocks):
            chan = slice(blk * 16, (blk + 1) * 16)
            one = two = jnp.zeros((16, LANES), f32)
            for pair in range(plan.pairs):
                here = slice(pair * LANES, (pair + 1) * LANES)
                for odd in range(2):
                    rows = slice(odd * D + blk * 16, odd * D + (blk + 1) * 16)
                    gap = gap_ref[rows, here]
                    one = one + gap * hits_ref[rows, here]
                    two = two + gap * vsum_ref[rows, here]
            one = jnp.broadcast_to(jnp.sum(one, axis=1, keepdims=True), (16, LANES)) * unit
            two = jnp.broadcast_to(jnp.sum(two, axis=1, keepdims=True), (16, LANES)) * unit
            mean, factor, scale, thr, gain, ratio = [stat_ref[n, chan, :] for n in range(6)]
            slope = factor * factor * (scale * two - one * (ratio * gain))
            col_ref[0, chan, :] = factor * gain * (0.25 * grad_factor)
            col_ref[1, chan, :] = slope
            col_ref[2, chan, :] = slope * mean - factor * (gain * one)

        wide = 2 * tile
        for t in range(plan.lanes // wide):
            at = t * wide
            y = mm(wl_ref[...], cols_ref[:, at : at + wide])
            inner = []
            for odd in range(2):
                for blk in range(blocks):
                    r0 = (odd * blocks + blk) * 64
                    chan = slice(blk * 16, (blk + 1) * 16)
                    thr_b, up_b, slope_b, off = stat_ref[3, chan, :], col_ref[0, chan, :], col_ref[1, chan, :], col_ref[2, chan, :]
                    ons = []
                    for half in range(wide // LANES):
                        gap = gap_ref[odd * D + blk * 16 : odd * D + (blk + 1) * 16, at + half * LANES : at + (half + 1) * LANES]
                        ons.append(up_b * gap + off)
                    for p in range(4):
                        both = []
                        for half in range(wide // LANES):
                            yp = y[r0 + p * 16 : r0 + (p + 1) * 16, half * LANES : (half + 1) * LANES]
                            both.append((jnp.where(yp > thr_b, ons[half], off) - slope_b * yp).astype(bf16))
                        inner.append(jnp.concatenate(both, axis=1))
            dcols_ref[:, at : at + wide] = mm(wlt_ref[...], jnp.concatenate(inner, axis=0))

        shifts = []
        for s in range(4):
            shifts.append(
                jnp.concatenate(
                    [
                        dcols_ref[
                            (s * plan.channels + c) * SLOTS : (s * plan.channels + c + 1) * SLOTS,
                            pair * LANES : (pair + 1) * LANES,
                        ]
                        for c in range(plan.channels)
                        for pair in range(plan.pairs)
                    ],
                    axis=0,
                )
            )
        high, low = split_two(jnp.concatenate(shifts, axis=1))
        back = (((1,), (1,)), ((), ()))
        pcol = pcol_ref[...]
        wide = lax.dot_general(high, pcol, back, preferred_element_type=f32) + lax.dot_general(
            low, pcol, back, preferred_element_type=f32
        )
        tall = jnp.concatenate(
            [
                jnp.concatenate(
                    [
                        wide[c * plan.span : (c + 1) * plan.span, half * plan.width : (half + 1) * plan.width]
                        for c in range(plan.channels)
                    ],
                    axis=1,
                )
                for half in range(plan.halves)
            ],
            axis=0,
        )
        high, low = split_two(tall)
        image = mm(prow, high) + mm(prow, low)
        for c in range(plan.channels):
            grad_ref[c] = image[:, c * plan.width : (c + 1) * plan.width]

    for i in range(n_own):

        @pl.when(flags[i] > 0)
        def _():
            gradient(i)

        @pl.when(flags[i] == 0)
        def _():
            grads_ref[i] = jnp.zeros(grads_ref.shape[1:], f32)

    for i in range(n_own):
        decay_ref = owns[i][6]
        for c in range(plan.channels):
            grad = grads_ref[i, c]
            first_new = decay_ref[0, c] + (1.0 - beta_one) * grad
            second_new = decay_ref[1, c] + (1.0 - beta_two) * grad * grad
            corrected = first_new / (1.0 - beta_one**adam_step)
            scale_hat = jnp.sqrt(second_new / (1.0 - beta_two**adam_step))
            new_syn_ref[i, c] = syn_ref[i, c] - learn_rate * corrected / (scale_hat + adam_eps)
            new_first_ref[i, c] = first_new
            new_second_ref[i, c] = second_new


def gather_params(conv_weight, norm_gain, norm_bias, taps_pad):
    taps = conv_weight.shape[0]
    tall = taps_pad + 16
    own = (
        jnp.pad(conv_weight, ((0, tall - taps), (0, 0)))
        + jnp.pad(norm_gain[None], ((taps_pad, tall - taps_pad - 1), (0, 0)))
        + jnp.pad(norm_bias[None], ((taps_pad + 1, tall - taps_pad - 2), (0, 0)))
    )
    if lax.axis_size("cls") == 2:
        other = lax.ppermute(own, "cls", [(0, 1), (1, 0)])
        return (1 - lax.axis_index("cls")).astype(jnp.int32)[None], own, other
    whole = lax.all_gather(own, "cls", axis=1, tiled=True)
    half = whole.shape[1] // 2
    return jnp.ones((1,), jnp.int32), whole[:, :half], whole[:, half:]


class Exchange:
    def __init__(self):
        self.n = lax.axis_size("wide")
        self.pos = lax.axis_index("wide")
        steps = []
        while 1 << (len(steps) + 1) <= self.n:
            steps.append(1 << len(steps))
        self.first, rest = steps[0], steps[1:]
        self.masks = [(self.first, self.first)] + list(zip(rest, rest[1:] + rest[:1]))

    def swap(self, x, masks):
        return lax.ppermute(x, "wide", [(i, i ^ masks[i & self.first]) for i in range(self.n)])

    def high(self, masks):
        return (self.pos & jnp.where((self.pos & self.first) > 0, masks[1], masks[0])) > 0

    def add(self, own, masks):
        high = self.high(masks)
        rows = own.shape[0] // 2
        kept = jnp.where(high, own[rows:], own[:rows])
        sent = jnp.where(high, own[:rows], own[rows:]).astype(jnp.float16)
        return kept, sent

    def join(self, own, other, masks):
        high = self.high(masks)
        return jnp.concatenate([jnp.where(high, other, own), jnp.where(high, own, other)], axis=0)


def exchange_sum(kept, away, where, middle, n_own):
    ex = Exchange()
    halved = ex.masks[:2]
    whole = ex.masks[2:]
    rounds = [(m, "halve") for m in halved] + [(m, "whole") for m in whole] + [(m, "join") for m in reversed(halved)]
    at_round = [min(1 + i, len(rounds) - 2) for i in range(n_own)]
    own, made = None, []
    for n, (masks, kind) in enumerate(rounds):
        if n == 0:
            own, sent = kept, away
        elif kind == "halve":
            own, sent = ex.add(own, masks)
        else:
            sent = own.astype(jnp.float16)
        todo = [i for i in range(n_own) if at_round[i] == n]
        if todo:
            sent, held = lax.optimization_barrier((sent, where))
        got = ex.swap(sent, masks)
        if todo:
            new = [middle(i, held) for i in todo]
            if n + 1 < len(rounds):
                got, new = lax.optimization_barrier((got, new))
            made += new
        own = ex.join(sent, got, masks) if kind == "join" else own + got.astype(f32)
    return own.astype(f32), made


def body(
    syn_images, adam_first, adam_second, real_pool, real_pick, real_count, syn_order,
    conv_weight, norm_gain, norm_bias,
):
    _, n_own, channels, height, width = syn_images.shape
    batch = syn_order.shape[1] // 2
    depth = conv_weight.shape[1] * lax.axis_size("cls")
    plan = Plan(channels, height, width, depth)
    pcol = jnp.asarray(plan.pick_cols(), bf16)
    ptap = jnp.asarray(plan.pick_taps(), bf16)
    n_pool = real_pool.shape[1]
    got = lax.ppermute(real_pool[0, n_pool - n_pool // 4 :], "wide", [(i, i ^ 1) for i in range(lax.axis_size("wide"))])
    low, near, far = gather_params(conv_weight, norm_gain, norm_bias, plan.taps_pad)
    where = lax.axis_index("wide").astype(jnp.int32)[None]

    smem = pl.BlockSpec(memory_space=pltpu.SMEM)
    vmem = pl.BlockSpec(memory_space=pltpu.VMEM)
    shape = jax.ShapeDtypeStruct
    rows = 2 * depth
    m_rows = plan.groups * depth
    weights = [
        pltpu.VMEM((channels * plan.tall, 4 * LANES), f32),
        pltpu.VMEM((depth, 3 * plan.deep), bf16),
        pltpu.VMEM((depth, plan.deep), f32),
        pltpu.VMEM((2 + channels, depth, LANES), f32),
    ]

    def within(mib):
        return pltpu.CompilerParams(vmem_limit_bytes=mib << 20)

    hbm = pl.BlockSpec(memory_space=pltpu.HBM)
    kept, sent = pl.pallas_call(
        functools.partial(forward_kernel, plan, n_own, batch),
        in_specs=[smem] + [hbm] * 4 + [pl.BlockSpec(memory_space=pl.ANY)] + [hbm] * 3 + [smem] + [vmem] * 2,
        out_specs=[vmem] * 2,
        out_shape=[shape((depth, plan.lanes), f32)] * 2,
        scratch_shapes=[
            pltpu.VMEM((rows, plan.lanes), f32),
            pltpu.VMEM((near.shape[0], depth), bf16),
            pltpu.VMEM((n_pool + got.shape[0] + n_own, channels, height, width), bf16),
            pltpu.VMEM((m_rows, plan.deep), bf16),
            *weights,
            pltpu.VMEM((plan.deep, plan.lanes), bf16),
            pltpu.VMEM((plan.used, plan.lanes), bf16),
            *[pltpu.VMEM((depth, LANES), f32)] * 2,
            pltpu.SMEM(real_pick.shape, jnp.int32),
            pltpu.SMEM(real_count.shape, jnp.int32),
            pltpu.SMEM(syn_order.shape, jnp.int32),
            pltpu.VMEM(syn_images.shape[1:], f32),
            pltpu.VMEM(pcol.shape, bf16),
            pltpu.VMEM(ptap.shape, bf16),
            pltpu.SemaphoreType.DMA((8,)),
        ],
        compiler_params=within(60),
        name="embed_sums",
    )(where, real_pick, real_count, syn_order, real_pool[0], got, syn_images[0], pcol, ptap, low, near, far)

    def middle(own, held):
        return pl.pallas_call(
            functools.partial(middle_kernel, plan, n_own, batch, own),
            in_specs=[smem] * 2 + [vmem] * 5 + [smem] + [vmem] * 2,
            out_specs=[vmem] * 7,
            out_shape=[
                shape((plan.deep, plan.lanes), bf16),
                shape((rows, plan.lanes), f32),
                shape((rows, plan.lanes), f32),
                shape((6, depth, LANES), f32),
                shape((m_rows, plan.deep), bf16),
                shape((plan.used, m_rows), bf16),
                shape((2, channels, height, width), f32),
            ],
            scratch_shapes=[pltpu.VMEM((near.shape[0], depth), bf16), *weights],
            compiler_params=within(18),
            name="syn_features",
        )(held, syn_order, syn_images[0], adam_first[0], adam_second[0], pcol, ptap, low, near, far)

    gap, made = exchange_sum(kept, sent, where, middle, n_own)

    img = shape((n_own, channels, height, width), f32)
    outs = pl.pallas_call(
        functools.partial(backward_kernel, plan, n_own, batch),
        in_specs=[smem] * 2 + [vmem] * (3 + 7 * n_own),
        out_specs=[vmem] * 3,
        out_shape=[img] * 3,
        scratch_shapes=[
            pltpu.VMEM((n_own, channels, height, width), f32),
            pltpu.VMEM((n_own, plan.used, plan.lanes), f32),
            pltpu.VMEM((n_own, 3, depth, LANES), f32),
        ],
        compiler_params=within(24),
        name="image_grads",
    )(
        where, syn_order, gap, *[x for one in made for x in one], pcol, syn_images[0],
    )
    return tuple(out[None] for out in outs)


def solution(mesh):
    image = P("cls", "wide", None, None, None)
    return jax.shard_map(
        body,
        mesh=mesh,
        in_specs=(
            image, image, image, image, P("cls", "wide", None), P("cls", None), P("cls", None),
            P(None, "cls"), P("cls"), P("cls"),
        ),
        out_specs=(image, image, image),
        check_vma=False,
    )
```

```python
import functools

import jax
import jax.numpy as jnp
import numpy as np
from jax import lax
from jax.experimental import pallas as pl
from jax.experimental.pallas import tpu as pltpu
from jax.sharding import PartitionSpec as P

beta_one = 0.9
beta_two = 0.99
adam_step = 10.0
learn_rate = 0.1
adam_eps = 1e-08
loss_scale = 512.0
norm_eps = 1e-05

LANES = 128
SLOTS = 8
f32 = jnp.float32
bf16 = jnp.bfloat16


def mm(a, b):
    return lax.dot_general(a, b, (((1,), (0,)), ((), ())), preferred_element_type=f32)


class Plan:
    def __init__(self, channels, height, width, depth):
        self.channels, self.height, self.width, self.depth = channels, height, width, depth
        self.cols = width // 2
        self.halves = LANES // self.cols
        self.rows = height // self.halves
        self.pairs = self.rows // 4
        self.tall = self.rows + 16
        self.span = self.pairs * SLOTS
        self.lanes = self.pairs * LANES
        self.taps = 9 * channels
        self.taps_pad = -(-self.taps // 32) * 32
        self.used = 4 * channels * SLOTS
        self.deep = -(-self.used // LANES) * LANES
        self.groups = 8
        self.pixels = height * width

    def pick_cols(self):
        out = np.zeros((self.halves, self.width, 4, self.halves, self.cols), np.float32)
        for shift in range(4):
            for col in range(self.cols):
                src = 2 * col + shift - 1
                if 0 <= src < self.width:
                    for half in range(self.halves):
                        out[half, src, shift, half, col] = 1.0
        return out.reshape(self.halves * self.width, 4 * LANES)

    def pick_taps(self):
        out = np.zeros((2, 2, 2, self.deep, self.taps_pad), np.float32)
        for odd in range(2):
            for a in range(2):
                for b in range(2):
                    for i in range(3):
                        for j in range(3):
                            for c in range(self.channels):
                                k = ((b + j) * self.channels + c) * SLOTS + 2 * odd + a + i
                                out[odd, a, b, k, (i * 3 + j) * self.channels + c] = 1.0
        return out.reshape(self.groups * self.deep, self.taps_pad)


def spread(row):
    return jnp.broadcast_to(row, (LANES, row.shape[1])).T


def split_two(x):
    high = x.astype(bf16)
    return high, (x - high.astype(f32)).astype(bf16)


class Prepare:
    def __init__(self, plan, planes, pcol, rows_ref, deep_ref, sums_ref, chan_ref):
        self.plan, self.planes, self.pcol, self.rows_ref = plan, planes, pcol, rows_ref
        self.deep_ref, self.sums_ref, self.chan_ref = deep_ref, sums_ref, chan_ref

    def stages(self, cols_ref):
        plan = self.plan
        D, KU, KP, C, tall = plan.depth, plan.used, plan.deep, plan.channels, plan.tall
        shifts, blocks = [], []
        for plane in self.planes:
            rows = plane.astype(f32)
            total = functools.reduce(lambda a, b: a + b, [rows[r : r + 8] for r in range(0, plan.height, 8)])
            total = jnp.sum(jnp.sum(total, axis=1, keepdims=True), axis=0, keepdims=True)
            shifts.append(jnp.round(total * (4.0 / plan.pixels)) * 0.25)
            rows = jnp.concatenate([jnp.zeros((1, plan.width), f32), rows, jnp.zeros((15, plan.width), f32)], axis=0)
            blocks.append(
                jnp.concatenate([rows[h * plan.rows : h * plan.rows + tall] for h in range(plan.halves)], axis=1).astype(bf16)
            )
        yield
        self.rows_ref[...] = mm(jnp.concatenate(blocks, axis=0), self.pcol)
        yield
        tail = jnp.ones((KP - KU, LANES), bf16)
        gram = None
        for half in range(2):
            lean = []
            for pair in range(half * plan.pairs // 2, (half + 1) * plan.pairs // 2):
                parts = [
                    (c, self.rows_ref[c * tall + 4 * pair : c * tall + 4 * pair + SLOTS, s * LANES : (s + 1) * LANES])
                    for s in range(4)
                    for c in range(C)
                ]
                cols_ref[0:KU, pair * LANES : (pair + 1) * LANES] = jnp.concatenate([x for _, x in parts], axis=0).astype(bf16)
                own = jnp.concatenate([x - shifts[c] for c, x in parts], axis=0).astype(bf16)
                lean.append(jnp.concatenate([own, tail], axis=0))
            yield
            lean = jnp.concatenate(lean, axis=1)
            part = lax.dot_general(lean, lean, (((1,), (1,)), ((), ())), preferred_element_type=f32)
            gram = part if gram is None else gram + part
            yield
        moved = gram
        for step in (1, 2, C * SLOTS):
            moved = moved + pltpu.roll(pltpu.roll(moved, KP - step, 0), KP - step, 1)
        high = moved.astype(bf16)
        rest = moved - high.astype(f32)
        mid = rest.astype(bf16)
        low = (rest - mid.astype(f32)).astype(bf16)
        quad = mm(self.deep_ref[...], jnp.concatenate([high, mid, low], axis=0))
        yield
        first = self.deep_ref[:, 0:KP].astype(f32)
        second = jnp.sum(quad * first, axis=1, keepdims=True) * (1.0 / plan.pixels)
        off = jnp.sum(self.sums_ref[...] * gram[KU : KU + 1, :], axis=1, keepdims=True) * (1.0 / plan.pixels)
        second = jnp.broadcast_to(second, (D, LANES))
        off = jnp.broadcast_to(off, (D, LANES))
        mean = off
        for c in range(C):
            mean = mean + shifts[c] * self.chan_ref[2 + c]
        var = jnp.maximum(second - off * off, 0.0) + norm_eps
        self.factor = lax.rsqrt(var)
        self.scale = self.chan_ref[0] * self.factor
        self.mean = mean
        self.thr = mean - self.chan_ref[1] * (var * self.factor)
        yield


def join_params(low_ref, near_ref, far_ref, param_ref):
    near, far = near_ref[...].astype(f32), far_ref[...].astype(f32)
    low = low_ref[0] > 0
    param_ref[...] = jnp.concatenate([jnp.where(low, near, far), jnp.where(low, far, near)], axis=1).astype(bf16)


def is_chosen(order_ref, batch, gid):
    return lax.fori_loop(0, batch, lambda j, t: t | (order_ref[0, j] == gid).astype(jnp.int32), jnp.int32(0))


def make_weights(plan, param_ref, ptap_ref, wl_ref, deep_ref, sums_ref, chan_ref):
    D, KP, C = plan.depth, plan.deep, plan.channels
    spread_taps = mm(ptap_ref[...], param_ref[0 : plan.taps_pad, :])
    sums = None
    for g in range(plan.groups):
        odd, phase = divmod(g, 4)
        turned = spread_taps[g * KP : (g + 1) * KP, :].T
        sums = turned if sums is None else sums + turned
        turned = turned.astype(bf16)
        if g == 0:
            for n in range(3):
                deep_ref[:, n * KP : (n + 1) * KP] = turned
        for blk in range(D // 16):
            at = ((odd * (D // 16) + blk) * 4 + phase) * 16
            rows = turned[blk * 16 : (blk + 1) * 16, :]
            wl_ref[at : at + 16, :] = rows
    sums_ref[...] = sums
    gain = param_ref[plan.taps_pad : plan.taps_pad + 1, :].astype(f32)
    bias = param_ref[plan.taps_pad + 1 : plan.taps_pad + 2, :].astype(f32)
    chan_ref[0] = spread(gain)
    chan_ref[1] = spread(bias / gain)
    first = spread_taps[0:KP, :]
    for c in range(C):
        total = functools.reduce(lambda a, b: a + b, [first[(s * C + c) * SLOTS : (s * C + c + 1) * SLOTS] for s in range(4)])
        chan_ref[2 + c] = spread(jnp.sum(total, axis=0, keepdims=True))


def forward_kernel(
    plan, n_own, batch, where_ref, pick_hbm, count_hbm, order_hbm,
    pool_hbm, sent_hbm, syn_hbm, pcol_hbm, ptap_hbm, low_ref, near_ref, far_ref,
    kept_ref, other_ref,
    part_ref, param_ref, all_ref, wl_ref, rows_ref, deep_ref, sums_ref, chan_ref, now_ref, next_ref, thr_ref, coef_ref,
    pick_ref, count_ref, order_ref, syn_ref, pcol_ref, ptap_ref, sems,
):
    D, KP, KU, C = plan.depth, plan.deep, plan.used, plan.channels
    n_pool, n_sent = pool_hbm.shape[0], sent_hbm.shape[0]
    copies = [
        pltpu.make_async_copy(src, dst, sems.at[n])
        for n, (src, dst) in enumerate(
            (
                (ptap_hbm, ptap_ref),
                (pick_hbm, pick_ref),
                (count_hbm, count_ref),
                (order_hbm, order_ref),
                (pcol_hbm, pcol_ref),
                (syn_hbm, syn_ref),
                (pool_hbm, all_ref.at[pl.ds(0, n_pool)]),
                (sent_hbm, all_ref.at[pl.ds(n_pool, n_sent)]),
            )
        )
    ]
    for copy in copies:
        copy.start()
    part_ref[...] = jnp.zeros_like(part_ref)
    if KP > KU:
        now_ref[KU:KP, :] = jnp.zeros((KP - KU, plan.lanes), bf16)
    join_params(low_ref, near_ref, far_ref, param_ref)
    copies[0].wait()
    make_weights(plan, param_ref, ptap_ref, wl_ref, deep_ref, sums_ref, chan_ref)
    for copy in copies[1:]:
        copy.wait()

    pos = where_ref[0]
    mate_count = count_ref[0, pos ^ 1]
    own_count = count_ref[0, pos]
    full = own_count == n_pool
    own_count = own_count - jnp.where(full, n_sent, 0)
    mate_count = jnp.where(mate_count == n_pool, n_sent, 0)
    total = lax.fori_loop(0, count_ref.shape[1], lambda i, t: t + count_ref[0, i], jnp.int32(0)).astype(f32)
    flags = [is_chosen(order_ref, batch, pos * n_own + i) for i in range(n_own)]
    n_syn = functools.reduce(lambda a, b: a + b, flags)
    n_real = n_pool + n_sent
    for i in range(n_own):
        all_ref[n_real + i] = syn_ref[i].astype(bf16)

    def image_of(i):
        syn_at = jnp.int32(n_real + n_own - 1)
        before = n_syn
        for s in reversed(range(n_own)):
            before = before - flags[s]
            syn_at = jnp.where((flags[s] > 0) & (i == before), n_real + s, syn_at)
        own_at = jnp.clip(i - n_syn, 0, n_pool - 1)
        own_at = jnp.where(full, own_at, pick_ref[0, 0, own_at])
        sent_at = n_pool + jnp.clip(i - n_syn - own_count, 0, n_sent - 1)
        real_at = jnp.where(i - n_syn < own_count, own_at, sent_at)
        return jnp.where(i < n_syn, syn_at, real_at), jnp.where(i < n_syn, 0.25 / batch, -0.25 / total)

    def begin(i):
        at, weight = image_of(i)
        planes = [all_ref[at, c] for c in range(C)]
        return Prepare(plan, planes, pcol_ref[...], rows_ref, deep_ref, sums_ref, chan_ref), weight

    prep, weight = begin(jnp.int32(0))
    for _ in prep.stages(now_ref):
        pass
    thr_ref[...] = prep.thr
    coef_ref[...] = prep.scale * weight
    tile = 2 * LANES

    def step(i, base):
        prep, weight = begin(i + 1)
        ahead = prep.stages(next_ref)
        base = base + coef_ref[...] * thr_ref[...]
        wide = 2 * tile
        for t in range(plan.lanes // wide):
            at = t * wide
            y = mm(wl_ref[...], now_ref[:, at : at + wide])
            for _ in range((3, 3, 2, 0)[min(t, 3)]):
                next(ahead, None)
            for odd in range(2):
                for blk in range(D // 16):
                    r0 = (odd * (D // 16) + blk) * 64
                    thr = thr_ref[blk * 16 : (blk + 1) * 16, :]
                    coef = coef_ref[blk * 16 : (blk + 1) * 16, :]
                    out = slice(odd * D + blk * 16, odd * D + (blk + 1) * 16)
                    for half in range(wide // LANES):
                        lanes = slice(half * LANES, (half + 1) * LANES)
                        ys = [jnp.maximum(y[r0 + p * 16 : r0 + (p + 1) * 16, lanes], thr) for p in range(4)]
                        here = slice(at + half * LANES, at + (half + 1) * LANES)
                        part_ref[out, here] += coef * ((ys[0] + ys[1]) + (ys[2] + ys[3]))
        for _ in ahead:
            pass
        now_ref[0:KU, :] = next_ref[0:KU, :]
        thr_ref[...] = prep.thr
        coef_ref[...] = prep.scale * weight
        return base

    base = lax.fori_loop(0, n_syn + own_count + mate_count, step, jnp.zeros((D, LANES), f32))
    base = 4.0 * base
    mine = pl.multiple_of((pos & 1) * D, D)
    for pair in range(plan.pairs):
        here = slice(pair * LANES, (pair + 1) * LANES)
        other_ref[:, here] = part_ref[pl.ds(D - mine, D), here] - base
        kept_ref[:, here] = part_ref[pl.ds(mine, D), here] - base


def middle_kernel(
    plan, n_own, batch, own, where_ref, order_ref, syn_ref, first_ref, second_ref, pcol_ref, ptap_ref, low_ref, near_ref, far_ref,
    cols_ref, vsum_ref, hits_ref, stat_ref, wl_ref, wlt_ref, decay_ref,
    param_ref, rows_ref, deep_ref, sums_ref, chan_ref,
):
    D, KP, KU, C = plan.depth, plan.deep, plan.used, plan.channels
    flag = is_chosen(order_ref, batch, where_ref[0] * n_own + own)
    tile = 2 * LANES
    decay_ref[0] = beta_one * first_ref[own]
    decay_ref[1] = beta_two * second_ref[own]

    @pl.when(flag > 0)
    def _():
        join_params(low_ref, near_ref, far_ref, param_ref)
        make_weights(plan, param_ref, ptap_ref, wl_ref, deep_ref, sums_ref, chan_ref)
        for g in range(plan.groups):
            wlt_ref[:, g * D : (g + 1) * D] = wl_ref[g * D : (g + 1) * D, :].astype(f32).T.astype(bf16)[0:KU, :]
        if KP > KU:
            cols_ref[KU:KP, :] = jnp.zeros((KP - KU, plan.lanes), bf16)
        planes = [syn_ref[own, c].astype(bf16) for c in range(C)]
        prep = Prepare(plan, planes, pcol_ref[...], rows_ref, deep_ref, sums_ref, chan_ref)
        for _ in prep.stages(cols_ref):
            pass
        for n, value in enumerate((prep.mean, prep.factor, prep.scale, prep.thr, chan_ref[0], chan_ref[1])):
            stat_ref[n] = value

        for t in range(plan.lanes // tile):
            at = t * tile
            y = mm(wl_ref[...], cols_ref[:, at : at + tile])
            for odd in range(2):
                for blk in range(D // 16):
                    r0 = (odd * (D // 16) + blk) * 64
                    thr = stat_ref[3, blk * 16 : (blk + 1) * 16, :]
                    out = slice(odd * D + blk * 16, odd * D + (blk + 1) * 16)
                    for half in range(2):
                        lanes = slice(half * LANES, (half + 1) * LANES)
                        yp = [y[r0 + p * 16 : r0 + (p + 1) * 16, lanes] for p in range(4)]
                        ys = [jnp.maximum(a, thr) for a in yp]
                        hs = [jnp.where(a > thr, 1.0, 0.0) for a in yp]
                        here = slice(at + half * LANES, at + (half + 1) * LANES)
                        vsum_ref[out, here] = ((ys[0] + ys[1]) + (ys[2] + ys[3])) - 4.0 * thr
                        hits_ref[out, here] = (hs[0] + hs[1]) + (hs[2] + hs[3])


def backward_kernel(
    plan, n_own, batch, where_ref, order_ref, *refs,
):
    D, KU, blocks = plan.depth, plan.used, plan.depth // 16
    gap_ref = refs[0]
    owns = [refs[1 + 7 * i : 8 + 7 * i] for i in range(n_own)]
    (
        pcol_ref, syn_ref, new_syn_ref, new_first_ref, new_second_ref,
        grads_ref, shared_dcols, shared_col,
    ) = refs[1 + 7 * n_own :]
    pos = where_ref[0]
    tile = 2 * LANES
    grad_factor = 2.0 * loss_scale / batch
    shape = (plan.height, plan.halves * plan.span)
    spot = lax.broadcasted_iota(jnp.int32, shape, 1)
    slot = lax.rem(spot, SLOTS)
    row = lax.div(spot, plan.span) * plan.rows + lax.div(lax.rem(spot, plan.span), SLOTS) * 4 + slot - 1
    prow = jnp.where((lax.broadcasted_iota(jnp.int32, shape, 0) == row) & (slot < 6), 1.0, 0.0).astype(bf16)
    flags = [is_chosen(order_ref, batch, pos * n_own + i) for i in range(n_own)]

    def gradient(i):
        grad_ref, dcols_ref, col_ref = grads_ref.at[i], shared_dcols.at[i], shared_col.at[i]
        cols_ref, vsum_ref, hits_ref, stat_ref, wl_ref, wlt_ref, decay_ref = owns[i]
        unit = grad_factor / (4.0 * plan.pixels)
        for blk in range(blocks):
            chan = slice(blk * 16, (blk + 1) * 16)
            one = two = jnp.zeros((16, LANES), f32)
            for pair in range(plan.pairs):
                here = slice(pair * LANES, (pair + 1) * LANES)
                for odd in range(2):
                    rows = slice(odd * D + blk * 16, odd * D + (blk + 1) * 16)
                    gap = gap_ref[rows, here]
                    one = one + gap * hits_ref[rows, here]
                    two = two + gap * vsum_ref[rows, here]
            one = jnp.broadcast_to(jnp.sum(one, axis=1, keepdims=True), (16, LANES)) * unit
            two = jnp.broadcast_to(jnp.sum(two, axis=1, keepdims=True), (16, LANES)) * unit
            mean, factor, scale, thr, gain, ratio = [stat_ref[n, chan, :] for n in range(6)]
            slope = factor * factor * (scale * two - one * (ratio * gain))
            col_ref[0, chan, :] = factor * gain * (0.25 * grad_factor)
            col_ref[1, chan, :] = slope
            col_ref[2, chan, :] = slope * mean - factor * (gain * one)

        wide = 2 * tile
        for t in range(plan.lanes // wide):
            at = t * wide
            y = mm(wl_ref[...], cols_ref[:, at : at + wide])
            inner = []
            for odd in range(2):
                for blk in range(blocks):
                    r0 = (odd * blocks + blk) * 64
                    chan = slice(blk * 16, (blk + 1) * 16)
                    thr_b, up_b, slope_b, off = stat_ref[3, chan, :], col_ref[0, chan, :], col_ref[1, chan, :], col_ref[2, chan, :]
                    ons = []
                    for half in range(wide // LANES):
                        gap = gap_ref[odd * D + blk * 16 : odd * D + (blk + 1) * 16, at + half * LANES : at + (half + 1) * LANES]
                        ons.append(up_b * gap + off)
                    for p in range(4):
                        both = []
                        for half in range(wide // LANES):
                            yp = y[r0 + p * 16 : r0 + (p + 1) * 16, half * LANES : (half + 1) * LANES]
                            both.append((jnp.where(yp > thr_b, ons[half], off) - slope_b * yp).astype(bf16))
                        inner.append(jnp.concatenate(both, axis=1))
            dcols_ref[:, at : at + wide] = mm(wlt_ref[...], jnp.concatenate(inner, axis=0))

        shifts = []
        for s in range(4):
            shifts.append(
                jnp.concatenate(
                    [
                        dcols_ref[
                            (s * plan.channels + c) * SLOTS : (s * plan.channels + c + 1) * SLOTS,
                            pair * LANES : (pair + 1) * LANES,
                        ]
                        for c in range(plan.channels)
                        for pair in range(plan.pairs)
                    ],
                    axis=0,
                )
            )
        high, low = split_two(jnp.concatenate(shifts, axis=1))
        back = (((1,), (1,)), ((), ()))
        pcol = pcol_ref[...]
        wide = lax.dot_general(high, pcol, back, preferred_element_type=f32) + lax.dot_general(
            low, pcol, back, preferred_element_type=f32
        )
        tall = jnp.concatenate(
            [
                jnp.concatenate(
                    [
                        wide[c * plan.span : (c + 1) * plan.span, half * plan.width : (half + 1) * plan.width]
                        for c in range(plan.channels)
                    ],
                    axis=1,
                )
                for half in range(plan.halves)
            ],
            axis=0,
        )
        high, low = split_two(tall)
        image = mm(prow, high) + mm(prow, low)
        for c in range(plan.channels):
            grad_ref[c] = image[:, c * plan.width : (c + 1) * plan.width]

    for i in range(n_own):

        @pl.when(flags[i] > 0)
        def _():
            gradient(i)

        @pl.when(flags[i] == 0)
        def _():
            grads_ref[i] = jnp.zeros(grads_ref.shape[1:], f32)

    for i in range(n_own):
        decay_ref = owns[i][6]
        for c in range(plan.channels):
            grad = grads_ref[i, c]
            first_new = decay_ref[0, c] + (1.0 - beta_one) * grad
            second_new = decay_ref[1, c] + (1.0 - beta_two) * grad * grad
            corrected = first_new / (1.0 - beta_one**adam_step)
            scale_hat = jnp.sqrt(second_new / (1.0 - beta_two**adam_step))
            new_syn_ref[i, c] = syn_ref[i, c] - learn_rate * corrected / (scale_hat + adam_eps)
            new_first_ref[i, c] = first_new
            new_second_ref[i, c] = second_new


def gather_params(conv_weight, norm_gain, norm_bias, taps_pad):
    taps = conv_weight.shape[0]
    tall = taps_pad + 16
    own = (
        jnp.pad(conv_weight, ((0, tall - taps), (0, 0)))
        + jnp.pad(norm_gain[None], ((taps_pad, tall - taps_pad - 1), (0, 0)))
        + jnp.pad(norm_bias[None], ((taps_pad + 1, tall - taps_pad - 2), (0, 0)))
    )
    if lax.axis_size("cls") == 2:
        other = lax.ppermute(own, "cls", [(0, 1), (1, 0)])
        return (1 - lax.axis_index("cls")).astype(jnp.int32)[None], own, other
    whole = lax.all_gather(own, "cls", axis=1, tiled=True)
    half = whole.shape[1] // 2
    return jnp.ones((1,), jnp.int32), whole[:, :half], whole[:, half:]


class Exchange:
    def __init__(self):
        self.n = lax.axis_size("wide")
        self.pos = lax.axis_index("wide")
        steps = []
        while 1 << (len(steps) + 1) <= self.n:
            steps.append(1 << len(steps))
        self.first, rest = steps[0], steps[1:]
        self.masks = [(self.first, self.first)] + list(zip(rest, rest[1:] + rest[:1]))

    def swap(self, x, masks):
        return lax.ppermute(x, "wide", [(i, i ^ masks[i & self.first]) for i in range(self.n)])

    def high(self, masks):
        return (self.pos & jnp.where((self.pos & self.first) > 0, masks[1], masks[0])) > 0

    def add(self, own, masks):
        high = self.high(masks)
        rows = own.shape[0] // 2
        kept = jnp.where(high, own[rows:], own[:rows])
        sent = jnp.where(high, own[:rows], own[rows:]).astype(jnp.float16)
        return kept, sent

    def join(self, own, other, masks):
        high = self.high(masks)
        return jnp.concatenate([jnp.where(high, other, own), jnp.where(high, own, other)], axis=0)


def exchange_sum(kept, away, where, middle, n_own):
    ex = Exchange()
    halved = ex.masks[:2]
    whole = ex.masks[2:]
    rounds = [(m, "halve") for m in halved] + [(m, "whole") for m in whole] + [(m, "join") for m in reversed(halved)]
    at_round = [min(2 + i, len(rounds) - 2) for i in range(n_own)]
    own, made = None, []
    for n, (masks, kind) in enumerate(rounds):
        if n == 0:
            own, sent = kept, away
        elif kind == "halve":
            own, sent = ex.add(own, masks)
        else:
            sent = own.astype(jnp.float16)
        todo = [i for i in range(n_own) if at_round[i] == n]
        if todo:
            sent, held = lax.optimization_barrier((sent, where))
        got = ex.swap(sent, masks)
        if todo:
            new = [middle(i, held) for i in todo]
            if n + 1 < len(rounds):
                got, new = lax.optimization_barrier((got, new))
            made += new
        own = ex.join(sent, got, masks) if kind == "join" else own + got.astype(f32)
    return own.astype(f32), made


def body(
    syn_images, adam_first, adam_second, real_pool, real_pick, real_count, syn_order,
    conv_weight, norm_gain, norm_bias,
):
    _, n_own, channels, height, width = syn_images.shape
    batch = syn_order.shape[1] // 2
    depth = conv_weight.shape[1] * lax.axis_size("cls")
    plan = Plan(channels, height, width, depth)
    pcol = jnp.asarray(plan.pick_cols(), bf16)
    ptap = jnp.asarray(plan.pick_taps(), bf16)
    n_pool = real_pool.shape[1]
    got = lax.ppermute(real_pool[0, n_pool - n_pool // 4 :], "wide", [(i, i ^ 1) for i in range(lax.axis_size("wide"))])
    low, near, far = gather_params(conv_weight, norm_gain, norm_bias, plan.taps_pad)
    where = lax.axis_index("wide").astype(jnp.int32)[None]

    smem = pl.BlockSpec(memory_space=pltpu.SMEM)
    vmem = pl.BlockSpec(memory_space=pltpu.VMEM)
    shape = jax.ShapeDtypeStruct
    rows = 2 * depth
    m_rows = plan.groups * depth
    weights = [
        pltpu.VMEM((channels * plan.tall, 4 * LANES), f32),
        pltpu.VMEM((depth, 3 * plan.deep), bf16),
        pltpu.VMEM((depth, plan.deep), f32),
        pltpu.VMEM((2 + channels, depth, LANES), f32),
    ]

    def within(mib):
        return pltpu.CompilerParams(vmem_limit_bytes=mib << 20)

    hbm = pl.BlockSpec(memory_space=pltpu.HBM)
    kept, sent = pl.pallas_call(
        functools.partial(forward_kernel, plan, n_own, batch),
        in_specs=[smem] + [hbm] * 4 + [pl.BlockSpec(memory_space=pl.ANY)] + [hbm] * 3 + [smem] + [vmem] * 2,
        out_specs=[vmem] * 2,
        out_shape=[shape((depth, plan.lanes), f32)] * 2,
        scratch_shapes=[
            pltpu.VMEM((rows, plan.lanes), f32),
            pltpu.VMEM((near.shape[0], depth), bf16),
            pltpu.VMEM((n_pool + got.shape[0] + n_own, channels, height, width), bf16),
            pltpu.VMEM((m_rows, plan.deep), bf16),
            *weights,
            pltpu.VMEM((plan.deep, plan.lanes), bf16),
            pltpu.VMEM((plan.used, plan.lanes), bf16),
            *[pltpu.VMEM((depth, LANES), f32)] * 2,
            pltpu.SMEM(real_pick.shape, jnp.int32),
            pltpu.SMEM(real_count.shape, jnp.int32),
            pltpu.SMEM(syn_order.shape, jnp.int32),
            pltpu.VMEM(syn_images.shape[1:], f32),
            pltpu.VMEM(pcol.shape, bf16),
            pltpu.VMEM(ptap.shape, bf16),
            pltpu.SemaphoreType.DMA((8,)),
        ],
        compiler_params=within(60),
        name="embed_sums",
    )(where, real_pick, real_count, syn_order, real_pool[0], got, syn_images[0], pcol, ptap, low, near, far)

    def middle(own, held):
        return pl.pallas_call(
            functools.partial(middle_kernel, plan, n_own, batch, own),
            in_specs=[smem] * 2 + [vmem] * 5 + [smem] + [vmem] * 2,
            out_specs=[vmem] * 7,
            out_shape=[
                shape((plan.deep, plan.lanes), bf16),
                shape((rows, plan.lanes), f32),
                shape((rows, plan.lanes), f32),
                shape((6, depth, LANES), f32),
                shape((m_rows, plan.deep), bf16),
                shape((plan.used, m_rows), bf16),
                shape((2, channels, height, width), f32),
            ],
            scratch_shapes=[pltpu.VMEM((near.shape[0], depth), bf16), *weights],
            compiler_params=within(18),
            name="syn_features",
        )(held, syn_order, syn_images[0], adam_first[0], adam_second[0], pcol, ptap, low, near, far)

    gap, made = exchange_sum(kept, sent, where, middle, n_own)

    img = shape((n_own, channels, height, width), f32)
    outs = pl.pallas_call(
        functools.partial(backward_kernel, plan, n_own, batch),
        in_specs=[smem] * 2 + [vmem] * (3 + 7 * n_own),
        out_specs=[vmem] * 3,
        out_shape=[img] * 3,
        scratch_shapes=[
            pltpu.VMEM((n_own, channels, height, width), f32),
            pltpu.VMEM((n_own, plan.used, plan.lanes), f32),
            pltpu.VMEM((n_own, 3, depth, LANES), f32),
        ],
        compiler_params=within(24),
        name="image_grads",
    )(
        where, syn_order, gap, *[x for one in made for x in one], pcol, syn_images[0],
    )
    return tuple(out[None] for out in outs)


def solution(mesh):
    image = P("cls", "wide", None, None, None)
    return jax.shard_map(
        body,
        mesh=mesh,
        in_specs=(
            image, image, image, image, P("cls", "wide", None), P("cls", None), P("cls", None),
            P(None, "cls"), P("cls"), P("cls"),
        ),
        out_specs=(image, image, image),
        check_vma=False,
    )
```
